32 devices in a mesh: dp: 2 (over y), ctx: 4 (over x, core), exp: 4 (over z).
Axes of the slice: x: 2, y: 2, z: 4, core: 2. Of those that a mesh axis runs over, the one named last changes fastest.
Arguments:
- hidden_in: bfloat16 [2, 4, 1536, 2048], P('dp', 'exp', 'ctx'), may hold values from -6 to 6
- segments: int32 [2, 4, 1536], P('dp', 'exp'), may hold values from 0 to 3, as said below
- routes: int32 [2, 4, 1536, 8], P('dp', 'exp', 'ctx'), may hold values from 0 to 15, all different within a row; in each aligned block of 384 rows (0 to 383, 384 to 767, ..., all dimensions but the last counted through in order) at most 240 rows name the same one
- attn_gain: bfloat16 [2048], replicated, may hold values from 0.5 to 1.5
- query_weight: bfloat16 [2048, 2048], P(('dp', 'ctx', 'exp')), may hold values from -0.125 to 0.125
- key_weight: bfloat16 [2048, 2048], P(('dp', 'ctx', 'exp')), may hold values from -0.125 to 0.125
- value_weight: bfloat16 [2048, 2048], P(('dp', 'ctx', 'exp')), may hold values from -0.125 to 0.125
- query_gain: bfloat16 [2048], replicated, may hold values from 0.5 to 1.5
- key_gain: bfloat16 [2048], replicated, may hold values from 0.5 to 1.5
- output_weight: bfloat16 [2048, 2048], P(('dp', 'ctx', 'exp')), may hold values from -1.5 to 1.5
- ffn_gain: bfloat16 [2048], replicated, may hold values from 0.5 to 1.5
- router_weight: bfloat16 [2048, 16], replicated, may hold values from -0.0625 to 0.0625
- gate_weight: bfloat16 [16, 2048, 1024], P(('ctx', 'exp')), may hold values from -0.125 to 0.125
- up_weight: bfloat16 [16, 2048, 1024], P(('ctx', 'exp')), may hold values from -0.125 to 0.125
- down_weight: bfloat16 [16, 1024, 2048], P(('ctx', 'exp')), may hold values from -7.1875 to 7.1875
- cotangent: bfloat16 [2, 4, 1536, 2048], P('dp', 'exp', 'ctx'), may hold values from -6 to 6
Outputs:
- output: bfloat16 [2, 4, 1536, 2048], P('dp', 'exp', 'ctx')
- hidden_grad: bfloat16 [2, 4, 1536, 2048], P('dp', 'exp', 'ctx')
- attn_gain_grad: float32 [2048], replicated
- query_weight_grad: float32 [2048, 2048], P(('dp', 'ctx', 'exp'))
- key_weight_grad: float32 [2048, 2048], P(('dp', 'ctx', 'exp'))
- value_weight_grad: float32 [2048, 2048], P(('dp', 'ctx', 'exp'))
- query_gain_grad: float32 [2048], replicated
- key_gain_grad: float32 [2048], replicated
- output_weight_grad: float32 [2048, 2048], P(('dp', 'ctx', 'exp'))
- ffn_gain_grad: float32 [2048], replicated
- router_weight_grad: float32 [2048, 16], replicated
- gate_weight_grad: float32 [16, 2048, 1024], P(('ctx', 'exp'))
- up_weight_grad: float32 [16, 2048, 1024], P(('ctx', 'exp'))
- down_weight_grad: float32 [16, 1024, 2048], P(('ctx', 'exp'))
The draws below stay inside these ranges and needn't reach their ends.
Inputs may be any that keep to these rules, and one draw needn't show every extreme that they name: `segments`: in each group the first 512 tokens have id 0; the others form (1024 + 512 - 1) // 512 + 1 continuations numbered 1, 2, ... in order, each of consecutive tokens and of 1 to 512 tokens, one of them exactly 512. `routes`: each row names 8 different experts; among the 384 rows of one device no expert is named more than 240 times.
All inputs are finite; a program needn't handle non-finite values.
Results may differ from the reference program's by a relative error of at most 0.022.
Values may be sent and summed in bfloat16 or wider, within the bound.
A program may use at most 448 MiB of HBM per device.

```python
import math
import jax
import jax.numpy as jnp
import numpy as np
from jax import lax

D = 2048
HEAD = 128
FF = 1024
TOPK = 8
PROMPT = 512
CONT_LEN = 512
CONT_TOK = 1024
GROUP_TOK = 1536
TOK_DEV = 384
EXPERTS = 16
CAP = 240
N_DP = 2
N_CTX = 4
N_EXP = 4


def draw_segments(key, part):
    number = (CONT_TOK + CONT_LEN - 1) // CONT_LEN + 1
    rest = CONT_TOK - CONT_LEN
    others = number - 1
    base_len = rest // others
    extra = rest % others
    start_lens = [base_len + (1 if index < extra else 0) for index in range(others)]
    pair_key, order_key = jax.random.split(jax.random.fold_in(key, 7))
    columns = []
    index = 0
    while index < others:
        if index + 1 < others:
            first_len = start_lens[index]
            second_len = start_lens[index + 1]
            low_move = max(1 - first_len, second_len - CONT_LEN)
            high_move = min(CONT_LEN - first_len, second_len - 1)
            moves = jax.random.randint(jax.random.fold_in(pair_key, index), (N_DP, N_EXP), low_move, high_move + 1).astype(jnp.int32)
            columns.append(first_len + moves)
            columns.append(second_len - moves)
            index = index + 2
        else:
            columns.append(jnp.full((N_DP, N_EXP), start_lens[index], jnp.int32))
            index = index + 1
    columns.append(jnp.full((N_DP, N_EXP), CONT_LEN, jnp.int32))
    pieces = jnp.stack(columns, axis=-1).astype(jnp.int32)
    draws = jax.random.randint(order_key, (N_DP, N_EXP, number), 0, 1 << 20)
    scores = draws * number + jnp.arange(number, dtype=jnp.int32)[None, None, :]
    order = jnp.argsort(scores, axis=-1)
    lengths = jnp.take_along_axis(pieces, order, axis=-1)
    bounds = jnp.cumsum(lengths, axis=-1)
    positions = jnp.arange(CONT_TOK, dtype=jnp.int32)
    labels = 1 + jnp.sum((bounds[:, :, None, :] <= positions[None, None, :, None]).astype(jnp.int32), axis=-1)
    prompt = jnp.zeros((N_DP, N_EXP, PROMPT), jnp.int32)
    return jnp.concatenate([prompt, labels.astype(jnp.int32)], axis=-1)


def steps_of(stream_key, extent, cuts, least, high):
    gain, own = 1.0, jax.random.fold_in(stream_key, 6)
    for dim, shards_of in cuts:
        steps = jnp.exp(jax.random.uniform(jax.random.fold_in(own, dim), (shards_of,), jnp.float32, least / len(cuts), high / len(cuts)))
        gain = gain * jnp.repeat(steps, extent[dim] // shards_of).reshape([-1 if axis == dim else 1 for axis in range(len(extent))])
    return gain


def assign_block(stream_key, own, number, rows, number_of, top, bound, slope):
    order = jax.random.permutation(stream_key, number_of)
    crowded, common = portions_of(number_of, rows * top, bound, slope, True), portions_of(number_of, rows * top, bound, slope, False)
    places = jnp.arange(number_of)

    def named(sizes, offset_by):
        used = int((sizes > 0).sum())
        fixed = max(1, used // 4)
        passed = fixed + (places - fixed + offset_by * (used - fixed)) % max(1, number_of - fixed)
        return jnp.zeros((number_of,), jnp.int32).at[order[jnp.where(places < fixed, places, passed)]].set(jnp.asarray(sizes, jnp.int32))

    sizes = jnp.where(number % 4 == 0, named(crowded, number // 4), named(common, number - number // 4 - 1))
    mixed = jax.random.permutation(jax.random.fold_in(own, 3), number_of)
    donor, receiver = mixed[0:number_of // 2 * 2:2], mixed[1:number_of // 2 * 2:2]
    room = jnp.minimum(sizes[donor] - 1, bound - sizes[receiver]) // 2
    room = jnp.where((donor == order[0]) | (receiver == order[0]) | (sizes[receiver] == 0), 0, jnp.maximum(room, 0))
    passed = jax.random.randint(jax.random.fold_in(own, 4), (number_of // 2,), 0, 1 << 20) % (room + 1)
    sizes = sizes.at[donor].add(-passed).at[receiver].add(passed)
    items = jnp.searchsorted(jnp.cumsum(sizes), jnp.arange(rows * top), side="right").astype(jnp.int32)
    grid = items.reshape(top, rows).T
    grid = grid[jax.random.permutation(jax.random.fold_in(own, 1), rows)]
    offset_by = jax.random.randint(jax.random.fold_in(own, 2), (rows, 1), 0, top)
    return jnp.take_along_axis(grid, (jnp.arange(top)[None, :] + offset_by) % top, axis=1)


def portions_of(number_of, total, limit, lean, full):
    loads = [(1 << 20) // math.isqrt(grade ** lean) + 1 for grade in range(1, number_of + 1)]
    largest = limit if full else min(limit, max(-(-total // number_of), total * loads[0] // sum(loads)))
    least = 1 if total - largest >= number_of - 1 else 0
    given, spare = [largest] + [least] * (number_of - 1), total - largest - least * (number_of - 1)
    while spare > 0:
        free = [i for i in range(1, number_of) if given[i] < largest] or [i for i in range(1, number_of) if given[i] < limit]
        mass, left = sum([loads[i] for i in free]), spare
        for i in free:
            addition = min(limit - given[i], max(1, left * loads[i] // mass), spare)
            given[i] = given[i] + addition
            spare = spare - addition
    return np.array(given)


def centred(own_key, shape, width, bound, shards=(), kind=jnp.bfloat16):
    array = width * jax.random.normal(own_key, shape, jnp.float32)
    if shards:
        array = array * steps_of(own_key, shape, shards, -0.22, 0.18)
    return jnp.clip(array, -bound, bound).astype(kind)


def setup_inputs(seed: int = 0) -> dict:
    splits = jax.random.split(jax.random.key(seed), 17)
    hidden_in = centred(splits[0], (N_DP, N_EXP, GROUP_TOK, D), 1.0, 6.0, ((0, 2), (1, 4), (2, 4)))
    segments = draw_segments(jax.random.fold_in(splits[16], 71), 0)
    routes_keys = jax.random.split(jax.random.fold_in(splits[2], 1), N_DP * N_EXP * GROUP_TOK // TOK_DEV)
    routes_turns = jax.random.permutation(jax.random.fold_in(splits[2], 3), N_DP * N_EXP * GROUP_TOK // TOK_DEV)
    routes = jax.vmap(lambda own, number: assign_block(jax.random.fold_in(splits[2], 2), own, number, TOK_DEV, EXPERTS, TOPK, CAP, 1))(routes_keys, routes_turns).reshape((N_DP, N_EXP, GROUP_TOK, TOPK))
    attn_gain = jnp.clip(1.0 + 0.1 * jax.random.normal(splits[3], (D,), jnp.float32), 0.5, 1.5).astype(jnp.bfloat16)
    query_weight = centred(splits[4], (D, D), D ** -0.5, 0.125, ((0, 32),))
    key_weight = centred(splits[5], (D, D), D ** -0.5, 0.125, ((0, 32),))
    value_weight = centred(splits[6], (D, D), D ** -0.5, 0.125, ((0, 32),))
    query_gain = jnp.clip(1.0 + 0.1 * jax.random.normal(splits[7], (D,), jnp.float32), 0.5, 1.5).astype(jnp.bfloat16)
    key_gain = jnp.clip(1.0 + 0.1 * jax.random.normal(splits[8], (D,), jnp.float32), 0.5, 1.5).astype(jnp.bfloat16)
    output_weight = centred(splits[9], (D, D), (D // 128) ** -0.5, 1.5, ((0, 32),))
    ffn_gain = jnp.clip(1.0 + 0.1 * jax.random.normal(splits[10], (D,), jnp.float32), 0.5, 1.5).astype(jnp.bfloat16)
    router_weight = centred(splits[11], (D, EXPERTS), (4 * D) ** -0.5, 0.0625)
    gate_weight = centred(splits[12], (EXPERTS, D, FF), D ** -0.5, 0.125, ((0, 16),))
    up_weight = centred(splits[13], (EXPERTS, D, FF), D ** -0.5, 0.125, ((0, 16),))
    down_weight = centred(splits[14], (EXPERTS, FF, D), 1.2, 7.1875, ((0, 16),))
    cotangent = centred(splits[15], (N_DP, N_EXP, GROUP_TOK, D), 1.0, 6.0, ((0, 2), (1, 4), (2, 4)))
    return dict(hidden_in=hidden_in, segments=segments, routes=routes, attn_gain=attn_gain, query_weight=query_weight, key_weight=key_weight, value_weight=value_weight, query_gain=query_gain, key_gain=key_gain, output_weight=output_weight, ffn_gain=ffn_gain, router_weight=router_weight, gate_weight=gate_weight, up_weight=up_weight, down_weight=down_weight, cotangent=cotangent)


epsilon = 1e-05
theta_base = 10000.0
masked_score = -1e+30
highest = lax.Precision.HIGHEST

@jax.custom_vjp
def low(v):
    return lax.optimization_barrier(v.astype(jnp.bfloat16)).astype(jnp.float32)

@jax.custom_vjp
def low_back(v):
    return v

def low_keep(v):
    return (low(v), None)

def low_pass(kept, grad):
    return (grad,)

def back_keep(v):
    return (v, None)

def back_low(kept, grad):
    return (low(grad),)
low.defvjp(low_keep, low_pass)
low_back.defvjp(back_keep, back_low)

def rms_scale(values, gain_vec):
    return values * lax.rsqrt(lax.optimization_barrier(jnp.mean(values * values, axis=-1, keepdims=True)) + epsilon) * gain_vec

def rotate(values, angles):
    half_size = values.shape[-1] // 2
    cosine = jnp.cos(angles)[:, None, :]
    sine_table = jnp.sin(angles)[:, None, :]
    front_half = values[..., :half_size]
    back_half = values[..., half_size:]
    return jnp.concatenate([front_half * cosine - back_half * sine_table, back_half * cosine + front_half * sine_table], axis=-1)

def token_positions(labels):
    length_all = labels.shape[0]
    before = lax.optimization_barrier(jnp.sum((labels[None, :] < labels[:, None]).astype(jnp.int32), axis=1))
    indices = jnp.arange(length_all, dtype=jnp.int32)
    return indices - before + jnp.where(labels > 0, PROMPT, 0).astype(jnp.int32)

def rotary_angles(positions):
    half_size = HEAD // 2
    frequency = theta_base ** (-(jnp.arange(half_size, dtype=jnp.float32) * 2.0 / HEAD))
    return positions.astype(jnp.float32)[:, None] * frequency[None, :]

def query_prep(raw_values, gain_vec, angles):
    row_count = raw_values.shape[0]
    normed = rms_scale(raw_values, gain_vec).reshape(row_count, raw_values.shape[1] // HEAD, HEAD)
    return rotate(normed, angles).reshape(row_count, raw_values.shape[1])

def attend(hidden, labels, gain_attn, weight_query, weight_key, weight_value, gain_query, gain_key, weight_output):
    length_all = hidden.shape[0]
    head_count = hidden.shape[1] // HEAD
    angles = rotary_angles(token_positions(labels))
    normed = low(rms_scale(hidden, gain_attn))
    query_raw = low_back(jnp.dot(normed, weight_query, precision=highest))
    key_raw = low_back(jnp.dot(normed, weight_key, precision=highest))
    value_raw = low_back(jnp.dot(normed, weight_value, precision=highest))
    query_rot = low(query_prep(query_raw, gain_query, angles)).reshape(length_all, head_count, HEAD)
    key_rot = low(query_prep(key_raw, gain_key, angles)).reshape(length_all, head_count, HEAD)
    value_low = low(value_raw).reshape(length_all, head_count, HEAD)
    scores = low_back(jnp.einsum('qhd,khd->hqk', query_rot, key_rot, precision=highest) * HEAD ** (-0.5))
    indices = jnp.arange(length_all, dtype=jnp.int32)
    allowed = (indices[None, :] <= indices[:, None]) & ((labels[None, :] == 0) | (labels[None, :] == labels[:, None]))
    attn_prob = jax.nn.softmax(jnp.where(allowed[None], scores, masked_score), axis=-1)
    prob_low = low(attn_prob)
    mixed = jnp.einsum('hqk,khd->qhd', prob_low, value_low, precision=highest).reshape(length_all, head_count * HEAD)
    mix_low = low(low_back(mixed))
    branch = low_back(jnp.dot(mix_low, weight_output, precision=highest))
    return hidden + branch

def to_senders(values):
    shaped = values.reshape((N_EXP, N_CTX, TOK_DEV) + values.shape[2:])
    return jnp.swapaxes(shaped, 0, 1).reshape((N_CTX * N_EXP, TOK_DEV) + values.shape[2:])

def sender_slots(routes_half):
    sent_routes = to_senders(routes_half)
    route_hits = lax.optimization_barrier(jnp.sum((sent_routes[:, :, :, None] == jnp.arange(EXPERTS, dtype=jnp.int32)).astype(jnp.int32), axis=2))
    tokens_at = jnp.arange(TOK_DEV, dtype=jnp.int32)
    lower_mask = (tokens_at[:, None] > tokens_at[None, :]).astype(jnp.int32)
    earlier = jnp.einsum('ab,sbe->sae', lower_mask, route_hits)
    slot_index = jnp.take_along_axis(earlier, sent_routes, axis=2)
    return slot_index + (jnp.arange(N_CTX * N_EXP, dtype=jnp.int32) * CAP)[:, None, None]

def expert_rows(expert_pack):
    rows_in, gate_matrix, up_matrix, down_matrix = expert_pack
    gate_pre = low_back(jnp.dot(rows_in, gate_matrix, precision=highest))
    up_pre = low_back(jnp.dot(rows_in, up_matrix, precision=highest))
    expert_hidden = low(jax.nn.silu(gate_pre) * up_pre)
    return low(low_back(jnp.dot(expert_hidden, down_matrix, precision=highest)))

def mixture(residual, routes_half, slot_rows, gain_ffn, weight_router, weight_gate, weight_up, weight_down):
    ffn_normed = low(rms_scale(residual, gain_ffn))
    logits = low_back(jnp.einsum('gtd,de->gte', ffn_normed, weight_router, precision=highest))
    router_prob = jax.nn.softmax(logits, axis=-1)
    gates = low(jnp.take_along_axis(router_prob, routes_half, axis=-1))
    senders = N_CTX * N_EXP
    sent_rows = to_senders(ffn_normed)
    sent_routes = to_senders(routes_half)
    sent_gates = to_senders(gates)
    spread_rows = jnp.broadcast_to(sent_rows[:, :, None, :], (senders, TOK_DEV, TOPK, D))
    dispatched = jnp.zeros((EXPERTS, senders * CAP, D), jnp.float32)
    dispatched = low_back(dispatched.at[sent_routes, slot_rows].set(spread_rows))
    expert_out = lax.map(jax.checkpoint(expert_rows), (dispatched, weight_gate, weight_up, weight_down))
    picked = expert_out[sent_routes, slot_rows]
    moe_out = lax.optimization_barrier(jnp.sum(sent_gates[..., None] * picked, axis=2))
    restored = jnp.swapaxes(moe_out.reshape(N_CTX, N_EXP, TOK_DEV, D), 0, 1).reshape(N_EXP, GROUP_TOK, D)
    return residual + restored

def reference(hidden_in, segments, routes, attn_gain, query_weight, key_weight, value_weight, query_gain, key_gain, output_weight, ffn_gain, router_weight, gate_weight, up_weight, down_weight, cotangent):
    slot_tables = [sender_slots(routes[dp_index]) for dp_index in range(N_DP)]
    label_groups = segments.reshape(N_DP * N_EXP, GROUP_TOK)

    def forward(hidden, gain_attn, weight_query, weight_key, weight_value, gain_query, gain_key, weight_output, gain_ffn, weight_router, weight_gate, weight_up, weight_down):
        groups = hidden.reshape(N_DP * N_EXP, GROUP_TOK, D)

        def one_group(group_pack):
            return attend(group_pack[0], group_pack[1], gain_attn, weight_query, weight_key, weight_value, gain_query, gain_key, weight_output)
        middle = lax.map(jax.checkpoint(one_group), (groups, label_groups)).reshape(N_DP, N_EXP, GROUP_TOK, D)
        results = [mixture(middle[dp_index], routes[dp_index], slot_tables[dp_index], gain_ffn, weight_router, weight_gate, weight_up, weight_down) for dp_index in range(N_DP)]
        return jnp.stack(results)
    result, pullback = jax.vjp(forward, hidden_in.astype(jnp.float32), attn_gain.astype(jnp.float32), query_weight.astype(jnp.float32), key_weight.astype(jnp.float32), value_weight.astype(jnp.float32), query_gain.astype(jnp.float32), key_gain.astype(jnp.float32), output_weight.astype(jnp.float32), ffn_gain.astype(jnp.float32), router_weight.astype(jnp.float32), gate_weight.astype(jnp.float32), up_weight.astype(jnp.float32), down_weight.astype(jnp.float32))
    gradients = pullback(cotangent.astype(jnp.float32))
    return (result.astype(jnp.bfloat16), gradients[0].astype(jnp.bfloat16), gradients[1], gradients[2], gradients[3], gradients[4], gradients[5], gradients[6], gradients[7], gradients[8], gradients[9], gradients[10], gradients[11], gradients[12])
```

```python
import jax
import jax.numpy as jnp
from jax import lax
from jax.sharding import PartitionSpec as P

HEAD = 128
PROMPT = 512
EPS = 1e-05
THETA = 10000.0
MASKED = -1e30
BF = jnp.bfloat16
F32 = jnp.float32
ALL = ("dp", "ctx", "exp")
MOE = ("ctx", "exp")
ROWS = ("dp", "exp")


def dot_nn(a, b):
    return lax.dot_general(a, b, (((1,), (0,)), ((), ())), preferred_element_type=F32)


def dot_tn(a, b):
    return lax.dot_general(a, b, (((0,), (0,)), ((), ())), preferred_element_type=F32)


def dot_nt(a, b):
    return lax.dot_general(a, b, (((1,), (1,)), ((), ())), preferred_element_type=F32)


def rope(v, cos, sin, sign):
    rows, width = v.shape
    half = HEAD // 2
    v = v.reshape(rows, width // HEAD, HEAD)
    a, b = v[..., :half], v[..., half:]
    c, s = cos[:, None, :], sin[:, None, :] * sign
    return jnp.concatenate([a * c - b * s, b * c + a * s], axis=-1).reshape(rows, width)


def per_device(
    hidden_in,
    segments,
    routes,
    attn_gain,
    query_weight,
    key_weight,
    value_weight,
    query_gain,
    key_gain,
    output_weight,
    ffn_gain,
    router_weight,
    gate_weight,
    up_weight,
    down_weight,
    cotangent,
):
    n_dp, n_ctx, n_exp = (lax.axis_size(a) for a in ALL)
    tok, width = hidden_in.shape[2:]
    topk = routes.shape[3]
    experts = n_ctx * n_exp
    cap = (5 * tok * topk + 4 * experts - 1) // (4 * experts)
    group = segments.shape[2]
    shard = query_weight.shape[0]
    cols = width // n_ctx
    piece = cols // n_dp
    heads = cols // HEAD
    scale = HEAD**-0.5
    ctx_me = lax.axis_index("ctx")
    exp_me = lax.axis_index("exp")
    expert_me = ctx_me * n_exp + exp_me

    def own_cols(vec):
        return lax.dynamic_index_in_dim(
            vec.reshape(n_dp, n_ctx, piece), ctx_me, 1, keepdims=False
        ).reshape(cols)

    packed = jnp.stack([query_weight, key_weight, value_weight], axis=1)
    packed = packed.reshape(shard, 3, n_dp, n_ctx, piece).transpose(3, 0, 1, 2, 4)
    packed = lax.all_to_all(packed, "ctx", split_axis=0, concat_axis=0, tiled=True)
    packed = packed.reshape(n_ctx * shard, 3 * cols)
    qkv_w = lax.all_gather(packed, ROWS, axis=0, tiled=True)
    qkv_w = (
        qkv_w.reshape(n_dp, n_exp, n_ctx, shard, 3 * cols)
        .transpose(0, 2, 1, 3, 4)
        .reshape(width, 3 * cols)
    )
    out_w = lax.all_gather(output_weight, ROWS, axis=0, tiled=True)

    own_routes = routes[0, 0]
    expert_ids = jnp.arange(experts, dtype=jnp.int32)
    hits = jnp.sum((own_routes[:, :, None] == expert_ids).astype(jnp.int32), axis=1)
    tokens = jnp.arange(tok, dtype=jnp.int32)
    lower = (tokens[:, None] > tokens[None, :]).astype(BF)
    earlier = dot_nn(lower, hits.astype(BF)).astype(jnp.int32)
    slot_local = jnp.where(hits > 0, earlier, -1).T
    slot = lax.all_to_all(slot_local, MOE, split_axis=0, concat_axis=0, tiled=True)
    pick = (
        slot[:, None, :] == jnp.arange(cap, dtype=jnp.int32)[None, :, None]
    )

    hidden = hidden_in[0, 0].astype(F32)
    labels = segments[0, 0]
    index = jnp.arange(group, dtype=jnp.int32)
    before = jnp.sum((labels[None, :] < labels[:, None]).astype(jnp.int32), axis=1)
    positions = index - before + jnp.where(labels > 0, PROMPT, 0).astype(jnp.int32)
    half = HEAD // 2
    frequency = THETA ** (-(jnp.arange(half, dtype=F32) * 2.0 / HEAD))
    angles = positions.astype(F32)[:, None] * frequency[None, :]
    cos, sin = jnp.cos(angles), jnp.sin(angles)
    attn_gain_f = attn_gain.astype(F32)
    ffn_gain_f = ffn_gain.astype(F32)
    q_gain = own_cols(query_gain.astype(F32))
    k_gain = own_cols(key_gain.astype(F32))

    attn_r = lax.rsqrt(jnp.mean(hidden * hidden, axis=-1, keepdims=True) + EPS)
    normed = (hidden * attn_r * attn_gain_f).astype(BF)
    normed_g = lax.all_gather(normed, "ctx", axis=0, tiled=True)
    raw = dot_nn(normed_g, qkv_w)
    q_raw, k_raw, v_raw = raw[:, :cols], raw[:, cols : 2 * cols], raw[:, 2 * cols :]
    squares = lax.psum(
        jnp.stack([jnp.sum(q_raw * q_raw, axis=1), jnp.sum(k_raw * k_raw, axis=1)]), "ctx"
    )
    inv = lax.rsqrt(squares / width + EPS)
    q_r, k_r = inv[0][:, None], inv[1][:, None]
    q_rot = rope(q_raw * q_r * q_gain, cos, sin, 1.0).astype(BF)
    k_rot = rope(k_raw * k_r * k_gain, cos, sin, 1.0).astype(BF)
    v_low = v_raw.astype(BF)
    q_h, k_h, v_h = (x.reshape(group, heads, HEAD) for x in (q_rot, k_rot, v_low))
    allowed = (index[None, :] <= index[:, None]) & (
        (labels[None, :] == 0) | (labels[None, :] == labels[:, None])
    )
    scores = jnp.einsum("qhd,khd->hqk", q_h, k_h, preferred_element_type=F32) * scale
    prob = jax.nn.softmax(jnp.where(allowed[None], scores, MASKED), axis=-1)
    prob_low = prob.astype(BF)
    mix = (
        jnp.einsum("hqk,khd->qhd", prob_low, v_h, preferred_element_type=F32)
        .reshape(group, cols)
        .astype(BF)
    )
    branch = lax.psum_scatter(
        dot_nn(mix, out_w).astype(BF), "ctx", scatter_dimension=0, tiled=True
    )
    residual = hidden + branch.astype(F32)

    ffn_r = lax.rsqrt(jnp.mean(residual * residual, axis=-1, keepdims=True) + EPS)
    ffn_normed = (residual * ffn_r * ffn_gain_f).astype(BF)
    logits = dot_nn(ffn_normed, router_weight)
    router_prob = jax.nn.softmax(logits, axis=-1)
    gates = jnp.where(hits > 0, router_prob, 0.0).astype(BF)
    rows_all = lax.all_gather(ffn_normed, MOE, axis=0, tiled=False)
    gate_at = lax.all_to_all(gates.T, MOE, split_axis=0, concat_axis=0, tiled=True)
    cot = cotangent[0, 0]
    cot_all = lax.all_gather(cot, MOE, axis=0, tiled=False)

    pick_low = pick.astype(BF)
    combine = jnp.where(pick, gate_at[:, None, :], jnp.zeros((), BF))
    gate_row = jnp.sum(jnp.where(pick, gate_at[:, None, :].astype(F32), 0.0), axis=2)

    def pick_rows(x):
        return lax.dot_general(
            pick_low, x, (((2,), (1,)), ((0,), (0,))), preferred_element_type=F32
        )

    def place_rows(table, x):
        return lax.dot_general(
            table, x, (((1,), (1,)), ((0,), (0,))), preferred_element_type=F32
        )

    total = experts * cap
    received = pick_rows(rows_all).astype(BF).reshape(total, width)
    gate_mat, up_mat, down_mat = gate_weight[0], up_weight[0], down_weight[0]
    gate_pre = dot_nn(received, gate_mat)
    up_pre = dot_nn(received, up_mat)
    sig = jax.nn.sigmoid(gate_pre)
    silu = gate_pre * sig
    expert_hidden = (silu * up_pre).astype(BF)
    expert_out = dot_nn(expert_hidden, down_mat).astype(BF)
    moe_part = place_rows(combine, expert_out.reshape(experts, cap, width)).astype(BF)
    moe_out = lax.psum_scatter(
        moe_part.reshape(experts * tok, width), MOE, scatter_dimension=0, tiled=True
    )
    output = (residual + moe_out.astype(F32)).astype(BF)

    cot_rows = pick_rows(cot_all)
    d_out = (cot_rows * gate_row[:, :, None]).astype(BF).reshape(total, width)
    d_gate_rows = jnp.sum(cot_rows * expert_out.reshape(experts, cap, width).astype(F32), axis=2)
    d_gate_at = jnp.sum(jnp.where(pick, d_gate_rows[:, :, None], 0.0), axis=1)
    d_gate = lax.all_to_all(d_gate_at, MOE, split_axis=0, concat_axis=0, tiled=True).T
    d_hidden_e = dot_nt(d_out, down_mat)
    d_gate_pre = (d_hidden_e * up_pre * sig * (1.0 + gate_pre * (1.0 - sig))).astype(BF)
    d_up_pre = (d_hidden_e * silu).astype(BF)
    d_disp = (dot_nt(d_gate_pre, gate_mat) + dot_nt(d_up_pre, up_mat)).astype(BF)
    d_part = place_rows(pick_low, d_disp.reshape(experts, cap, width)).astype(BF)
    d_tokens = lax.psum_scatter(
        d_part.reshape(experts * tok, width), MOE, scatter_dimension=0, tiled=True
    )
    down_grad = dot_tn(expert_hidden, d_out)
    gate_grad = dot_tn(received, d_gate_pre)
    up_grad = dot_tn(received, d_up_pre)
    gate_sum, up_sum, down_sum = (
        lax.psum(g.astype(BF), "dp").astype(F32) for g in (gate_grad, up_grad, down_grad)
    )

    d_router = d_gate
    d_logits = (
        router_prob * (d_router - jnp.sum(router_prob * d_router, axis=-1, keepdims=True))
    ).astype(BF)
    router_grad = dot_tn(d_logits, ffn_normed)
    d_ffn = d_tokens.astype(F32) + dot_nt(d_logits, router_weight)
    ffn_gain_grad = jnp.sum(d_ffn * residual * ffn_r, axis=0)
    weighted = d_ffn * ffn_gain_f
    d_residual = cot.astype(F32) + (
        weighted * ffn_r
        - residual * ffn_r**3 * jnp.mean(residual * weighted, axis=-1, keepdims=True)
    )
    d_branch = d_residual.astype(BF)

    d_branch_g = lax.all_gather(d_branch, "ctx", axis=0, tiled=True)
    out_grad = dot_tn(mix, d_branch_g)
    d_mix_h = dot_nt(d_branch_g, out_w).astype(BF).reshape(group, heads, HEAD)
    d_prob = jnp.einsum("qhd,khd->hqk", d_mix_h, v_h, preferred_element_type=F32)
    row_total = jnp.sum(prob * d_prob, axis=-1, keepdims=True)
    d_scores = (prob * (d_prob - row_total)).astype(BF)
    d_q = jnp.einsum("hqk,khd->qhd", d_scores, k_h, preferred_element_type=F32)
    d_k = jnp.einsum("hqk,qhd->khd", d_scores, q_h, preferred_element_type=F32)
    d_v = jnp.einsum("hqk,qhd->khd", prob_low, d_mix_h, preferred_element_type=F32)
    d_qn = rope(d_q.reshape(group, cols) * scale, cos, sin, -1.0)
    d_kn = rope(d_k.reshape(group, cols) * scale, cos, sin, -1.0)
    q_gain_part = jnp.sum(d_qn * q_raw * q_r, axis=0)
    k_gain_part = jnp.sum(d_kn * k_raw * k_r, axis=0)
    d_qw, d_kw = d_qn * q_gain, d_kn * k_gain
    dots = (
        lax.psum(jnp.stack([jnp.sum(q_raw * d_qw, axis=1), jnp.sum(k_raw * d_kw, axis=1)]), "ctx")
        / width
    )
    d_q_raw = d_qw * q_r - q_raw * q_r**3 * dots[0][:, None]
    d_k_raw = d_kw * k_r - k_raw * k_r**3 * dots[1][:, None]
    d_raw = jnp.concatenate(
        [d_q_raw.astype(BF), d_k_raw.astype(BF), d_v.reshape(group, cols).astype(BF)], axis=1
    )
    d_normed = lax.psum_scatter(
        dot_nt(d_raw, qkv_w).astype(BF), "ctx", scatter_dimension=0, tiled=True
    ).astype(F32)
    attn_gain_grad = jnp.sum(d_normed * hidden * attn_r, axis=0)
    weighted = d_normed * attn_gain_f
    hidden_grad = (
        d_residual
        + weighted * attn_r
        - hidden * attn_r**3 * jnp.mean(hidden * weighted, axis=-1, keepdims=True)
    ).astype(BF)

    qkv_grad = dot_tn(normed_g, d_raw).astype(BF)
    qkv_grad = (
        qkv_grad.reshape(n_dp, n_ctx, n_exp, shard, 3 * cols)
        .transpose(0, 2, 1, 3, 4)
        .reshape(width, 3 * cols)
    )
    qkv_sum = lax.psum_scatter(qkv_grad, ROWS, scatter_dimension=0, tiled=True)
    qkv_sum = lax.all_to_all(
        qkv_sum.reshape(n_ctx, shard, 3, n_dp, piece), "ctx", split_axis=0, concat_axis=0, tiled=True
    )
    qkv_sum = qkv_sum.transpose(2, 1, 3, 0, 4).reshape(3, shard, width).astype(F32)
    out_sum = lax.psum_scatter(
        out_grad.astype(BF), ROWS, scatter_dimension=0, tiled=True
    ).astype(F32)

    spread = jnp.zeros((2, n_dp, n_ctx, piece), F32)
    spread = lax.dynamic_update_slice(
        spread,
        jnp.stack([q_gain_part, k_gain_part]).reshape(2, n_dp, 1, piece),
        (0, 0, ctx_me, 0),
    ).reshape(2, width)
    early = lax.psum(jnp.concatenate([router_grad, ffn_gain_grad[None]], axis=0), ALL)
    late = lax.psum(jnp.concatenate([spread, attn_gain_grad[None]], axis=0), ALL)
    return (
        output[None, None],
        hidden_grad[None, None],
        late[2],
        qkv_sum[0],
        qkv_sum[1],
        qkv_sum[2],
        late[0],
        late[1],
        out_sum,
        early[experts],
        early[:experts].T,
        gate_sum[None],
        up_sum[None],
        down_sum[None],
    )


def solution(mesh):
    tokens = P("dp", "exp", "ctx", None)
    rows = P(ALL, None)
    expert = P(MOE, None, None)
    return jax.shard_map(
        per_device,
        mesh=mesh,
        in_specs=(
            tokens,
            P("dp", "exp", None),
            tokens,
            P(),
            rows,
            rows,
            rows,
            P(),
            P(),
            rows,
            P(),
            P(),
            expert,
            expert,
            expert,
            tokens,
        ),
        out_specs=(
            tokens,
            tokens,
            P(),
            rows,
            rows,
            rows,
            P(),
            P(),
            rows,
            P(),
            P(),
            expert,
            expert,
            expert,
        ),
        check_vma=False,
    )
```

```python
import functools

import jax
import jax.numpy as jnp
from jax import lax
from jax.experimental import pallas as pl
from jax.experimental.pallas import tpu as pltpu
from jax.sharding import PartitionSpec as P

HEAD = 128
PROMPT = 512
EPS = 1e-05
THETA = 10000.0
MASKED = -1e30
BF = jnp.bfloat16
F32 = jnp.float32
ALL = ("dp", "ctx", "exp")
MOE = ("ctx", "exp")
ROWS = ("dp", "exp")
MESH = pl.DeviceIdType.MESH


def by_distance(me, n):
    far=[jnp.abs(me-j)*n+j for j in range(n)]
    rank=[sum(((far[i]>far[j]).astype(jnp.int32) for i in range(n) if i!=j), jnp.int32(0)) for j in range(n)]
    def at(k):
        v=jnp.int32(0)
        for j in range(n): v=v+jnp.where(rank[j]==k,j,0)
        return v
    return at


def loop(n, body):
    def step(i,_):
        body(i)
        return 0
    lax.fori_loop(0,n,step,0)


def add_into(dst, src, rows=16):
    n=dst.shape[-2]//rows
    lead=dst.shape[:-2]
    assert not lead
    def body(i,_):
        sl=pl.ds(pl.multiple_of(i*rows,rows),rows)
        dst[sl,:]=(dst[sl,:].astype(F32)+src[sl,:].astype(F32)).astype(dst.dtype)
        return 0
    lax.fori_loop(0,n,body,0)


def add3(dst,src):
    if len(dst.shape)==2: add_into(dst,src); return
    def body(i,_):
        add_into(dst.at[i],src.at[i]); return 0
    lax.fori_loop(0,dst.shape[0],body,0)

def tail_kernel(N,C,E,gq,go,dn,oq,oo,od,own_q,own_o,own_d,yq,yo,uq,uo,vq,vo,d1,d2,ld,ldd,ys,yr,zs,zu,zd,s1,r1,s2,r2,a_s,a_r,osem):
    p=lax.axis_index("dp"); c=lax.axis_index("ctx"); e=lax.axis_index("exp")
    H=C//2; h=c//2; l=c%2
    def dpeer(j): return lax.rem(p+j,N)
    def cpeer(j): return lax.rem(c+j,C)
    def hpeer(j): return lax.rem(h+j,H)
    bar=pltpu.get_barrier_semaphore()
    def sig(**kw): pl.semaphore_signal(bar,inc=1,device_id=kw,device_id_type=MESH)
    for j in range(1,N): sig(dp=dpeer(j))
    for j in range(1,C): sig(ctx=cpeer(j))
    @pl.when(e>0)
    def _(): sig(exp=e-1)
    @pl.when(e<E-1)
    def _(): sig(exp=e+1)
    order=by_distance(e,E)
    def rc(src,dst,ss,rs,**kw): return pltpu.make_async_remote_copy(src,dst,ss,rs,device_id=kw,device_id_type=MESH)
    def loads(o): return [pltpu.make_async_copy(gq.at[p,:,o],own_q.at[o],ld.at[0,o]),pltpu.make_async_copy(go.at[p,o],own_o.at[o],ld.at[1,o])]
    def cy(j,o):
        q=dpeer(j)
        return [rc(gq.at[q,:,o],yq.at[j-1,o],ys.at[0,j-1,o],yr.at[0,j-1,o],dp=q), rc(go.at[q,o],yo.at[j-1,o],ys.at[1,j-1,o],yr.at[1,j-1,o],dp=q)]
    def cu(o): return [rc(own_q.at[o],uq.at[o],zs.at[0,o],zu.at[0,o],exp=e+1), rc(own_o.at[o],uo.at[o],zs.at[1,o],zu.at[1,o],exp=e+1)]
    def cd(o): return [rc(own_q.at[o],vq.at[o],zs.at[0,o],zd.at[0,o],exp=e-1), rc(own_o.at[o],vo.at[o],zs.at[1,o],zd.at[1,o],exp=e-1)]
    def loadd(hh): return pltpu.make_async_copy(dn.at[hh*2+l],own_d.at[hh],ldd.at[hh])
    def c1(hh): return rc(dn.at[hh*2+1-l],d1.at[hh],s1.at[hh],r1.at[hh],ctx=h*2+1-l)
    def c2(j):
        hh=hpeer(j); return rc(own_d.at[hh],d2.at[j-1],s2.at[j-1],r2.at[j-1],ctx=hh*2+l)
    hs=[hpeer(j) for j in range(1,H)]+[h]
    def start_loads(k):
        for x in loads(k): x.start()
    loop(E,start_loads)
    for hh in hs: loadd(hh).start()
    pl.semaphore_wait(bar,(N-1)+(C-1)+(e>0).astype(jnp.int32)+(e<E-1).astype(jnp.int32))
    for j in range(1,N):
        for x in cy(j,order(0)): x.start()
    for hh in hs: c1(hh).start()
    def start_dp(k):
        for j in range(1,N):
            for x in cy(j,order(k+1)): x.start()
    loop(E-1,start_dp)
    for i,hh in enumerate(hs):
        loadd(hh).wait(); c1(hh).wait_recv(); add_into(own_d.at[hh],d1.at[hh])
        if i<H-1: c2(i+1).start()
    def line(k):
        o=order(k)
        for x in loads(o): x.wait()
        for j in range(1,N):
            for x in cy(j,o): x.wait_recv()
            add3(own_q.at[o],yq.at[j-1,o]); add3(own_o.at[o],yo.at[j-1,o])
        if True:
            @pl.when(o>e)
            def _():
                @pl.when(e>0)
                def _():
                    for x in cu(o): x.wait_recv()
                    add3(own_q.at[o],uq.at[o]); add3(own_o.at[o],uo.at[o])
                for x in cu(o): x.start()
            @pl.when(o<e)
            def _():
                @pl.when(e<E-1)
                def _():
                    for x in cd(o): x.wait_recv()
                    add3(own_q.at[o],vq.at[o]); add3(own_o.at[o],vo.at[o])
                for x in cd(o): x.start()
    def lines(k):
        line(k)
        @pl.when(k==0)
        def _():
            for j in range(1,H):
                c2(j).wait_recv(); add_into(own_d.at[h],d2.at[j-1])
            pltpu.make_async_copy(own_d.at[h],od,osem.at[0]).start()
    loop(E,lines)
    @pl.when(e>0)
    def _():
        for x in cu(e): x.wait_recv()
        add3(own_q.at[e],uq.at[e]); add3(own_o.at[e],uo.at[e])
    @pl.when(e<E-1)
    def _():
        for x in cd(e): x.wait_recv()
        add3(own_q.at[e],vq.at[e]); add3(own_o.at[e],vo.at[e])
    def ca(j):
        q=cpeer(j); return rc(own_q.at[e,q],oq.at[c],a_s.at[j-1],a_r.at[j-1],ctx=q)
    for j in range(1,C): ca(j).start()
    l1=pltpu.make_async_copy(own_q.at[e,c],oq.at[c],osem.at[1]); l1.start()
    l2=pltpu.make_async_copy(own_o.at[e],oo,osem.at[2]); l2.start()
    def drain(k):
        for j in range(1,N):
            for x in cy(j,k): x.wait_send()
        @pl.when(k!=e)
        def _():
            for x in cu(k): x.wait_send()
    loop(E,drain)
    for hh in hs: c1(hh).wait_send()
    for j in range(1,H): c2(j).wait_send()
    for j in range(1,C):
        ca(j).wait_send();
        src=lax.rem(c+C-j,C)
        rc(own_q.at[e,c],oq.at[src],a_s.at[j-1],a_r.at[j-1],ctx=src).wait_recv()
    pltpu.make_async_copy(own_d.at[h],od,osem.at[0]).wait(); l1.wait(); l2.wait()

def tail(gq,go,dn,cid=2):
    N,C,E,S,W3=gq.shape; D=go.shape[-1]; T=dn.shape[1]; H=C//2
    dma=pltpu.SemaphoreType.DMA; V=lambda *s: pltpu.VMEM(s,BF)
    return pl.pallas_call(functools.partial(tail_kernel,N,C,E),
        out_shape=[jax.ShapeDtypeStruct((C,S,W3),BF),jax.ShapeDtypeStruct((S,D),BF),jax.ShapeDtypeStruct((T,D),BF)],
        in_specs=[pl.BlockSpec(memory_space=pl.ANY)]*3,
        out_specs=[pl.BlockSpec(memory_space=pl.ANY)]*3,
        scratch_shapes=[V(E,C,S,W3),V(E,S,D),V(H,T,D),V(N-1,E,C,S,W3),V(N-1,E,S,D),V(E,C,S,W3),V(E,S,D),V(E,C,S,W3),V(E,S,D),V(H,T,D),V(H-1,T,D),
            dma((2,E)),dma((H,)),dma((2,N-1,E)),dma((2,N-1,E)),dma((2,E)),dma((2,E)),dma((2,E)),dma((H,)),dma((H,)),dma((H-1,)),dma((H-1,)),dma((C-1,)),dma((C-1,)),dma((3,))],
        compiler_params=pltpu.CompilerParams(collective_id=cid,has_side_effects=True,vmem_limit_bytes=60*2**20),
        name="tail")(gq,go,dn)

def sums_kernel(sizes,x_ref,o_ref,*scr):
    names=("dp","ctx","exp")
    bufs=scr[:3]; ss=scr[3:6]; rs=scr[6:9]
    bar=pltpu.get_barrier_semaphore(); cnt=0
    me=[lax.axis_index(a) for a in names]
    for a,n,i in zip(names,sizes,me):
        for j in range(1,n):
            pl.semaphore_signal(bar,inc=1,device_id={a:lax.rem(i+j,n)},device_id_type=MESH); cnt+=1
    pl.semaphore_wait(bar,cnt)
    for t,(a,n,i) in enumerate(zip(names,sizes,me)):
        buf=bufs[t]
        buf[i]=x_ref[...] if t==0 else o_ref[...]
        def cp(j): return pltpu.make_async_remote_copy(buf.at[i],buf.at[i],ss[t].at[j-1],rs[t].at[j-1],device_id={a:lax.rem(i+j,n)},device_id_type=MESH)
        for j in range(1,n): cp(j).start()
        for j in range(1,n):
            src=lax.rem(i+n-j,n)
            pltpu.make_async_remote_copy(buf.at[src],buf.at[src],ss[t].at[j-1],rs[t].at[j-1],device_id={a:src},device_id_type=MESH).wait_recv()
        acc=buf[0]
        for j in range(1,n): acc=acc+buf[j]
        o_ref[...]=acc
        for j in range(1,n): cp(j).wait_send()

def sums(x,sizes,cid=3):
    R,D=x.shape; dma=pltpu.SemaphoreType.DMA
    return pl.pallas_call(functools.partial(sums_kernel,sizes),out_shape=jax.ShapeDtypeStruct((R,D),F32),
        in_specs=[pl.BlockSpec(memory_space=pltpu.VMEM)],out_specs=pl.BlockSpec(memory_space=pltpu.VMEM),
        scratch_shapes=[pltpu.VMEM((n,R,D),F32) for n in sizes]+[dma((n-1,)) for n in sizes]*2,
        compiler_params=pltpu.CompilerParams(collective_id=cid,has_side_effects=True,vmem_limit_bytes=32*2**20),name="sums")(x)


def nn(a,b): return lax.dot_general(a,b,(((1,),(0,)),((),())),preferred_element_type=F32)
def tn(a,b): return lax.dot_general(a,b,(((0,),(0,)),((),())),preferred_element_type=F32)
def nt(a,b): return lax.dot_general(a,b,(((1,),(1,)),((),())),preferred_element_type=F32)

def pick_of(slot_row, cap):
    T=slot_row.shape[1]
    return jnp.broadcast_to(slot_row,(cap,T))==lax.broadcasted_iota(jnp.int32,(cap,T),0)

def back_kernel(H,E,cap,slot,dgp,dup,gw,uw,o_ref,own,r1,r2,rz,snd,gb,ub,slv,wg,wu,ld_sem,w_sem,s1,q1,s2,q2,s3,qz,o_sem):
    c=lax.axis_index("ctx"); e=lax.axis_index("exp")
    h=c//2; l=c%2
    T,W=own.shape[2:]; FF=wg.shape[1]
    sib={"ctx":h*2+1-l}
    def xpeer(j): return lax.rem(h+j,H)
    bar=pltpu.get_barrier_semaphore()
    pl.semaphore_signal(bar,inc=1,device_id=sib,device_id_type=MESH)
    for j in range(1,H):
        pl.semaphore_signal(bar,inc=1,device_id={"ctx":xpeer(j)*2+l},device_id_type=MESH)
    @pl.when(e>0)
    def _(): pl.semaphore_signal(bar,inc=1,device_id={"exp":e-1},device_id_type=MESH)
    @pl.when(e<E-1)
    def _(): pl.semaphore_signal(bar,inc=1,device_id={"exp":e+1},device_id_type=MESH)
    order=by_distance(e,E)
    wl=[pltpu.make_async_copy(gw,wg,w_sem.at[0]),pltpu.make_async_copy(uw,wu,w_sem.at[1])]
    for x in wl: x.start()
    NS=snd.shape[0]; M=H*E
    def place(m):
        return lax.rem(h+1+m//E,H),order(lax.rem(m,E))
    def loads(n):
        hh,o=place(n//2)
        s=(hh*2+jnp.where(lax.rem(n,2)==0,1-l,l))*E+o; b=lax.rem(n,2)
        return [pltpu.make_async_copy(dgp.at[s],gb.at[b],ld_sem.at[0,b]),pltpu.make_async_copy(dup.at[s],ub.at[b],ld_sem.at[1,b])],s
    for x in loads(0)[0]: x.start()
    def c1(m):
        hh,o=place(m)
        return pltpu.make_async_remote_copy(snd.at[lax.rem(m,NS)],r1.at[hh,o],s1.at[m],q1.at[hh,o],device_id=sib,device_id_type=MESH)
    def c2(j,o):
        hh=xpeer(j)
        return pltpu.make_async_remote_copy(own.at[hh,o],r2.at[j-1,o],s2.at[j-1,o],q2.at[j-1,o],device_id={"ctx":hh*2+l},device_id_type=MESH)
    def cz(o,to,slot_): return pltpu.make_async_remote_copy(own.at[h,o],rz.at[slot_],s3.at[o],qz.at[slot_],device_id={"exp":to},device_id_type=MESH)
    step=min(512,W)
    def compute(n,dst):
        x,s=loads(n); b=lax.rem(n,2)
        for y in x: y.wait()
        @pl.when(n+1<2*M)
        def _():
            for y in loads(n+1)[0]: y.start()
        low=pick_of(slv[pl.ds(s,1),:],cap).astype(F32).astype(BF)
        def body(i):
            sl=pl.ds(pl.multiple_of(i*step,step),step)
            d=(nt(gb[b],wg[sl,:])+nt(ub[b],wu[sl,:])).astype(BF)
            dst[:,sl]=tn(low,d).astype(BF)
        loop(W//step,body)
    pltpu.sync_copy(slot,slv)
    for x in wl: x.wait()
    pl.semaphore_wait(bar,H+(e>0).astype(jnp.int32)+(e<E-1).astype(jnp.int32))
    def zstep(k):
        o=order(k)
        for j in range(1,H):
            c2(j,o).wait_recv()
            add_into(own.at[h,o],r2.at[j-1,o])
        @pl.when(o>e)
        def _():
            @pl.when(e>0)
            def _():
                cz(o,e-1,o).wait_recv(); add_into(own.at[h,o],rz.at[o])
            cz(o,e+1,o).start()
        @pl.when(o<e)
        def _():
            @pl.when(e<E-1)
            def _():
                cz(o,e+1,o).wait_recv(); add_into(own.at[h,o],rz.at[o])
            cz(o,e-1,jnp.where(o==e-1,E,o)).start()
    def pair(m):
        hh,o=place(m)
        @pl.when(m>=NS)
        def _(): c1(m-NS).wait_send()
        compute(2*m,snd.at[lax.rem(m,NS)])
        c1(m).start()
        compute(2*m+1,own.at[hh,o])
        c1(m).wait_recv()
        add_into(own.at[hh,o],r1.at[hh,o])
        for j in range(1,H):
            @pl.when(m//E==j-1)
            def _(): c2(j,o).start()
        @pl.when(m//E==H-1)
        def _(): zstep(lax.rem(m,E))
    loop(M,pair)
    for m in range(max(0,M-NS),M): c1(m).wait_send()
    @pl.when(e>0)
    def _():
        cz(e,e-1,e).wait_recv(); add_into(own.at[h,e],rz.at[e])
    @pl.when(e<E-1)
    def _():
        cz(e,e+1,E).wait_recv(); add_into(own.at[h,e],rz.at[E])
    out=pltpu.make_async_copy(own.at[h,e],o_ref,o_sem); out.start()
    def drain(k):
        for j in range(1,H): c2(j,order(k)).wait_send()
        @pl.when(k<E-1)
        def _(): cz(order(k),e,order(k)).wait_send()
    loop(E,drain)
    out.wait()


def back_call(slot,dgp,dup,gw,uw,C,E,T,cids):
    S,cap,FF=dgp.shape; D=gw.shape[0]; H=C//2
    dma=pltpu.SemaphoreType.DMA; V=lambda *s: pltpu.VMEM(s,BF)
    blocks=2*H*E+(H-1)*E+E+4
    parts=1
    while 2*(blocks*T*D//parts+2*D//parts*FF+4*cap*FF)>60*2**20: parts*=2
    W=D//parts
    def part(i):
        a,b=(gw,uw) if parts==1 else (gw[i*W:(i+1)*W],uw[i*W:(i+1)*W])
        return pl.pallas_call(functools.partial(back_kernel,H,E,cap),
            out_shape=jax.ShapeDtypeStruct((T,W),BF),
            in_specs=[pl.BlockSpec(memory_space=pl.ANY)]*5,
            out_specs=pl.BlockSpec(memory_space=pl.ANY),
            scratch_shapes=[V(H,E,T,W),V(H,E,T,W),V(H-1,E,T,W),V(E+1,T,W),V(3,T,W),V(2,cap,FF),V(2,cap,FF),pltpu.VMEM((S,T),jnp.int32),V(W,FF),V(W,FF),
                dma((2,2)),dma((2,)),dma((H*E,)),dma((H,E)),dma((H-1,E)),dma((H-1,E)),dma((E,)),dma((E+1,)),dma(())],
            cost_estimate=pl.CostEstimate(flops=2*S*cap*(2*W*FF+T*W),bytes_accessed=S*4*cap*FF,transcendentals=0),
            compiler_params=pltpu.CompilerParams(collective_id=cids[i],has_side_effects=True,vmem_limit_bytes=61*2**20),
            name="back")(slot,dgp,dup,a,b)
    out=[part(i) for i in range(parts)]
    return out[0] if parts==1 else jnp.concatenate(out,axis=1)

def fwd_kernel(H,E,T,cap,in_vmem,slot,rows,cot,gw,uw,dw,recv,hid,dout,dgp,dup,moe,dg,*scr):
    if in_vmem: allr=scr[0]; scr=scr[1:]; rb=None
    else: allr=scr[0]; rb=scr[1]; scr=scr[2:]
    (slv,wg,wu,wd,cb,srecv,shid,sdout,sdgp,sdup,smoe,sdg,cr,w_sem,c_sem,l_sem,o_sem,up_s,dn_s,up_r,dn_r,x_s,x_r,b_s,b_r)=scr
    c=lax.axis_index("ctx"); e=lax.axis_index("exp")
    h=c//2; l=c%2; C=2*H; S=C*E
    D=wg.shape[0]; FF=wg.shape[1]; EXT=allr.shape[1]
    expert=c*E+e
    def xpeer(j): return lax.rem(h+j,H)
    def idx(hh,ll,ee): return (hh*2+ll)*E+ee
    bar=pltpu.get_barrier_semaphore()
    pl.semaphore_signal(bar,inc=1,device_id={"ctx":h*2+1-l},device_id_type=MESH)
    for j in range(1,H):
        pl.semaphore_signal(bar,inc=1,device_id={"ctx":xpeer(j)*2+l},device_id_type=MESH)
    @pl.when(e>0)
    def _(): pl.semaphore_signal(bar,inc=1,device_id={"exp":e-1},device_id_type=MESH)
    @pl.when(e<E-1)
    def _(): pl.semaphore_signal(bar,inc=1,device_id={"exp":e+1},device_id_type=MESH)
    order=by_distance(e,E)
    def near(k): return order(E-1-k)
    own=idx(h,l,e)
    wl=[pltpu.make_async_copy(a,b,w_sem.at[i]) for i,(a,b) in enumerate(((gw,wg),(uw,wu),(dw,wd)))]
    first=pltpu.make_async_copy(rows,allr.at[own],w_sem.at[3])
    first.start()
    for x in wl: x.start()
    def job(n):
        m=jnp.maximum(n-2,0)
        r=jnp.where(n<2,0,1+m//(2*H)); t=jnp.where(n<2,n,lax.rem(m,2*H))
        t=jnp.where(r==E,t+2,t)
        j=t//2
        return r,t,j,lax.rem(t,2),jnp.where(j==0,r,r-1)
    def hi(j): return jnp.where(j==0,h,lax.rem(h+H-j,H))
    def sender(n):
        r,t,j,s,k=job(n)
        return idx(hi(j),jnp.where(s==1,1-l,l),near(k))
    def cload(n): return pltpu.make_async_copy(cot.at[sender(n)],cb.at[lax.rem(n,2)],c_sem.at[lax.rem(n,2)])
    cload(0).start()
    def rc(i,ss,rs,**kw): return pltpu.make_async_remote_copy(allr.at[i],allr.at[i],ss,rs,device_id=kw,device_id_type=MESH)
    def up(ee): return rc(idx(h,l,ee),up_s.at[ee],up_r.at[ee],exp=e+1)
    def dn(ee): return rc(idx(h,l,ee),dn_s.at[ee],dn_r.at[ee],exp=e-1)
    def xs(j,ee): return rc(idx(h,l,ee),x_s.at[j-1,ee],x_r.at[j-1,ee],ctx=xpeer(j)*2+l)
    def xr(j,ee):
        return rc(idx(hi(j),l,ee),x_s.at[j-1,ee],x_r.at[j-1,ee],ctx=hi(j)*2+l)
    def bs(j,ee): return rc(idx(hi(j),l,ee),b_s.at[j,ee],b_r.at[j,ee],ctx=h*2+1-l)
    def br(j,ee): return rc(idx(hi(j),1-l,ee),b_s.at[j,ee],b_r.at[j,ee],ctx=h*2+1-l)
    outs=[(srecv,recv),(shid,hid),(sdout,dout),(sdgp,dgp),(sdup,dup),(smoe,moe),(sdg,dg)]
    def odma(n):
        s=sender(n); b=lax.rem(n,2)
        return [pltpu.make_async_copy(a.at[b],o.at[s],o_sem.at[i,b]) for i,(a,o) in enumerate(outs)]
    def compute(n):
        s=sender(n); b=lax.rem(n,2)
        if in_vmem: rw=allr.at[s]
        else:
            cp=pltpu.make_async_copy(allr.at[s],rb,l_sem); cp.start(); cp.wait(); rw=rb
        cload(n).wait()
        @pl.when(n+1<S)
        def _(): cload(n+1).start()
        @pl.when(n>=2)
        def _():
            for x in odma(n-2): x.wait()
        ct=cb.at[b]
        pk=pick_of(slv[pl.ds(s,1),:],cap); pf=pk.astype(F32); low=pf.astype(BF)
        gm=rw[T:EXT,:T].astype(F32)
        g=jnp.sum(jnp.where(lax.broadcasted_iota(jnp.int32,gm.shape,0)==expert,gm,0.0),axis=0,keepdims=True)
        gsel=jnp.where(pk,jnp.broadcast_to(g,(cap,T)),0.0)
        grow=jnp.sum(gsel,axis=1,keepdims=True)
        comb=gsel.astype(BF)
        step=512
        for m in range(0,D,step):
            srecv[b,:,m:m+step]=nn(low,rw[:T,m:m+step]).astype(BF)
            q=nn(low,ct[:,m:m+step])
            sdout[b,:,m:m+step]=(q*grow).astype(BF)
            cr[:,m:m+step]=q.astype(BF)
        half=FF//2
        for m in range(0,FF,half):
            gp=nn(srecv[b],wg[:,m:m+half]); upp=nn(srecv[b],wu[:,m:m+half])
            dh=nt(sdout[b],wd[m:m+half,:])
            sg=jax.nn.sigmoid(gp); si=gp*sg
            shid[b,:,m:m+half]=(si*upp).astype(BF)
            sdgp[b,:,m:m+half]=(dh*upp*sg*(1.0+gp*(1.0-sg))).astype(BF)
            sdup[b,:,m:m+half]=(dh*si).astype(BF)
        acc=jnp.zeros((cap,1),F32)
        for m in range(0,D,step):
            ev=nn(shid[b],wd[:,m:m+step]).astype(BF)
            acc=acc+jnp.sum(cr[:,m:m+step].astype(F32)*ev.astype(F32),axis=1,keepdims=True)
            smoe[b,:,m:m+step]=tn(comb,ev).astype(BF)
        sdg[b]=jnp.sum(pf*acc,axis=0,keepdims=True)
        for x in odma(n): x.start()
    pltpu.sync_copy(slot,slv)
    first.wait()
    pl.semaphore_wait(bar,H+(e>0).astype(jnp.int32)+(e<E-1).astype(jnp.int32))
    @pl.when(e<E-1)
    def _(): up(e).start()
    @pl.when(e>0)
    def _(): dn(e).start()
    for j in range(1,H): xs(j,e).start()
    bs(0,e).start()
    for x in wl: x.wait()
    def step_(n):
        r,t,j,sib_,k=job(n)
        @pl.when(jnp.logical_and(t==0,r>0))
        def _():
            @pl.when(e>=r)
            def _():
                up(e-r).wait_recv()
                @pl.when(e<E-1)
                def _(): up(e-r).start()
                for q in range(1,H): xs(q,e-r).start()
                bs(0,e-r).start()
            @pl.when(e+r<E)
            def _():
                dn(e+r).wait_recv()
                @pl.when(e>0)
                def _(): dn(e+r).start()
                for q in range(1,H): xs(q,e+r).start()
                bs(0,e+r).start()
        @pl.when(jnp.logical_and(sib_==0,j>0))
        def _():
            xr(j,near(k)).wait_recv(); bs(j,near(k)).start()
        @pl.when(sib_==1)
        def _(): br(j,near(k)).wait_recv()
        compute(n)
    loop(S,step_)
    for x in odma(S-2)+odma(S-1): x.wait()
    def drain(ee):
        @pl.when(jnp.logical_and(e<E-1,ee<=e))
        def _(): up(ee).wait_send()
        @pl.when(jnp.logical_and(e>0,ee>=e))
        def _(): dn(ee).wait_send()
        for j in range(1,H): xs(j,ee).wait_send()
        for j in range(H): bs(j,ee).wait_send()
    loop(E,drain)


def fwd_call(slot,rows,cot,gw,uw,dw,cap,C,E,T,cid=4):
    EXT,D=rows.shape; S=C*E; H=C//2; FF=gw.shape[1]
    dma=pltpu.SemaphoreType.DMA; V=lambda *s: pltpu.VMEM(s,BF)
    in_vmem=S*EXT*D*2<=28*2**20
    A=pl.BlockSpec(memory_space=pl.ANY)
    sd=lambda a,b,dt=BF: jax.ShapeDtypeStruct((S,a,b),dt)
    out_shape=[sd(cap,D),sd(cap,FF),sd(cap,D),sd(cap,FF),sd(cap,FF),sd(T,D),sd(1,T,F32)]
    land=[V(S,EXT,D)] if in_vmem else [V(EXT,D)]
    if not in_vmem: out_shape=out_shape+[sd(EXT,D)]
    body=functools.partial(fwd_kernel,H,E,T,cap,in_vmem)
    r=pl.pallas_call(body,out_shape=out_shape,in_specs=[A]*6,out_specs=[A]*len(out_shape),
        scratch_shapes=land+[pltpu.VMEM((S,T),jnp.int32),V(D,FF),V(D,FF),V(FF,D),V(2,T,D),V(2,cap,D),V(2,cap,FF),V(2,cap,D),V(2,cap,FF),V(2,cap,FF),V(2,T,D),pltpu.VMEM((2,1,T),F32),V(cap,D),
            dma((4,)),dma((2,)),dma(()),dma((7,2)),dma((E,)),dma((E,)),dma((E,)),dma((E,)),dma((H-1,E)),dma((H-1,E)),dma((H,E)),dma((H,E))],
        cost_estimate=pl.CostEstimate(flops=2*S*cap*(4*D*FF+3*T*D),bytes_accessed=S*2*(T*D+2*cap*D+3*cap*FF+T*D)+6*D*FF,transcendentals=S*cap*FF),
        compiler_params=pltpu.CompilerParams(collective_id=cid,has_side_effects=True,vmem_limit_bytes=61*2**20),name="experts_fwd")(slot,rows,cot,gw,uw,dw)
    return r[:7]


def mask_bias(lab_r,lab_c,i0,bq,K):
    lr=lab_r[:,:K]; lc=lab_c
    row=lax.broadcasted_iota(jnp.int32,(bq,K),0)+i0; col=lax.broadcasted_iota(jnp.int32,(bq,K),1)
    ok=(col<=row)&((lr==0)|(lr==lc))
    return jnp.where(ok,0.0,-1e30).astype(F32)

def attn_fwd_kernel(heads,bq,scale,raw,rr,cos,sin,lab_r,lab_c,gains,qo,ko,vo,mix,bias):
    G=raw.shape[0]; cols=heads*HEAD
    rb=min(128,G)
    def prep(i,_):
        sl=pl.ds(pl.multiple_of(i*rb,rb),rb)
        cs,sn=cos[sl,:],sin[sl,:]
        for t,o in ((0,qo),(1,ko)):
            r=rr[sl,t:t+1]
            for hd in range(heads):
                a=hd*HEAD
                v=raw[sl,t*cols+a:t*cols+a+HEAD]*r*gains[t:t+1,a:a+HEAD]
                o[sl,a:a+HEAD]=(v*cs+pltpu.roll(v,HEAD//2,1)*sn).astype(BF)
        vo[sl,:]=raw[sl,2*cols:].astype(BF)
        return 0
    lax.fori_loop(0,G//rb,prep,0)
    def block(i,K):
        rows=pl.ds(pl.multiple_of(i*bq,bq),bq)
        bias[:,:K]=mask_bias(lab_r,lab_c[rows,:],i*bq,bq,K)
        def head(hd,_):
            ln=pl.ds(pl.multiple_of(hd*HEAD,HEAD),HEAD)
            s=nt(qo[rows,ln],ko[:K,ln])*scale+bias[:,:K]
            p=jnp.exp(s-jnp.max(s,axis=1,keepdims=True))
            pr=(p*(1.0/jnp.sum(p,axis=1,keepdims=True))).astype(BF)
            mix[rows,ln]=nn(pr,vo[:K,ln]).astype(BF)
            return 0
        lax.fori_loop(0,heads,head,0)
    per=G//bq//3
    for g in range(3):
        loop(per,lambda i,g=g: block(i+g*per,(g+1)*per*bq))

def attn_fwd(raw,rr,cos,sin,lab_r,lab_c,gains,heads,bq=128):
    G=raw.shape[0]; cols=heads*HEAD
    o=jax.ShapeDtypeStruct((G,cols),BF)
    V=pl.BlockSpec(memory_space=pltpu.VMEM)
    return pl.pallas_call(functools.partial(attn_fwd_kernel,heads,bq,HEAD**-0.5),out_shape=[o]*4,in_specs=[V]*7,out_specs=[V]*4,
        scratch_shapes=[pltpu.VMEM((bq,G),F32)],
        cost_estimate=pl.CostEstimate(flops=2*2*heads*G*G*HEAD,bytes_accessed=G*cols*20,transcendentals=heads*G*G),
        compiler_params=pltpu.CompilerParams(vmem_limit_bytes=48*2**20),name="attn_fwd")(raw,rr,cos,sin,lab_r,lab_c,gains)

def attn_bwd_kernel(heads,bq,scale,q,k,v,dm,cos,sin,lab_r,lab_c,dq,dk,dv,bias,ak,av):
    G=q.shape[0]
    ak[...]=jnp.zeros_like(ak); av[...]=jnp.zeros_like(av)
    def block(i,K):
        rows=pl.ds(pl.multiple_of(i*bq,bq),bq)
        bias[:,:K]=mask_bias(lab_r,lab_c[rows,:],i*bq,bq,K)
        def head(hd,_):
            ln=pl.ds(pl.multiple_of(hd*HEAD,HEAD),HEAD)
            qb=q[rows,ln]; kb=k[:K,ln]; db=dm[rows,ln]
            s=nt(qb,kb)*scale+bias[:,:K]
            p=jnp.exp(s-jnp.max(s,axis=1,keepdims=True))
            p=p*(1.0/jnp.sum(p,axis=1,keepdims=True))
            dp=nt(db,v[:K,ln])
            ds=(p*(dp-jnp.sum(p*dp,axis=1,keepdims=True))).astype(BF)
            g=nn(ds,kb)*scale
            dq[rows,ln]=g*cos[rows,:]-pltpu.roll(g,HEAD//2,1)*sin[rows,:]
            ak[:K,ln]+=tn(ds,qb)
            av[:K,ln]+=tn(p.astype(BF),db)
            return 0
        lax.fori_loop(0,heads,head,0)
    per=G//bq//3
    for g in range(3):
        loop(per,lambda i,g=g: block(i+g*per,(g+1)*per*bq))
    rb=min(128,G)
    def fin(i,_):
        sl=pl.ds(pl.multiple_of(i*rb,rb),rb)
        for hd in range(heads):
            a=hd*HEAD
            g=ak[sl,a:a+HEAD]*scale
            dk[sl,a:a+HEAD]=g*cos[sl,:]-pltpu.roll(g,HEAD//2,1)*sin[sl,:]
        dv[sl,:]=av[sl,:].astype(BF)
        return 0
    lax.fori_loop(0,G//rb,fin,0)

def attn_bwd(q,k,v,dm,cos,sin,lab_r,lab_c,heads,bq=128):
    G,cols=q.shape
    V=pl.BlockSpec(memory_space=pltpu.VMEM)
    f=jax.ShapeDtypeStruct((G,cols),F32)
    return pl.pallas_call(functools.partial(attn_bwd_kernel,heads,bq,HEAD**-0.5),out_shape=[f,f,jax.ShapeDtypeStruct((G,cols),BF)],in_specs=[V]*8,out_specs=[V]*3,
        scratch_shapes=[pltpu.VMEM((bq,G),F32),pltpu.VMEM((G,cols),F32),pltpu.VMEM((G,cols),F32)],
        cost_estimate=pl.CostEstimate(flops=5*2*heads*G*G*HEAD,bytes_accessed=G*cols*20,transcendentals=heads*G*G),
        compiler_params=pltpu.CompilerParams(vmem_limit_bytes=48*2**20),name="attn_bwd")(q,k,v,dm,cos,sin,lab_r,lab_c)

def ctx_barrier(H,c,h,l):
    bar=pltpu.get_barrier_semaphore()
    pl.semaphore_signal(bar,inc=1,device_id={"ctx":h*2+1-l},device_id_type=MESH)
    for j in range(1,H):
        pl.semaphore_signal(bar,inc=1,device_id={"ctx":lax.rem(h+j,H)*2+l},device_id_type=MESH)
    pl.semaphore_wait(bar,H)

def ag_ctx_kernel(H,Q,x,o,xs,xr,bs,br,lsem):
    c=lax.axis_index("ctx"); h=c//2; l=c%2
    T=x.shape[0]; R=T//Q
    loc=pltpu.make_async_copy(x,o.at[c],lsem); loc.start()
    ctx_barrier(H,c,h,l)
    sib=h*2+1-l
    def sl(q): return pl.ds(q*R,R)
    def rc(a,b,s,r,to): return pltpu.make_async_remote_copy(a,b,s,r,device_id={"ctx":to},device_id_type=MESH)
    def xc(j,q): return rc(x.at[sl(q)],o.at[c,sl(q)],xs.at[j-1,q],xr.at[j-1,q],lax.rem(h+j,H)*2+l)
    def xw(j,q):
        p=lax.rem(h+H-j,H)*2+l; return rc(x.at[sl(q)],o.at[p,sl(q)],xs.at[j-1,q],xr.at[j-1,q],p)
    def bc(j,q):
        p=c if j==0 else lax.rem(h+H-j,H)*2+l
        src=x if j==0 else o.at[p]
        return rc(src.at[sl(q)],o.at[p,sl(q)],bs.at[j,q],br.at[j,q],sib)
    def bw(j,q):
        p=sib if j==0 else lax.rem(h+H-j,H)*2+1-l
        return rc(x.at[sl(q)],o.at[p,sl(q)],bs.at[j,q],br.at[j,q],sib)
    for q in range(Q):
        for j in range(1,H): xc(j,q).start()
    for q in range(Q): bc(0,q).start()
    for q in range(Q):
        for j in range(1,H):
            xw(j,q).wait_recv(); bc(j,q).start()
    for j in range(H):
        for q in range(Q):
            bw(j,q).wait_recv(); bc(j,q).wait_send()
            if j>0: xc(j,q).wait_send()
    loc.wait()

def ag_ctx(x,C,cid,Q=4):
    T,D=x.shape; H=C//2; dma=pltpu.SemaphoreType.DMA
    A=pl.BlockSpec(memory_space=pl.ANY)
    return pl.pallas_call(functools.partial(ag_ctx_kernel,H,Q),out_shape=jax.ShapeDtypeStruct((C,T,D),x.dtype),in_specs=[A],out_specs=A,
        scratch_shapes=[dma((H-1,Q)),dma((H-1,Q)),dma((H,Q)),dma((H,Q)),dma(())],
        compiler_params=pltpu.CompilerParams(collective_id=cid,has_side_effects=True),name="ag_ctx")(x)

def rs_ctx_kernel(H,Q,x,o,own,r1,r2,ld,s1,q1,s2,q2,osem):
    c=lax.axis_index("ctx"); h=c//2; l=c%2
    T=own.shape[1]; R=T//Q
    def sl(q): return pl.ds(q*R,R)
    hs=[lax.rem(h+j,H) for j in range(1,H)]+[h]
    def load(i): return pltpu.make_async_copy(x.at[hs[i]*2+l],own.at[hs[i]],ld.at[i])
    for i in range(H): load(i).start()
    ctx_barrier(H,c,h,l)
    def c1(i,q): return pltpu.make_async_remote_copy(x.at[hs[i]*2+1-l,sl(q)],r1.at[hs[i],sl(q)],s1.at[hs[i],q],q1.at[hs[i],q],device_id={"ctx":h*2+1-l},device_id_type=MESH)
    def c2(j,q): return pltpu.make_async_remote_copy(own.at[hs[j-1],sl(q)],r2.at[j-1,sl(q)],s2.at[j-1,q],q2.at[j-1,q],device_id={"ctx":hs[j-1]*2+l},device_id_type=MESH)
    for i in range(H):
        for q in range(Q): c1(i,q).start()
    for i in range(H):
        load(i).wait()
        for q in range(Q):
            c1(i,q).wait_recv()
            add_into(own.at[hs[i],sl(q)],r1.at[hs[i],sl(q)])
            if i<H-1: c2(i+1,q).start()
    for q in range(Q):
        for j in range(1,H):
            c2(j,q).wait_recv()
            add_into(own.at[h,sl(q)],r2.at[j-1,sl(q)])
    out=pltpu.make_async_copy(own.at[h],o,osem); out.start()
    for q in range(Q):
        for i in range(H): c1(i,q).wait_send()
        for j in range(1,H): c2(j,q).wait_send()
    out.wait()

def rs_ctx(x,cid,Q=4):
    C,T,D=x.shape; H=C//2; dma=pltpu.SemaphoreType.DMA
    A=pl.BlockSpec(memory_space=pl.ANY)
    return pl.pallas_call(functools.partial(rs_ctx_kernel,H,Q),out_shape=jax.ShapeDtypeStruct((T,D),x.dtype),in_specs=[A],out_specs=A,
        scratch_shapes=[pltpu.VMEM((H,T,D),BF),pltpu.VMEM((H,T,D),BF),pltpu.VMEM((H-1,T,D),BF),dma((H,)),dma((H,Q)),dma((H,Q)),dma((H-1,Q)),dma((H-1,Q)),dma(())],
        compiler_params=pltpu.CompilerParams(collective_id=cid,has_side_effects=True,vmem_limit_bytes=40*2**20),name="rs_ctx")(x)


def dot_nn(a, b):
    return lax.dot_general(a, b, (((1,), (0,)), ((), ())), preferred_element_type=F32)


def dot_tn(a, b):
    return lax.dot_general(a, b, (((0,), (0,)), ((), ())), preferred_element_type=F32)


def dot_nt(a, b):
    return lax.dot_general(a, b, (((1,), (1,)), ((), ())), preferred_element_type=F32)


def low_dp(grad, n_dp):
    low = grad.astype(BF)
    if n_dp != 2:
        return (lax.psum(low, "dp"),)
    return low, lax.ppermute(low, "dp", [(0, 1), (1, 0)])


def per_device(
    hidden_in,
    segments,
    routes,
    attn_gain,
    query_weight,
    key_weight,
    value_weight,
    query_gain,
    key_gain,
    output_weight,
    ffn_gain,
    router_weight,
    gate_weight,
    up_weight,
    down_weight,
    cotangent,
):
    n_dp, n_ctx, n_exp = (lax.axis_size(a) for a in ALL)
    tok, width = hidden_in.shape[2:]
    topk = routes.shape[3]
    experts = n_ctx * n_exp
    cap = (5 * tok * topk + 4 * experts - 1) // (4 * experts)
    cap = -(-cap // 16) * 16
    group = segments.shape[2]
    shard = query_weight.shape[0]
    cols = width // n_ctx
    piece = cols // n_dp
    heads = cols // HEAD
    ctx_me = lax.axis_index("ctx")
    exp_me = lax.axis_index("exp")
    expert_me = ctx_me * n_exp + exp_me

    def own_cols(vec):
        return lax.dynamic_index_in_dim(
            vec.reshape(n_dp, n_ctx, piece), ctx_me, 1, keepdims=False
        ).reshape(cols)

    packed = jnp.stack([query_weight, key_weight, value_weight], axis=1)
    packed = packed.reshape(shard, 3, n_dp, n_ctx, piece).transpose(3, 0, 1, 2, 4)
    packed = lax.all_to_all(packed, "ctx", split_axis=0, concat_axis=0, tiled=True)
    packed = packed.reshape(n_ctx * shard, 3 * cols)
    qkv_w = lax.all_gather(packed, ROWS, axis=0, tiled=True)
    qkv_w = (
        qkv_w.reshape(n_dp, n_exp, n_ctx, shard, 3 * cols)
        .transpose(0, 2, 1, 3, 4)
        .reshape(width, 3 * cols)
    )
    out_w = lax.all_gather(output_weight, ROWS, axis=0, tiled=True)

    own_routes = routes[0, 0]
    expert_ids = jnp.arange(experts, dtype=jnp.int32)
    hits = jnp.sum((own_routes[:, :, None] == expert_ids).astype(jnp.int32), axis=1)
    tokens = jnp.arange(tok, dtype=jnp.int32)
    lower = (tokens[:, None] > tokens[None, :]).astype(BF)
    earlier = dot_nn(lower, hits.astype(BF)).astype(jnp.int32)
    slot_local = jnp.where(hits > 0, earlier, -1).T
    slot = lax.all_to_all(slot_local, MOE, split_axis=0, concat_axis=0, tiled=True)
    slot = slot.reshape(experts, tok)
    cot = cotangent[0, 0]
    cot_all = lax.all_gather(cot, MOE, axis=0, tiled=False)

    hidden = hidden_in[0, 0].astype(F32)
    labels = segments[0, 0]
    index = jnp.arange(group, dtype=jnp.int32)
    before = jnp.sum((labels[None, :] < labels[:, None]).astype(jnp.int32), axis=1)
    positions = index - before + jnp.where(labels > 0, PROMPT, 0).astype(jnp.int32)
    half = HEAD // 2
    frequency = THETA ** (-(jnp.arange(half, dtype=F32) * 2.0 / HEAD))
    angles = positions.astype(F32)[:, None] * frequency[None, :]
    cos, sin = jnp.cos(angles), jnp.sin(angles)
    cos = jnp.concatenate([cos, cos], axis=1)
    sin = jnp.concatenate([-sin, sin], axis=1)
    label_row, label_col = labels[None, :], labels[:, None]
    attn_gain_f = attn_gain.astype(F32)
    ffn_gain_f = ffn_gain.astype(F32)
    q_gain = own_cols(query_gain.astype(F32))
    k_gain = own_cols(key_gain.astype(F32))

    attn_r = lax.rsqrt(jnp.mean(hidden * hidden, axis=-1, keepdims=True) + EPS)
    normed = (hidden * attn_r * attn_gain_f).astype(BF)
    normed_g = ag_ctx(normed, n_ctx, 5).reshape(group, width)
    raw = dot_nn(normed_g, qkv_w)
    q_raw, k_raw = raw[:, :cols], raw[:, cols : 2 * cols]
    squares = lax.psum(
        jnp.stack([jnp.sum(q_raw * q_raw, axis=1), jnp.sum(k_raw * k_raw, axis=1)]), "ctx"
    )
    inv = lax.rsqrt(squares / width + EPS)
    q_r, k_r = inv[0][:, None], inv[1][:, None]
    q_rot, k_rot, v_low, mix = attn_fwd(
        raw, inv.T, cos, sin, label_row, label_col, jnp.stack([q_gain, k_gain]), heads
    )
    branch = rs_ctx(dot_nn(mix, out_w).astype(BF).reshape(n_ctx, tok, width), 6)
    residual = hidden + branch.astype(F32)

    ffn_r = lax.rsqrt(jnp.mean(residual * residual, axis=-1, keepdims=True) + EPS)
    ffn_normed = (residual * ffn_r * ffn_gain_f).astype(BF)
    logits = dot_nn(ffn_normed, router_weight)
    router_prob = jax.nn.softmax(logits, axis=-1)
    gates = jnp.where(hits > 0, router_prob, 0.0).astype(BF)
    padded = jnp.zeros((experts, width), BF).at[:, :tok].set(gates.T)
    rows_ext = jnp.concatenate([ffn_normed, padded], axis=0)
    gate_mat, up_mat, down_mat = gate_weight[0], up_weight[0], down_weight[0]
    received, expert_hidden, d_out, d_gate_pre, d_up_pre, moe_part, d_gate_at = fwd_call(
        slot, rows_ext, cot_all, gate_mat, up_mat, down_mat, cap, n_ctx, n_exp, tok
    )
    total = experts * cap

    d_gate = lax.all_to_all(
        d_gate_at.reshape(experts, tok), MOE, split_axis=0, concat_axis=0, tiled=True
    ).T
    d_tokens = back_call(slot, d_gate_pre, d_up_pre, gate_mat, up_mat, n_ctx, n_exp, tok, (1, 8))
    moe_part, d_tokens = lax.optimization_barrier((moe_part, d_tokens))
    moe_out = lax.psum_scatter(
        moe_part.reshape(experts * tok, width), MOE, scatter_dimension=0, tiled=True
    )
    received = received.reshape(total, width)
    down_grad = dot_tn(expert_hidden.reshape(total, -1), d_out.reshape(total, width))
    gate_grad = dot_tn(received, d_gate_pre.reshape(total, -1))
    up_grad = dot_tn(received, d_up_pre.reshape(total, -1))
    wide = [low_dp(g, n_dp) for g in (gate_grad, up_grad, down_grad)]

    d_router = d_gate
    d_logits = (
        router_prob * (d_router - jnp.sum(router_prob * d_router, axis=-1, keepdims=True))
    ).astype(BF)
    router_grad = dot_tn(d_logits, ffn_normed)
    d_ffn = d_tokens.astype(F32) + dot_nt(d_logits, router_weight)
    ffn_gain_grad = jnp.sum(d_ffn * residual * ffn_r, axis=0)
    weighted = d_ffn * ffn_gain_f
    d_residual = cot.astype(F32) + (
        weighted * ffn_r
        - residual * ffn_r**3 * jnp.mean(residual * weighted, axis=-1, keepdims=True)
    )
    d_branch = d_residual.astype(BF)

    d_branch_g = ag_ctx(d_branch, n_ctx, 7).reshape(group, width)
    out_grad = dot_tn(mix, d_branch_g)
    d_mix = dot_nt(d_branch_g, out_w).astype(BF)
    d_qn, d_kn, d_v = attn_bwd(q_rot, k_rot, v_low, d_mix, cos, sin, label_row, label_col, heads)
    q_gain_part = jnp.sum(d_qn * q_raw * q_r, axis=0)
    k_gain_part = jnp.sum(d_kn * k_raw * k_r, axis=0)
    d_qw, d_kw = d_qn * q_gain, d_kn * k_gain
    dots = (
        lax.psum(jnp.stack([jnp.sum(q_raw * d_qw, axis=1), jnp.sum(k_raw * d_kw, axis=1)]), "ctx")
        / width
    )
    d_q_raw = d_qw * q_r - q_raw * q_r**3 * dots[0][:, None]
    d_k_raw = d_kw * k_r - k_raw * k_r**3 * dots[1][:, None]
    d_raw = jnp.concatenate(
        [d_q_raw.astype(BF), d_k_raw.astype(BF), d_v], axis=1
    )
    d_raw, moe_out = lax.optimization_barrier((d_raw, moe_out))
    output = (residual + moe_out.astype(F32)).astype(BF)
    d_part_n = dot_nt(d_raw, qkv_w).astype(BF).reshape(n_ctx, tok, width)
    qkv_grad = dot_tn(normed_g, d_raw).astype(BF).reshape(n_dp, n_ctx, n_exp, shard, 3 * cols)
    out_part = out_grad.astype(BF).reshape(n_dp, n_exp, shard, width)
    qkv_sum, out_sum, d_normed = tail(qkv_grad, out_part, d_part_n)
    d_normed = d_normed.astype(F32)
    wide, d_normed = lax.optimization_barrier((wide, d_normed))
    gate_sum, up_sum, down_sum = (sum(x.astype(F32) for x in pair) for pair in wide)
    attn_gain_grad = jnp.sum(d_normed * hidden * attn_r, axis=0)
    weighted = d_normed * attn_gain_f
    hidden_grad = (
        d_residual
        + weighted * attn_r
        - hidden * attn_r**3 * jnp.mean(hidden * weighted, axis=-1, keepdims=True)
    ).astype(BF)

    qkv_sum = qkv_sum.reshape(n_ctx, shard, 3, n_dp, piece)
    qkv_sum = qkv_sum.transpose(2, 1, 3, 0, 4).reshape(3, shard, width).astype(F32)
    out_sum = out_sum.astype(F32)

    spread = jnp.zeros((2, n_dp, n_ctx, piece), F32)
    spread = lax.dynamic_update_slice(
        spread,
        jnp.stack([q_gain_part, k_gain_part]).reshape(2, n_dp, 1, piece),
        (0, 0, ctx_me, 0),
    ).reshape(2, width)
    small = jnp.concatenate(
        [router_grad, spread, attn_gain_grad[None], ffn_gain_grad[None]], axis=0
    )
    pad = -small.shape[0] % 8
    small = sums(jnp.pad(small, ((0, pad), (0, 0))), (n_dp, n_ctx, n_exp))
    late, early = small[experts:], small
    return (
        output[None, None],
        hidden_grad[None, None],
        late[2],
        qkv_sum[0],
        qkv_sum[1],
        qkv_sum[2],
        late[0],
        late[1],
        out_sum,
        late[3],
        early[:experts].T,
        gate_sum[None],
        up_sum[None],
        down_sum[None],
    )


def solution(mesh):
    tokens = P("dp", "exp", "ctx", None)
    rows = P(ALL, None)
    expert = P(MOE, None, None)
    return jax.shard_map(
        per_device,
        mesh=mesh,
        in_specs=(
            tokens,
            P("dp", "exp", None),
            tokens,
            P(),
            rows,
            rows,
            rows,
            P(),
            P(),
            rows,
            P(),
            P(),
            expert,
            expert,
            expert,
            tokens,
        ),
        out_specs=(
            tokens,
            tokens,
            P(),
            rows,
            rows,
            rows,
            P(),
            P(),
            rows,
            P(),
            P(),
            expert,
            expert,
            expert,
        ),
        check_vma=False,
    )
```

```python
import functools

import jax
import jax.numpy as jnp
from jax import lax
from jax.experimental import pallas as pl
from jax.experimental.pallas import tpu as pltpu
from jax.sharding import PartitionSpec as P

HEAD = 128
PROMPT = 512
EPS = 1e-05
THETA = 10000.0
MASKED = -1e30
BF = jnp.bfloat16
F32 = jnp.float32
ALL = ("dp", "ctx", "exp")
MOE = ("ctx", "exp")
ROWS = ("dp", "exp")
MESH = pl.DeviceIdType.MESH


def by_distance(me, n):
    far=[jnp.abs(me-j)*n+j for j in range(n)]
    rank=[sum(((far[i]>far[j]).astype(jnp.int32) for i in range(n) if i!=j), jnp.int32(0)) for j in range(n)]
    def at(k):
        v=jnp.int32(0)
        for j in range(n): v=v+jnp.where(rank[j]==k,j,0)
        return v
    return at


def loop(n, body):
    def step(i,_):
        body(i)
        return 0
    lax.fori_loop(0,n,step,0)


def add_into(dst, src, rows=16):
    n=dst.shape[-2]//rows
    lead=dst.shape[:-2]
    assert not lead
    def body(i,_):
        sl=pl.ds(pl.multiple_of(i*rows,rows),rows)
        dst[sl,:]=(dst[sl,:].astype(F32)+src[sl,:].astype(F32)).astype(dst.dtype)
        return 0
    lax.fori_loop(0,n,body,0)


def add3(dst,src):
    if len(dst.shape)==2: add_into(dst,src); return
    def body(i,_):
        add_into(dst.at[i],src.at[i]); return 0
    lax.fori_loop(0,dst.shape[0],body,0)

def tail_kernel(N,C,E,gq,go,dn,hid,dres,gain,sm,oq,oo,od,osm,own_q,own_o,own_d,yq,yo,uq,uo,vq,vo,d1,d2,ld,ldd,ys,yr,zs,zu,zd,s1,r1,s2,r2,a_s,a_r,osem,hv,rv,gv,b0,b1,b2,t_s,t_r):
    p=lax.axis_index("dp"); c=lax.axis_index("ctx"); e=lax.axis_index("exp")
    H=C//2; h=c//2; l=c%2
    def dpeer(j): return lax.rem(p+j,N)
    def cpeer(j): return lax.rem(c+j,C)
    def hpeer(j): return lax.rem(h+j,H)
    bar=pltpu.get_barrier_semaphore()
    def sig(**kw): pl.semaphore_signal(bar,inc=1,device_id=kw,device_id_type=MESH)
    for j in range(1,N): sig(dp=dpeer(j))
    for j in range(1,C): sig(ctx=cpeer(j))
    for j in range(1,E): sig(exp=lax.rem(e+j,E))
    order=by_distance(e,E)
    def rc(src,dst,ss,rs,**kw): return pltpu.make_async_remote_copy(src,dst,ss,rs,device_id=kw,device_id_type=MESH)
    def loads(o): return [pltpu.make_async_copy(gq.at[p,:,o],own_q.at[o],ld.at[0,o]),pltpu.make_async_copy(go.at[p,o],own_o.at[o],ld.at[1,o])]
    def cy(j,o):
        q=dpeer(j)
        return [rc(gq.at[q,:,o],yq.at[j-1,o],ys.at[0,j-1,o],yr.at[0,j-1,o],dp=q), rc(go.at[q,o],yo.at[j-1,o],ys.at[1,j-1,o],yr.at[1,j-1,o],dp=q)]
    def cu(o): return [rc(own_q.at[o],uq.at[o],zs.at[0,o],zu.at[0,o],exp=e+1), rc(own_o.at[o],uo.at[o],zs.at[1,o],zu.at[1,o],exp=e+1)]
    def cd(o): return [rc(own_q.at[o],vq.at[o],zs.at[0,o],zd.at[0,o],exp=e-1), rc(own_o.at[o],vo.at[o],zs.at[1,o],zd.at[1,o],exp=e-1)]
    def loadd(hh): return pltpu.make_async_copy(dn.at[hh*2+l],own_d.at[hh],ldd.at[hh])
    def c1(hh): return rc(dn.at[hh*2+1-l],d1.at[hh],s1.at[hh],r1.at[hh],ctx=h*2+1-l)
    def c2(j):
        hh=hpeer(j); return rc(own_d.at[hh],d2.at[j-1],s2.at[j-1],r2.at[j-1],ctx=hh*2+l)
    hs=[hpeer(j) for j in range(1,H)]+[h]
    def start_loads(k):
        for x in loads(k): x.start()
    side=[pltpu.make_async_copy(hid,hv,osem.at[3]),pltpu.make_async_copy(dres,rv,osem.at[4]),pltpu.make_async_copy(gain,gv,osem.at[5]),pltpu.make_async_copy(sm,b0.at[p],osem.at[6])]
    for x in side: x.start()
    loop(E,start_loads)
    for hh in hs: loadd(hh).start()
    pl.semaphore_wait(bar,(N-1)+(C-1)+(E-1))
    for j in range(1,N):
        for x in cy(j,order(0)): x.start()
    for hh in hs: c1(hh).start()
    def start_dp(k):
        for j in range(1,N):
            for x in cy(j,order(k+1)): x.start()
    loop(E-1,start_dp)
    for i,hh in enumerate(hs):
        loadd(hh).wait(); c1(hh).wait_recv(); add_into(own_d.at[hh],d1.at[hh])
        if i<H-1: c2(i+1).start()
    def line(k):
        o=order(k)
        for x in loads(o): x.wait()
        for j in range(1,N):
            for x in cy(j,o): x.wait_recv()
            add3(own_q.at[o],yq.at[j-1,o]); add3(own_o.at[o],yo.at[j-1,o])
        if True:
            @pl.when(o>e)
            def _():
                @pl.when(e>0)
                def _():
                    for x in cu(o): x.wait_recv()
                    add3(own_q.at[o],uq.at[o]); add3(own_o.at[o],uo.at[o])
                for x in cu(o): x.start()
            @pl.when(o<e)
            def _():
                @pl.when(e<E-1)
                def _():
                    for x in cd(o): x.wait_recv()
                    add3(own_q.at[o],vq.at[o]); add3(own_o.at[o],vo.at[o])
                for x in cd(o): x.start()
    small=((b0,"dp",N,p),(b1,"ctx",C,c),(b2,"exp",E,e))
    def hop(t,j):
        b,a,n,i=small[t]
        return rc(b.at[i],b.at[i],t_s.at[t,j-1],t_r.at[t,j-1],**{a:lax.rem(i+j,n)})
    def gathered(t):
        b,a,n,i=small[t]
        for j in range(1,n):
            q=lax.rem(i+n-j,n)
            rc(b.at[q],b.at[q],t_s.at[t,j-1],t_r.at[t,j-1],**{a:q}).wait_recv()
        x=b[0]
        for j in range(1,n): x=x+b[j]
        return x
    def send(t):
        for j in range(1,small[t][2]): hop(t,j).start()
    T,D=hv.shape; RB=16
    lastrow=b0.shape[1]-1
    def epilogue(i):
        sl=pl.ds(pl.multiple_of(i*RB,RB),RB)
        d=own_d[h,sl,:].astype(F32); x=hv[sl,:].astype(F32)
        r=lax.rsqrt(jnp.mean(x*x,axis=1,keepdims=True)+EPS)
        b0[p,lastrow:,:]+=jnp.sum(d*x*r,axis=0,keepdims=True)
        w=d*gv[...]
        own_d[h,sl,:]=(rv[sl,:]+(w*r-x*(r*r*r)*jnp.mean(x*w,axis=1,keepdims=True))).astype(BF)
    def lines(k):
        line(k)
        @pl.when(k==0)
        def _():
            for j in range(1,H):
                c2(j).wait_recv(); add_into(own_d.at[h],d2.at[j-1])
            for x in side: x.wait()
            loop(T//RB,epilogue)
            send(0)
            pltpu.make_async_copy(own_d.at[h],od,osem.at[0]).start()
        @pl.when(k==1)
        def _():
            b1[c]=gathered(0); send(1)
        @pl.when(k==2)
        def _():
            b2[e]=gathered(1); send(2)
    loop(E,lines)
    @pl.when(e>0)
    def _():
        for x in cu(e): x.wait_recv()
        add3(own_q.at[e],uq.at[e]); add3(own_o.at[e],uo.at[e])
    @pl.when(e<E-1)
    def _():
        for x in cd(e): x.wait_recv()
        add3(own_q.at[e],vq.at[e]); add3(own_o.at[e],vo.at[e])
    def ca(j):
        q=cpeer(j); return rc(own_q.at[e,q],oq.at[c],a_s.at[j-1],a_r.at[j-1],ctx=q)
    for j in range(1,C): ca(j).start()
    l1=pltpu.make_async_copy(own_q.at[e,c],oq.at[c],osem.at[1]); l1.start()
    l2=pltpu.make_async_copy(own_o.at[e],oo,osem.at[2]); l2.start()
    def drain(k):
        for j in range(1,N):
            for x in cy(j,k): x.wait_send()
        @pl.when(k!=e)
        def _():
            for x in cu(k): x.wait_send()
    loop(E,drain)
    for hh in hs: c1(hh).wait_send()
    for j in range(1,H): c2(j).wait_send()
    for j in range(1,C):
        ca(j).wait_send();
        src=lax.rem(c+C-j,C)
        rc(own_q.at[e,c],oq.at[src],a_s.at[j-1],a_r.at[j-1],ctx=src).wait_recv()
    for t in range(3):
        for j in range(1,small[t][2]): hop(t,j).wait_send()
    b0[0]=gathered(2)
    so=pltpu.make_async_copy(b0.at[0],osm,osem.at[7]); so.start()
    pltpu.make_async_copy(own_d.at[h],od,osem.at[0]).wait(); l1.wait(); l2.wait(); so.wait()

def tail(gq,go,dn,hid,dres,gain,sm,cid=2):
    N,C,E,S,W3=gq.shape; D=go.shape[-1]; T=dn.shape[1]; H=C//2; R=sm.shape[0]
    dma=pltpu.SemaphoreType.DMA; V=lambda *s: pltpu.VMEM(s,BF); FV=lambda *s: pltpu.VMEM(s,F32)
    M=max(N,C,E)-1
    return pl.pallas_call(functools.partial(tail_kernel,N,C,E),
        out_shape=[jax.ShapeDtypeStruct((C,S,W3),BF),jax.ShapeDtypeStruct((S,D),BF),jax.ShapeDtypeStruct((T,D),BF),jax.ShapeDtypeStruct((R,D),F32)],
        in_specs=[pl.BlockSpec(memory_space=pl.ANY)]*7,
        out_specs=[pl.BlockSpec(memory_space=pl.ANY)]*4,
        scratch_shapes=[V(E,C,S,W3),V(E,S,D),V(H,T,D),V(N-1,E,C,S,W3),V(N-1,E,S,D),V(E,C,S,W3),V(E,S,D),V(E,C,S,W3),V(E,S,D),V(H,T,D),V(H-1,T,D),
            dma((2,E)),dma((H,)),dma((2,N-1,E)),dma((2,N-1,E)),dma((2,E)),dma((2,E)),dma((2,E)),dma((H,)),dma((H,)),dma((H-1,)),dma((H-1,)),dma((C-1,)),dma((C-1,)),dma((8,)),
            V(T,D),FV(T,D),FV(1,D),FV(N,R,D),FV(C,R,D),FV(E,R,D),dma((3,M)),dma((3,M))],
        compiler_params=pltpu.CompilerParams(collective_id=cid,has_side_effects=True,vmem_limit_bytes=61*2**20),
        name="tail")(gq,go,dn,hid,dres,gain,sm)

def nn(a,b): return lax.dot_general(a,b,(((1,),(0,)),((),())),preferred_element_type=F32)
def tn(a,b): return lax.dot_general(a,b,(((0,),(0,)),((),())),preferred_element_type=F32)
def nt(a,b): return lax.dot_general(a,b,(((1,),(1,)),((),())),preferred_element_type=F32)

def pick_of(slot_row, cap):
    T=slot_row.shape[1]
    return jnp.broadcast_to(slot_row,(cap,T))==lax.broadcasted_iota(jnp.int32,(cap,T),0)

def back_kernel(H,E,cap,X,slot,dgp,dup,gw,uw,*rest):
    ex_in,o_ref,ex_out=rest[:X],rest[X],rest[X+1:2*X+1]
    own,r1,r2,rz,snd,gb,ub,slv,wg,wu,ld_sem,w_sem,s1,q1,s2,q2,s3,qz,o_sem=rest[2*X+1:2*X+20]
    c=lax.axis_index("ctx"); e=lax.axis_index("exp")
    h=c//2; l=c%2
    T,W=own.shape[2:]; FF=wg.shape[1]
    sib={"ctx":h*2+1-l}
    def xpeer(j): return lax.rem(h+j,H)
    bar=pltpu.get_barrier_semaphore()
    pl.semaphore_signal(bar,inc=1,device_id=sib,device_id_type=MESH)
    for j in range(1,H):
        pl.semaphore_signal(bar,inc=1,device_id={"ctx":xpeer(j)*2+l},device_id_type=MESH)
    @pl.when(e>0)
    def _(): pl.semaphore_signal(bar,inc=1,device_id={"exp":e-1},device_id_type=MESH)
    @pl.when(e<E-1)
    def _(): pl.semaphore_signal(bar,inc=1,device_id={"exp":e+1},device_id_type=MESH)
    def ex(i):
        es,er=rest[2*X+20:]
        return pltpu.make_async_remote_copy(ex_in[i],ex_out[i],es.at[i],er.at[i],device_id={"dp":1-lax.axis_index("dp")},device_id_type=MESH)
    if X: pl.semaphore_signal(bar,inc=1,device_id={"dp":1-lax.axis_index("dp")},device_id_type=MESH)
    order=by_distance(e,E)
    wl=[pltpu.make_async_copy(gw,wg,w_sem.at[0]),pltpu.make_async_copy(uw,wu,w_sem.at[1])]
    for x in wl: x.start()
    NS=snd.shape[0]; M=H*E
    def place(m):
        return lax.rem(h+1+m//E,H),order(lax.rem(m,E))
    def loads(n):
        hh,o=place(n//2)
        s=(hh*2+jnp.where(lax.rem(n,2)==0,1-l,l))*E+o; b=lax.rem(n,2)
        return [pltpu.make_async_copy(dgp.at[s],gb.at[b],ld_sem.at[0,b]),pltpu.make_async_copy(dup.at[s],ub.at[b],ld_sem.at[1,b])],s
    for x in loads(0)[0]: x.start()
    def c1(m):
        hh,o=place(m)
        return pltpu.make_async_remote_copy(snd.at[lax.rem(m,NS)],r1.at[hh,o],s1.at[m],q1.at[hh,o],device_id=sib,device_id_type=MESH)
    def c2(j,o):
        hh=xpeer(j)
        return pltpu.make_async_remote_copy(own.at[hh,o],r2.at[j-1,o],s2.at[j-1,o],q2.at[j-1,o],device_id={"ctx":hh*2+l},device_id_type=MESH)
    def cz(o,to,slot_): return pltpu.make_async_remote_copy(own.at[h,o],rz.at[slot_],s3.at[o],qz.at[slot_],device_id={"exp":to},device_id_type=MESH)
    step=min(512,W)
    def compute(n,dst):
        x,s=loads(n); b=lax.rem(n,2)
        for y in x: y.wait()
        @pl.when(n+1<2*M)
        def _():
            for y in loads(n+1)[0]: y.start()
        low=pick_of(slv[pl.ds(s,1),:],cap).astype(F32).astype(BF)
        def body(i):
            sl=pl.ds(pl.multiple_of(i*step,step),step)
            d=(nt(gb[b],wg[sl,:])+nt(ub[b],wu[sl,:])).astype(BF)
            dst[:,sl]=tn(low,d).astype(BF)
        loop(W//step,body)
    pltpu.sync_copy(slot,slv)
    for x in wl: x.wait()
    pl.semaphore_wait(bar,H+min(X,1)+(e>0).astype(jnp.int32)+(e<E-1).astype(jnp.int32))
    for i in range(X): ex(i).start()
    def zstep(k):
        o=order(k)
        for j in range(1,H):
            c2(j,o).wait_recv()
            add_into(own.at[h,o],r2.at[j-1,o])
        @pl.when(o>e)
        def _():
            @pl.when(e>0)
            def _():
                cz(o,e-1,o).wait_recv(); add_into(own.at[h,o],rz.at[o])
            cz(o,e+1,o).start()
        @pl.when(o<e)
        def _():
            @pl.when(e<E-1)
            def _():
                cz(o,e+1,o).wait_recv(); add_into(own.at[h,o],rz.at[o])
            cz(o,e-1,jnp.where(o==e-1,E,o)).start()
    def pair(m):
        hh,o=place(m)
        @pl.when(m>=NS)
        def _(): c1(m-NS).wait_send()
        compute(2*m,snd.at[lax.rem(m,NS)])
        c1(m).start()
        compute(2*m+1,own.at[hh,o])
        c1(m).wait_recv()
        add_into(own.at[hh,o],r1.at[hh,o])
        for j in range(1,H):
            @pl.when(m//E==j-1)
            def _(): c2(j,o).start()
        @pl.when(m//E==H-1)
        def _(): zstep(lax.rem(m,E))
    loop(M,pair)
    for m in range(max(0,M-NS),M): c1(m).wait_send()
    @pl.when(e>0)
    def _():
        cz(e,e-1,e).wait_recv(); add_into(own.at[h,e],rz.at[e])
    @pl.when(e<E-1)
    def _():
        cz(e,e+1,E).wait_recv(); add_into(own.at[h,e],rz.at[E])
    out=pltpu.make_async_copy(own.at[h,e],o_ref,o_sem); out.start()
    def drain(k):
        for j in range(1,H): c2(j,order(k)).wait_send()
        @pl.when(k<E-1)
        def _(): cz(order(k),e,order(k)).wait_send()
    loop(E,drain)
    out.wait()
    for i in range(X): ex(i).wait()


def back_call(slot,dgp,dup,gw,uw,swap,C,E,T,cids):
    S,cap,FF=dgp.shape; D=gw.shape[0]; H=C//2
    dma=pltpu.SemaphoreType.DMA; V=lambda *s: pltpu.VMEM(s,BF)
    blocks=2*H*E+(H-1)*E+E+4
    parts=1
    while 2*(blocks*T*D//parts+2*D//parts*FF+4*cap*FF)>60*2**20: parts*=2
    W=D//parts
    A=pl.BlockSpec(memory_space=pl.ANY)
    def part(i):
        a,b=(gw,uw) if parts==1 else (gw[i*W:(i+1)*W],uw[i*W:(i+1)*W])
        ex=tuple(swap) if i==0 else ()
        X=len(ex)
        return pl.pallas_call(functools.partial(back_kernel,H,E,cap,X),
            out_shape=[jax.ShapeDtypeStruct((T,W),BF)]+[jax.ShapeDtypeStruct(g.shape,g.dtype) for g in ex],
            in_specs=[A]*(5+X),
            out_specs=[A]*(1+X),
            scratch_shapes=[V(H,E,T,W),V(H,E,T,W),V(H-1,E,T,W),V(E+1,T,W),V(3,T,W),V(2,cap,FF),V(2,cap,FF),pltpu.VMEM((S,T),jnp.int32),V(W,FF),V(W,FF),
                dma((2,2)),dma((2,)),dma((H*E,)),dma((H,E)),dma((H-1,E)),dma((H-1,E)),dma((E,)),dma((E+1,)),dma(())]+([dma((X,)),dma((X,))] if X else []),
            cost_estimate=pl.CostEstimate(flops=2*S*cap*(2*W*FF+T*W),bytes_accessed=S*4*cap*FF,transcendentals=0),
            compiler_params=pltpu.CompilerParams(collective_id=cids[i],has_side_effects=True,vmem_limit_bytes=61*2**20),
            name="back")(slot,dgp,dup,a,b,*ex)
    out=[part(i) for i in range(parts)]
    tok=out[0][0] if parts==1 else jnp.concatenate([o[0] for o in out],axis=1)
    return tok,out[0][1:]


def fwd_kernel(H,E,T,cap,in_vmem,slot,rows,cot,gw,uw,dw,recv,hid,dout,dgp,dup,moe,dg,*scr):
    if in_vmem: allr=scr[0]; scr=scr[1:]; rb=None
    else: allr=scr[0]; rb=scr[1]; scr=scr[2:]
    (slv,wg,wu,wd,cb,srecv,shid,sdout,sdgp,sdup,smoe,sdg,cr,w_sem,c_sem,l_sem,o_sem,up_s,dn_s,up_r,dn_r,x_s,x_r,b_s,b_r)=scr
    c=lax.axis_index("ctx"); e=lax.axis_index("exp")
    h=c//2; l=c%2; C=2*H; S=C*E
    D=wg.shape[0]; FF=wg.shape[1]; EXT=allr.shape[1]
    expert=c*E+e
    def xpeer(j): return lax.rem(h+j,H)
    def idx(hh,ll,ee): return (hh*2+ll)*E+ee
    bar=pltpu.get_barrier_semaphore()
    pl.semaphore_signal(bar,inc=1,device_id={"ctx":h*2+1-l},device_id_type=MESH)
    for j in range(1,H):
        pl.semaphore_signal(bar,inc=1,device_id={"ctx":xpeer(j)*2+l},device_id_type=MESH)
    @pl.when(e>0)
    def _(): pl.semaphore_signal(bar,inc=1,device_id={"exp":e-1},device_id_type=MESH)
    @pl.when(e<E-1)
    def _(): pl.semaphore_signal(bar,inc=1,device_id={"exp":e+1},device_id_type=MESH)
    order=by_distance(e,E)
    def near(k): return order(E-1-k)
    own=idx(h,l,e)
    wl=[pltpu.make_async_copy(a,b,w_sem.at[i]) for i,(a,b) in enumerate(((gw,wg),(uw,wu),(dw,wd)))]
    first=pltpu.make_async_copy(rows,allr.at[own],w_sem.at[3])
    first.start()
    for x in wl: x.start()
    def job(n):
        m=jnp.maximum(n-2,0)
        r=jnp.where(n<2,0,1+m//(2*H)); t=jnp.where(n<2,n,lax.rem(m,2*H))
        t=jnp.where(r==E,t+2,t)
        j=t//2
        return r,t,j,lax.rem(t,2),jnp.where(j==0,r,r-1)
    def hi(j): return jnp.where(j==0,h,lax.rem(h+H-j,H))
    def sender(n):
        r,t,j,s,k=job(n)
        return idx(hi(j),jnp.where(s==1,1-l,l),near(k))
    def cload(n): return pltpu.make_async_copy(cot.at[sender(n)],cb.at[lax.rem(n,2)],c_sem.at[lax.rem(n,2)])
    cload(0).start()
    def rc(i,ss,rs,**kw): return pltpu.make_async_remote_copy(allr.at[i],allr.at[i],ss,rs,device_id=kw,device_id_type=MESH)
    def up(ee): return rc(idx(h,l,ee),up_s.at[ee],up_r.at[ee],exp=e+1)
    def dn(ee): return rc(idx(h,l,ee),dn_s.at[ee],dn_r.at[ee],exp=e-1)
    def xs(j,ee): return rc(idx(h,l,ee),x_s.at[j-1,ee],x_r.at[j-1,ee],ctx=xpeer(j)*2+l)
    def xr(j,ee):
        return rc(idx(hi(j),l,ee),x_s.at[j-1,ee],x_r.at[j-1,ee],ctx=hi(j)*2+l)
    def bs(j,ee): return rc(idx(hi(j),l,ee),b_s.at[j,ee],b_r.at[j,ee],ctx=h*2+1-l)
    def br(j,ee): return rc(idx(hi(j),1-l,ee),b_s.at[j,ee],b_r.at[j,ee],ctx=h*2+1-l)
    outs=[(srecv,recv),(shid,hid),(sdout,dout),(sdgp,dgp),(sdup,dup),(smoe,moe),(sdg,dg)]
    def odma(n):
        s=sender(n); b=lax.rem(n,2)
        return [pltpu.make_async_copy(a.at[b],o.at[s],o_sem.at[i,b]) for i,(a,o) in enumerate(outs)]
    def compute(n):
        s=sender(n); b=lax.rem(n,2)
        if in_vmem: rw=allr.at[s]
        else:
            cp=pltpu.make_async_copy(allr.at[s],rb,l_sem); cp.start(); cp.wait(); rw=rb
        cload(n).wait()
        @pl.when(n+1<S)
        def _(): cload(n+1).start()
        @pl.when(n>=2)
        def _():
            for x in odma(n-2): x.wait()
        ct=cb.at[b]
        pk=pick_of(slv[pl.ds(s,1),:],cap); pf=pk.astype(F32); low=pf.astype(BF)
        gm=rw[T:EXT,:T].astype(F32)
        g=jnp.sum(jnp.where(lax.broadcasted_iota(jnp.int32,gm.shape,0)==expert,gm,0.0),axis=0,keepdims=True)
        gsel=jnp.where(pk,jnp.broadcast_to(g,(cap,T)),0.0)
        grow=jnp.sum(gsel,axis=1,keepdims=True)
        comb=gsel.astype(BF)
        step=512
        for m in range(0,D,step):
            srecv[b,:,m:m+step]=nn(low,rw[:T,m:m+step]).astype(BF)
            q=nn(low,ct[:,m:m+step])
            sdout[b,:,m:m+step]=(q*grow).astype(BF)
            cr[:,m:m+step]=q.astype(BF)
        half=FF//2
        for m in range(0,FF,half):
            gp=nn(srecv[b],wg[:,m:m+half]); upp=nn(srecv[b],wu[:,m:m+half])
            dh=nt(sdout[b],wd[m:m+half,:])
            sg=jax.nn.sigmoid(gp); si=gp*sg
            shid[b,:,m:m+half]=(si*upp).astype(BF)
            sdgp[b,:,m:m+half]=(dh*upp*sg*(1.0+gp*(1.0-sg))).astype(BF)
            sdup[b,:,m:m+half]=(dh*si).astype(BF)
        acc=jnp.zeros((cap,1),F32)
        for m in range(0,D,step):
            ev=nn(shid[b],wd[:,m:m+step]).astype(BF)
            acc=acc+jnp.sum(cr[:,m:m+step].astype(F32)*ev.astype(F32),axis=1,keepdims=True)
            smoe[b,:,m:m+step]=tn(comb,ev).astype(BF)
        sdg[b]=jnp.sum(pf*acc,axis=0,keepdims=True)
        for x in odma(n): x.start()
    pltpu.sync_copy(slot,slv)
    first.wait()
    pl.semaphore_wait(bar,H+(e>0).astype(jnp.int32)+(e<E-1).astype(jnp.int32))
    @pl.when(e<E-1)
    def _(): up(e).start()
    @pl.when(e>0)
    def _(): dn(e).start()
    for j in range(1,H): xs(j,e).start()
    bs(0,e).start()
    for x in wl: x.wait()
    def step_(n):
        r,t,j,sib_,k=job(n)
        @pl.when(jnp.logical_and(t==0,r>0))
        def _():
            @pl.when(e>=r)
            def _():
                up(e-r).wait_recv()
                @pl.when(e<E-1)
                def _(): up(e-r).start()
                for q in range(1,H): xs(q,e-r).start()
                bs(0,e-r).start()
            @pl.when(e+r<E)
            def _():
                dn(e+r).wait_recv()
                @pl.when(e>0)
                def _(): dn(e+r).start()
                for q in range(1,H): xs(q,e+r).start()
                bs(0,e+r).start()
        @pl.when(jnp.logical_and(sib_==0,j>0))
        def _():
            xr(j,near(k)).wait_recv(); bs(j,near(k)).start()
        @pl.when(sib_==1)
        def _(): br(j,near(k)).wait_recv()
        compute(n)
    loop(S,step_)
    for x in odma(S-2)+odma(S-1): x.wait()
    def drain(ee):
        @pl.when(jnp.logical_and(e<E-1,ee<=e))
        def _(): up(ee).wait_send()
        @pl.when(jnp.logical_and(e>0,ee>=e))
        def _(): dn(ee).wait_send()
        for j in range(1,H): xs(j,ee).wait_send()
        for j in range(H): bs(j,ee).wait_send()
    loop(E,drain)


def fwd_call(slot,rows,cot,gw,uw,dw,cap,C,E,T,cid=4):
    EXT,D=rows.shape; S=C*E; H=C//2; FF=gw.shape[1]
    dma=pltpu.SemaphoreType.DMA; V=lambda *s: pltpu.VMEM(s,BF)
    in_vmem=S*EXT*D*2<=28*2**20
    A=pl.BlockSpec(memory_space=pl.ANY)
    sd=lambda a,b,dt=BF: jax.ShapeDtypeStruct((S,a,b),dt)
    out_shape=[sd(cap,D),sd(cap,FF),sd(cap,D),sd(cap,FF),sd(cap,FF),sd(T,D),sd(1,T,F32)]
    land=[V(S,EXT,D)] if in_vmem else [V(EXT,D)]
    if not in_vmem: out_shape=out_shape+[sd(EXT,D)]
    body=functools.partial(fwd_kernel,H,E,T,cap,in_vmem)
    r=pl.pallas_call(body,out_shape=out_shape,in_specs=[A]*6,out_specs=[A]*len(out_shape),
        scratch_shapes=land+[pltpu.VMEM((S,T),jnp.int32),V(D,FF),V(D,FF),V(FF,D),V(2,T,D),V(2,cap,D),V(2,cap,FF),V(2,cap,D),V(2,cap,FF),V(2,cap,FF),V(2,T,D),pltpu.VMEM((2,1,T),F32),V(cap,D),
            dma((4,)),dma((2,)),dma(()),dma((7,2)),dma((E,)),dma((E,)),dma((E,)),dma((E,)),dma((H-1,E)),dma((H-1,E)),dma((H,E)),dma((H,E))],
        cost_estimate=pl.CostEstimate(flops=2*S*cap*(4*D*FF+3*T*D),bytes_accessed=S*2*(T*D+2*cap*D+3*cap*FF+T*D)+6*D*FF,transcendentals=S*cap*FF),
        compiler_params=pltpu.CompilerParams(collective_id=cid,has_side_effects=True,vmem_limit_bytes=61*2**20),name="experts_fwd")(slot,rows,cot,gw,uw,dw)
    return r[:7]


def mask_bias(lab_r,lab_c,i0,bq,K):
    lr=lab_r[:,:K]; lc=lab_c
    row=lax.broadcasted_iota(jnp.int32,(bq,K),0)+i0; col=lax.broadcasted_iota(jnp.int32,(bq,K),1)
    ok=(col<=row)&((lr==0)|(lr==lc))
    return jnp.where(ok,0.0,-1e30).astype(F32)

def eye_mask():
    return lax.broadcasted_iota(jnp.int32,(HEAD,HEAD),0)==lax.broadcasted_iota(jnp.int32,(HEAD,HEAD),1)

def to_row(col):
    return jnp.sum(jnp.where(eye_mask(),jnp.broadcast_to(col,(HEAD,HEAD)),0.0),axis=0,keepdims=True)

def to_col(row):
    return jnp.sum(jnp.where(eye_mask(),jnp.broadcast_to(row,(HEAD,HEAD)),0.0),axis=1,keepdims=True)

def greet_ctx(C):
    c=lax.axis_index("ctx"); bar=pltpu.get_barrier_semaphore()
    for j in range(1,C): pl.semaphore_signal(bar,inc=1,device_id={"ctx":lax.rem(c+j,C)},device_id_type=MESH)

def sum_ctx(C,buf,ss,rs):
    c=lax.axis_index("ctx")
    pl.semaphore_wait(pltpu.get_barrier_semaphore(),C-1)
    def cp(j): return pltpu.make_async_remote_copy(buf.at[c],buf.at[c],ss.at[j-1],rs.at[j-1],device_id={"ctx":lax.rem(c+j,C)},device_id_type=MESH)
    for j in range(1,C): cp(j).start()
    for j in range(1,C):
        q=lax.rem(c+C-j,C)
        pltpu.make_async_remote_copy(buf.at[q],buf.at[q],ss.at[j-1],rs.at[j-1],device_id={"ctx":q},device_id_type=MESH).wait_recv()
    acc=buf[0]
    for j in range(1,C): acc=acc+buf[j]
    for j in range(1,C): cp(j).wait_send()
    return acc

def attn_fwd_kernel(C,heads,bq,scale,raw,cos,sin,lab_r,lab_c,gains,qo,ko,vo,mix,inv,bias,buf,ss,rs):
    G=raw.shape[0]; cols=heads*HEAD; nb=G//HEAD
    c=lax.axis_index("ctx")
    greet_ctx(C)
    def squares(i):
        sl=pl.ds(pl.multiple_of(i*HEAD,HEAD),HEAD)
        for t in range(2):
            v=raw[sl,t*cols:(t+1)*cols]
            buf[c,pl.ds(t*nb+i,1),:]=to_row(jnp.sum(v*v,axis=1,keepdims=True))
        vo[sl,:]=raw[sl,2*cols:].astype(BF)
    loop(nb,squares)
    inv[...]=lax.rsqrt(sum_ctx(C,buf,ss,rs)/(C*cols)+EPS)
    def prep(i):
        sl=pl.ds(pl.multiple_of(i*HEAD,HEAD),HEAD)
        cs,sn=cos[sl,:],sin[sl,:]
        for t,o in ((0,qo),(1,ko)):
            r=to_col(inv[pl.ds(t*nb+i,1),:])
            for hd in range(heads):
                a=hd*HEAD
                v=raw[sl,t*cols+a:t*cols+a+HEAD]*r*gains[t:t+1,a:a+HEAD]
                o[sl,a:a+HEAD]=(v*cs+pltpu.roll(v,HEAD//2,1)*sn).astype(BF)
    loop(nb,prep)
    def block(i,K):
        rows=pl.ds(pl.multiple_of(i*bq,bq),bq)
        bias[:,:K]=mask_bias(lab_r,lab_c[rows,:],i*bq,bq,K)
        def head(hd):
            ln=pl.ds(pl.multiple_of(hd*HEAD,HEAD),HEAD)
            s=nt(qo[rows,ln],ko[:K,ln])*scale+bias[:,:K]
            p=jnp.exp(s-jnp.max(s,axis=1,keepdims=True))
            pr=(p*(1.0/jnp.sum(p,axis=1,keepdims=True))).astype(BF)
            mix[rows,ln]=nn(pr,vo[:K,ln]).astype(BF)
        loop(heads,head)
    per=G//bq//3
    for g in range(3):
        loop(per,lambda i,g=g: block(i+g*per,(g+1)*per*bq))

def attn_fwd(raw,cos,sin,lab_r,lab_c,gains,C,heads,cid,bq=128):
    G=raw.shape[0]; cols=heads*HEAD; R=2*G//HEAD; dma=pltpu.SemaphoreType.DMA
    o=jax.ShapeDtypeStruct((G,cols),BF)
    V=pl.BlockSpec(memory_space=pltpu.VMEM)
    return pl.pallas_call(functools.partial(attn_fwd_kernel,C,heads,bq,HEAD**-0.5),out_shape=[o]*4+[jax.ShapeDtypeStruct((R,HEAD),F32)],in_specs=[V]*6,out_specs=[V]*5,
        scratch_shapes=[pltpu.VMEM((bq,G),F32),pltpu.VMEM((C,R,HEAD),F32),dma((C-1,)),dma((C-1,))],
        cost_estimate=pl.CostEstimate(flops=2*2*heads*G*G*HEAD,bytes_accessed=G*cols*20,transcendentals=heads*G*G),
        compiler_params=pltpu.CompilerParams(collective_id=cid,has_side_effects=True,vmem_limit_bytes=48*2**20),name="attn_fwd")(raw,cos,sin,lab_r,lab_c,gains)

def attn_bwd_kernel(C,heads,bq,scale,q,k,v,dm,raw,inv,cos,sin,lab_r,lab_c,gains,draw,gsum,bias,aq,ak,av,buf,ss,rs):
    G=q.shape[0]; cols=heads*HEAD; nb=G//HEAD
    c=lax.axis_index("ctx")
    greet_ctx(C)
    ak[...]=jnp.zeros_like(ak); av[...]=jnp.zeros_like(av)
    def block(i,K):
        rows=pl.ds(pl.multiple_of(i*bq,bq),bq)
        bias[:,:K]=mask_bias(lab_r,lab_c[rows,:],i*bq,bq,K)
        def head(hd):
            ln=pl.ds(pl.multiple_of(hd*HEAD,HEAD),HEAD)
            qb=q[rows,ln]; kb=k[:K,ln]; db=dm[rows,ln]
            s=nt(qb,kb)*scale+bias[:,:K]
            p=jnp.exp(s-jnp.max(s,axis=1,keepdims=True))
            p=p*(1.0/jnp.sum(p,axis=1,keepdims=True))
            dp=nt(db,v[:K,ln])
            ds=(p*(dp-jnp.sum(p*dp,axis=1,keepdims=True))).astype(BF)
            aq[rows,ln]=nn(ds,kb)
            ak[:K,ln]+=tn(ds,qb)
            av[:K,ln]+=tn(p.astype(BF),db)
        loop(heads,head)
    per=G//bq//3
    for g in range(3):
        loop(per,lambda i,g=g: block(i+g*per,(g+1)*per*bq))
    gsum[...]=jnp.zeros_like(gsum)
    def unrope(i):
        sl=pl.ds(pl.multiple_of(i*HEAD,HEAD),HEAD)
        for t,a in ((0,aq),(1,ak)):
            r=to_col(inv[pl.ds(t*nb+i,1),:])
            dot=jnp.zeros((HEAD,1),F32)
            for hd in range(heads):
                b=hd*HEAD
                g=a[sl,b:b+HEAD]*scale
                g=g*cos[sl,:]-pltpu.roll(g,HEAD//2,1)*sin[sl,:]
                x=raw[sl,t*cols+b:t*cols+b+HEAD]
                gsum[t:t+1,b:b+HEAD]+=jnp.sum(g*x*r,axis=0,keepdims=True)
                g=g*gains[t:t+1,b:b+HEAD]
                a[sl,b:b+HEAD]=g
                dot=dot+jnp.sum(g*x,axis=1,keepdims=True)
            buf[c,pl.ds(t*nb+i,1),:]=to_row(dot)
        draw[sl,2*cols:]=av[sl,:].astype(BF)
    loop(nb,unrope)
    buf[0]=sum_ctx(C,buf,ss,rs)/(C*cols)
    def fin(i):
        sl=pl.ds(pl.multiple_of(i*HEAD,HEAD),HEAD)
        for t,a in ((0,aq),(1,ak)):
            r=to_col(inv[pl.ds(t*nb+i,1),:]); dot=to_col(buf[0,pl.ds(t*nb+i,1),:])
            m=r*r*r*dot
            draw[sl,t*cols:(t+1)*cols]=(a[sl,:]*r-raw[sl,t*cols:(t+1)*cols]*m).astype(BF)
    loop(nb,fin)

def attn_bwd(q,k,v,dm,raw,inv,cos,sin,lab_r,lab_c,gains,C,heads,cid,bq=128):
    G,cols=q.shape; R=2*G//HEAD; dma=pltpu.SemaphoreType.DMA
    V=pl.BlockSpec(memory_space=pltpu.VMEM)
    acc=pltpu.VMEM((G,cols),F32)
    return pl.pallas_call(functools.partial(attn_bwd_kernel,C,heads,bq,HEAD**-0.5),out_shape=[jax.ShapeDtypeStruct((G,3*cols),BF),jax.ShapeDtypeStruct((2,cols),F32)],in_specs=[V]*11,out_specs=[V]*2,
        scratch_shapes=[pltpu.VMEM((bq,G),F32),acc,acc,acc,pltpu.VMEM((C,R,HEAD),F32),dma((C-1,)),dma((C-1,))],
        cost_estimate=pl.CostEstimate(flops=5*2*heads*G*G*HEAD,bytes_accessed=G*cols*20,transcendentals=heads*G*G),
        compiler_params=pltpu.CompilerParams(collective_id=cid,has_side_effects=True,vmem_limit_bytes=56*2**20),name="attn_bwd")(q,k,v,dm,raw,inv,cos,sin,lab_r,lab_c,gains)

def ctx_barrier(H,c,h,l):
    bar=pltpu.get_barrier_semaphore()
    pl.semaphore_signal(bar,inc=1,device_id={"ctx":h*2+1-l},device_id_type=MESH)
    for j in range(1,H):
        pl.semaphore_signal(bar,inc=1,device_id={"ctx":lax.rem(h+j,H)*2+l},device_id_type=MESH)
    pl.semaphore_wait(bar,H)

def ag_ctx_kernel(H,Q,x,o,xs,xr,bs,br,lsem):
    c=lax.axis_index("ctx"); h=c//2; l=c%2
    T=x.shape[0]; R=T//Q
    loc=pltpu.make_async_copy(x,o.at[c],lsem); loc.start()
    ctx_barrier(H,c,h,l)
    sib=h*2+1-l
    def sl(q): return pl.ds(q*R,R)
    def rc(a,b,s,r,to): return pltpu.make_async_remote_copy(a,b,s,r,device_id={"ctx":to},device_id_type=MESH)
    def xc(j,q): return rc(x.at[sl(q)],o.at[c,sl(q)],xs.at[j-1,q],xr.at[j-1,q],lax.rem(h+j,H)*2+l)
    def xw(j,q):
        p=lax.rem(h+H-j,H)*2+l; return rc(x.at[sl(q)],o.at[p,sl(q)],xs.at[j-1,q],xr.at[j-1,q],p)
    def bc(j,q):
        p=c if j==0 else lax.rem(h+H-j,H)*2+l
        src=x if j==0 else o.at[p]
        return rc(src.at[sl(q)],o.at[p,sl(q)],bs.at[j,q],br.at[j,q],sib)
    def bw(j,q):
        p=sib if j==0 else lax.rem(h+H-j,H)*2+1-l
        return rc(x.at[sl(q)],o.at[p,sl(q)],bs.at[j,q],br.at[j,q],sib)
    for q in range(Q):
        for j in range(1,H): xc(j,q).start()
    for q in range(Q): bc(0,q).start()
    for q in range(Q):
        for j in range(1,H):
            xw(j,q).wait_recv(); bc(j,q).start()
    for j in range(H):
        for q in range(Q):
            bw(j,q).wait_recv(); bc(j,q).wait_send()
            if j>0: xc(j,q).wait_send()
    loc.wait()

def ag_ctx(x,C,cid,Q=4):
    T,D=x.shape; H=C//2; dma=pltpu.SemaphoreType.DMA
    A=pl.BlockSpec(memory_space=pl.ANY)
    return pl.pallas_call(functools.partial(ag_ctx_kernel,H,Q),out_shape=jax.ShapeDtypeStruct((C,T,D),x.dtype),in_specs=[A],out_specs=A,
        scratch_shapes=[dma((H-1,Q)),dma((H-1,Q)),dma((H,Q)),dma((H,Q)),dma(())],
        compiler_params=pltpu.CompilerParams(collective_id=cid,has_side_effects=True),name="ag_ctx")(x)

def rs_ctx_kernel(H,Q,x,o,own,r1,r2,ld,s1,q1,s2,q2,osem):
    c=lax.axis_index("ctx"); h=c//2; l=c%2
    T=own.shape[1]; R=T//Q
    def sl(q): return pl.ds(q*R,R)
    hs=[lax.rem(h+j,H) for j in range(1,H)]+[h]
    def load(i): return pltpu.make_async_copy(x.at[hs[i]*2+l],own.at[hs[i]],ld.at[i])
    for i in range(H): load(i).start()
    ctx_barrier(H,c,h,l)
    def c1(i,q): return pltpu.make_async_remote_copy(x.at[hs[i]*2+1-l,sl(q)],r1.at[hs[i],sl(q)],s1.at[hs[i],q],q1.at[hs[i],q],device_id={"ctx":h*2+1-l},device_id_type=MESH)
    def c2(j,q): return pltpu.make_async_remote_copy(own.at[hs[j-1],sl(q)],r2.at[j-1,sl(q)],s2.at[j-1,q],q2.at[j-1,q],device_id={"ctx":hs[j-1]*2+l},device_id_type=MESH)
    for i in range(H):
        for q in range(Q): c1(i,q).start()
    for i in range(H):
        load(i).wait()
        for q in range(Q):
            c1(i,q).wait_recv()
            add_into(own.at[hs[i],sl(q)],r1.at[hs[i],sl(q)])
            if i<H-1: c2(i+1,q).start()
    for q in range(Q):
        for j in range(1,H):
            c2(j,q).wait_recv()
            add_into(own.at[h,sl(q)],r2.at[j-1,sl(q)])
    out=pltpu.make_async_copy(own.at[h],o,osem); out.start()
    for q in range(Q):
        for i in range(H): c1(i,q).wait_send()
        for j in range(1,H): c2(j,q).wait_send()
    out.wait()

def rs_ctx(x,cid,Q=4):
    C,T,D=x.shape; H=C//2; dma=pltpu.SemaphoreType.DMA
    A=pl.BlockSpec(memory_space=pl.ANY)
    return pl.pallas_call(functools.partial(rs_ctx_kernel,H,Q),out_shape=jax.ShapeDtypeStruct((T,D),x.dtype),in_specs=[A],out_specs=A,
        scratch_shapes=[pltpu.VMEM((H,T,D),BF),pltpu.VMEM((H,T,D),BF),pltpu.VMEM((H-1,T,D),BF),dma((H,)),dma((H,Q)),dma((H,Q)),dma((H-1,Q)),dma((H-1,Q)),dma(())],
        compiler_params=pltpu.CompilerParams(collective_id=cid,has_side_effects=True,vmem_limit_bytes=40*2**20),name="rs_ctx")(x)


def front_kernel(N,C,E,Q,wq,wk,wv,wo,nx,qkv,ow,na,a_s,a_r,up_s,up_r,dn_s,dn_r,y_s,y_r,xs_,xr_,bs_,br_,lsem):
    p=lax.axis_index("dp"); c=lax.axis_index("ctx"); e=lax.axis_index("exp")
    H=C//2; h=c//2; l=c%2; sib=h*2+1-l
    D=wq.shape[1]; cols=D//C; piece=cols//N; T=nx.shape[0]; R=T//Q
    def dpeer(j): return lax.rem(p+j,N)
    def cpeer(j): return lax.rem(c+j,C)
    bar=pltpu.get_barrier_semaphore()
    def sig(**kw): pl.semaphore_signal(bar,inc=1,device_id=kw,device_id_type=MESH)
    for j in range(1,N): sig(dp=dpeer(j))
    for j in range(1,C): sig(ctx=cpeer(j))
    @pl.when(e>0)
    def _(): sig(exp=e-1)
    @pl.when(e<E-1)
    def _(): sig(exp=e+1)
    def rc(a,b,s,r,**kw): return pltpu.make_async_remote_copy(a,b,s,r,device_id=kw,device_id_type=MESH)
    W=(wq,wk,wv)
    def src(t,d,q): return W[t].at[:,pl.ds(pl.multiple_of(d*(D//N)+q*piece,128),piece)]
    def dst(t,d,q): return qkv.at[p,q,e,:,pl.ds(t*cols+d*piece,piece)]
    TD=[(t,d) for t in range(3) for d in range(N)]
    local=[pltpu.make_async_copy(src(t,d,c),dst(t,d,c),lsem.at[i]) for i,(t,d) in enumerate(TD)]
    local_w=pltpu.make_async_copy(wo,ow.at[p,e],lsem.at[len(TD)])
    local_n=pltpu.make_async_copy(nx,na.at[c],lsem.at[len(TD)+1])
    for x in local+[local_w,local_n]: x.start()
    def away(j,i):
        t,d=TD[i]; q=cpeer(j)
        return rc(src(t,d,q),dst(t,d,c),a_s.at[j-1,i],a_r.at[j-1,i],ctx=q)
    def home(j,i):
        t,d=TD[i]; q=lax.rem(c+C-j,C)
        return rc(src(t,d,q),dst(t,d,q),a_s.at[j-1,i],a_r.at[j-1,i],ctx=q)
    def both(q,ee): return ((0,qkv.at[q,:,ee]),(1,ow.at[q,ee]))
    def up(i,ee): b=both(p,ee)[i][1]; return rc(b,b,up_s.at[i,ee],up_r.at[i,ee],exp=e+1)
    def dn(i,ee): b=both(p,ee)[i][1]; return rc(b,b,dn_s.at[i,ee],dn_r.at[i,ee],exp=e-1)
    def ys(i,j,ee): b=both(p,ee)[i][1]; return rc(b,b,y_s.at[i,j-1,ee],y_r.at[i,j-1,ee],dp=dpeer(j))
    def yr(i,j,ee): q=lax.rem(p+N-j,N); b=both(q,ee)[i][1]; return rc(b,b,y_s.at[i,j-1,ee],y_r.at[i,j-1,ee],dp=q)
    def sl(q): return pl.ds(q*R,R)
    def xc(j,q): return rc(nx.at[sl(q)],na.at[c,sl(q)],xs_.at[j-1,q],xr_.at[j-1,q],ctx=lax.rem(h+j,H)*2+l)
    def xw(j,q):
        s=lax.rem(h+H-j,H)*2+l; return rc(nx.at[sl(q)],na.at[s,sl(q)],xs_.at[j-1,q],xr_.at[j-1,q],ctx=s)
    def bc(j,q):
        s=c if j==0 else lax.rem(h+H-j,H)*2+l
        a=nx if j==0 else na.at[s]
        return rc(a.at[sl(q)],na.at[s,sl(q)],bs_.at[j,q],br_.at[j,q],ctx=sib)
    def bw(j,q):
        s=sib if j==0 else lax.rem(h+H-j,H)*2+1-l
        return rc(nx.at[sl(q)],na.at[s,sl(q)],bs_.at[j,q],br_.at[j,q],ctx=sib)
    pl.semaphore_wait(bar,(N-1)+(C-1)+(e>0).astype(jnp.int32)+(e<E-1).astype(jnp.int32))
    for j in range(1,C):
        for i in range(len(TD)): away(j,i).start()
    for q in range(Q):
        for j in range(1,H): xc(j,q).start()
    for q in range(Q): bc(0,q).start()
    for x in local: x.wait()
    local_w.wait()
    for j in range(1,C):
        for i in range(len(TD)): home(j,i).wait_recv()
    for i in range(2):
        for j in range(1,N): ys(i,j,e).start()
        @pl.when(e<E-1)
        def _(): up(i,e).start()
        @pl.when(e>0)
        def _(): dn(i,e).start()
    def rounds(r0):
        r=r0+1
        for i in range(2):
            @pl.when(e>=r)
            def _():
                up(i,e-r).wait_recv()
                @pl.when(e<E-1)
                def _(): up(i,e-r).start()
                for j in range(1,N): ys(i,j,e-r).start()
            @pl.when(e+r<E)
            def _():
                dn(i,e+r).wait_recv()
                @pl.when(e>0)
                def _(): dn(i,e+r).start()
                for j in range(1,N): ys(i,j,e+r).start()
        @pl.when(r0==0)
        def _():
            for q in range(Q):
                for j in range(1,H):
                    xw(j,q).wait_recv(); bc(j,q).start()
    loop(E-1,rounds)
    def finish(ee):
        for i in range(2):
            for j in range(1,N):
                yr(i,j,ee).wait_recv(); ys(i,j,ee).wait_send()
            @pl.when(jnp.logical_and(e<E-1,ee<=e))
            def _(): up(i,ee).wait_send()
            @pl.when(jnp.logical_and(e>0,ee>=e))
            def _(): dn(i,ee).wait_send()
    loop(E,finish)
    for j in range(1,C):
        for i in range(len(TD)): away(j,i).wait_send()
    for q in range(Q):
        for j in range(1,H): xc(j,q).wait_send()
        for j in range(H):
            bc(j,q).wait_send(); bw(j,q).wait_recv()
    local_n.wait()


def front(wq,wk,wv,wo,nx,N,C,E,cid,Q=2):
    S,D=wq.shape; T=nx.shape[0]; H=C//2; dma=pltpu.SemaphoreType.DMA
    A=pl.BlockSpec(memory_space=pl.ANY)
    return pl.pallas_call(functools.partial(front_kernel,N,C,E,Q),
        out_shape=[jax.ShapeDtypeStruct((N,C,E,S,3*D//C),BF),jax.ShapeDtypeStruct((N,E,S,D),BF),jax.ShapeDtypeStruct((C,T,D),BF)],
        in_specs=[A]*5,out_specs=[A]*3,
        scratch_shapes=[dma((C-1,3*N)),dma((C-1,3*N)),dma((2,E)),dma((2,E)),dma((2,E)),dma((2,E)),dma((2,N-1,E)),dma((2,N-1,E)),dma((H-1,Q)),dma((H-1,Q)),dma((H,Q)),dma((H,Q)),dma((3*N+2,))],
        compiler_params=pltpu.CompilerParams(collective_id=cid,has_side_effects=True),name="front")(wq,wk,wv,wo,nx)


def dot_nn(a, b):
    return lax.dot_general(a, b, (((1,), (0,)), ((), ())), preferred_element_type=F32)


def dot_tn(a, b):
    return lax.dot_general(a, b, (((0,), (0,)), ((), ())), preferred_element_type=F32)


def dot_nt(a, b):
    return lax.dot_general(a, b, (((1,), (1,)), ((), ())), preferred_element_type=F32)


def low_dp(grad, n_dp):
    low = grad.astype(BF)
    if n_dp != 2:
        return (lax.psum(low, "dp"),)
    return low, lax.ppermute(low, "dp", [(0, 1), (1, 0)])


def per_device(
    hidden_in,
    segments,
    routes,
    attn_gain,
    query_weight,
    key_weight,
    value_weight,
    query_gain,
    key_gain,
    output_weight,
    ffn_gain,
    router_weight,
    gate_weight,
    up_weight,
    down_weight,
    cotangent,
):
    n_dp, n_ctx, n_exp = (lax.axis_size(a) for a in ALL)
    tok, width = hidden_in.shape[2:]
    topk = routes.shape[3]
    experts = n_ctx * n_exp
    cap = (5 * tok * topk + 4 * experts - 1) // (4 * experts)
    cap = -(-cap // 16) * 16
    group = segments.shape[2]
    shard = query_weight.shape[0]
    cols = width // n_ctx
    piece = cols // n_dp
    heads = cols // HEAD
    ctx_me = lax.axis_index("ctx")
    exp_me = lax.axis_index("exp")
    expert_me = ctx_me * n_exp + exp_me

    def own_cols(vec):
        return lax.dynamic_index_in_dim(
            vec.reshape(n_dp, n_ctx, piece), ctx_me, 1, keepdims=False
        ).reshape(cols)

    own_routes = routes[0, 0]
    expert_ids = jnp.arange(experts, dtype=jnp.int32)
    hits = jnp.sum((own_routes[:, :, None] == expert_ids).astype(jnp.int32), axis=1)
    tokens = jnp.arange(tok, dtype=jnp.int32)
    lower = (tokens[:, None] > tokens[None, :]).astype(BF)
    earlier = dot_nn(lower, hits.astype(BF)).astype(jnp.int32)
    slot_local = jnp.where(hits > 0, earlier, -1).T
    slot = lax.all_to_all(slot_local, MOE, split_axis=0, concat_axis=0, tiled=True)
    slot = slot.reshape(experts, tok)
    cot = cotangent[0, 0]

    hidden = hidden_in[0, 0].astype(F32)
    labels = segments[0, 0]
    index = jnp.arange(group, dtype=jnp.int32)
    before = jnp.sum((labels[None, :] < labels[:, None]).astype(jnp.int32), axis=1)
    positions = index - before + jnp.where(labels > 0, PROMPT, 0).astype(jnp.int32)
    half = HEAD // 2
    frequency = THETA ** (-(jnp.arange(half, dtype=F32) * 2.0 / HEAD))
    angles = positions.astype(F32)[:, None] * frequency[None, :]
    cos, sin = jnp.cos(angles), jnp.sin(angles)
    cos = jnp.concatenate([cos, cos], axis=1)
    sin = jnp.concatenate([-sin, sin], axis=1)
    label_row, label_col = labels[None, :], labels[:, None]
    attn_gain_f = attn_gain.astype(F32)
    ffn_gain_f = ffn_gain.astype(F32)
    q_gain = own_cols(query_gain.astype(F32))
    k_gain = own_cols(key_gain.astype(F32))

    attn_r = lax.rsqrt(jnp.mean(hidden * hidden, axis=-1, keepdims=True) + EPS)
    normed = (hidden * attn_r * attn_gain_f).astype(BF)
    qkv_w, out_w, normed_g = front(
        query_weight, key_weight, value_weight, output_weight, normed, n_dp, n_ctx, n_exp, 5
    )
    qkv_w = qkv_w.reshape(width, 3 * cols)
    out_w = out_w.reshape(cols, width)
    normed_g = normed_g.reshape(group, width)
    cot, normed_g = lax.optimization_barrier((cot, normed_g))
    cot_all = lax.all_gather(cot, MOE, axis=0, tiled=False)
    raw = dot_nn(normed_g, qkv_w)
    gains = jnp.stack([q_gain, k_gain])
    q_rot, k_rot, v_low, mix, inv = attn_fwd(
        raw, cos, sin, label_row, label_col, gains, n_ctx, heads, 9
    )
    branch = rs_ctx(dot_nn(mix, out_w).astype(BF).reshape(n_ctx, tok, width), 6)
    residual = hidden + branch.astype(F32)

    ffn_r = lax.rsqrt(jnp.mean(residual * residual, axis=-1, keepdims=True) + EPS)
    ffn_normed = (residual * ffn_r * ffn_gain_f).astype(BF)
    logits = dot_nn(ffn_normed, router_weight)
    router_prob = jax.nn.softmax(logits, axis=-1)
    gates = jnp.where(hits > 0, router_prob, 0.0).astype(BF)
    padded = jnp.zeros((experts, width), BF).at[:, :tok].set(gates.T)
    rows_ext = jnp.concatenate([ffn_normed, padded], axis=0)
    gate_mat, up_mat, down_mat = gate_weight[0], up_weight[0], down_weight[0]
    received, expert_hidden, d_out, d_gate_pre, d_up_pre, moe_part, d_gate_at = fwd_call(
        slot, rows_ext, cot_all, gate_mat, up_mat, down_mat, cap, n_ctx, n_exp, tok
    )
    total = experts * cap

    d_gate = lax.all_to_all(
        d_gate_at.reshape(experts, tok), MOE, split_axis=0, concat_axis=0, tiled=True
    ).T
    received = received.reshape(total, width)
    gate_low = dot_tn(received, d_gate_pre.reshape(total, -1)).astype(BF)
    up_low = dot_tn(received, d_up_pre.reshape(total, -1)).astype(BF)
    swap = (gate_low, up_low) if n_dp == 2 else ()
    d_tokens, others = back_call(
        slot, d_gate_pre, d_up_pre, gate_mat, up_mat, swap, n_ctx, n_exp, tok, (1, 8)
    )
    moe_part, d_tokens = lax.optimization_barrier((moe_part, d_tokens))
    moe_out = lax.psum_scatter(
        moe_part.reshape(experts * tok, width), MOE, scatter_dimension=0, tiled=True
    )
    down_grad = dot_tn(expert_hidden.reshape(total, -1), d_out.reshape(total, width))
    wide = [(a, b) for a, b in zip(swap, others)] or [low_dp(g, n_dp) for g in (gate_low, up_low)]
    wide = wide + [low_dp(down_grad, n_dp)]

    d_router = d_gate
    d_logits = (
        router_prob * (d_router - jnp.sum(router_prob * d_router, axis=-1, keepdims=True))
    ).astype(BF)
    router_grad = dot_tn(d_logits, ffn_normed)
    d_ffn = d_tokens.astype(F32) + dot_nt(d_logits, router_weight)
    ffn_gain_grad = jnp.sum(d_ffn * residual * ffn_r, axis=0)
    weighted = d_ffn * ffn_gain_f
    d_residual = cot.astype(F32) + (
        weighted * ffn_r
        - residual * ffn_r**3 * jnp.mean(residual * weighted, axis=-1, keepdims=True)
    )
    d_branch = d_residual.astype(BF)

    d_branch_g = ag_ctx(d_branch, n_ctx, 7).reshape(group, width)
    out_grad = dot_tn(mix, d_branch_g)
    d_mix = dot_nt(d_branch_g, out_w).astype(BF)
    d_raw, gain_parts = attn_bwd(
        q_rot, k_rot, v_low, d_mix, raw, inv, cos, sin, label_row, label_col, gains, n_ctx, heads, 10
    )
    spread = jnp.zeros((2, n_dp, n_ctx, piece), F32)
    spread = lax.dynamic_update_slice(
        spread, gain_parts.reshape(2, n_dp, 1, piece), (0, 0, ctx_me, 0)
    ).reshape(2, width)
    small = jnp.concatenate([router_grad, spread, ffn_gain_grad[None]], axis=0)
    small = jnp.pad(small, ((0, 8 - small.shape[0] % 8), (0, 0)))
    d_part_n = dot_nt(d_raw, qkv_w).astype(BF).reshape(n_ctx, tok, width)
    qkv_grad = dot_tn(normed_g, d_raw).astype(BF).reshape(n_dp, n_ctx, n_exp, shard, 3 * cols)
    out_part = out_grad.astype(BF).reshape(n_dp, n_exp, shard, width)
    qkv_sum, out_sum, hidden_grad, small = tail(
        qkv_grad, out_part, d_part_n, hidden_in[0, 0], d_residual, attn_gain_f[None], small
    )
    wide, moe_out, small = lax.optimization_barrier((wide, moe_out, small))
    output = (residual + moe_out.astype(F32)).astype(BF)
    gate_sum, up_sum, down_sum = (sum(x.astype(F32) for x in pair) for pair in wide)

    qkv_sum = qkv_sum.reshape(n_ctx, shard, 3, n_dp, piece)
    qkv_sum = qkv_sum.transpose(2, 1, 3, 0, 4).reshape(3, shard, width).astype(F32)
    out_sum = out_sum.astype(F32)
    return (
        output[None, None],
        hidden_grad[None, None],
        small[-1],
        qkv_sum[0],
        qkv_sum[1],
        qkv_sum[2],
        small[experts],
        small[experts + 1],
        out_sum,
        small[experts + 2],
        small[:experts].T,
        gate_sum[None],
        up_sum[None],
        down_sum[None],
    )


def solution(mesh):
    tokens = P("dp", "exp", "ctx", None)
    rows = P(ALL, None)
    expert = P(MOE, None, None)
    return jax.shard_map(
        per_device,
        mesh=mesh,
        in_specs=(
            tokens,
            P("dp", "exp", None),
            tokens,
            P(),
            rows,
            rows,
            rows,
            P(),
            P(),
            rows,
            P(),
            P(),
            expert,
            expert,
            expert,
            tokens,
        ),
        out_specs=(
            tokens,
            tokens,
            P(),
            rows,
            rows,
            rows,
            P(),
            P(),
            rows,
            P(),
            P(),
            expert,
            expert,
            expert,
        ),
        check_vma=False,
    )
```

```python
import functools

import jax
import jax.numpy as jnp
from jax import lax
from jax.experimental import pallas as pl
from jax.experimental.pallas import tpu as pltpu
from jax.sharding import PartitionSpec as P

HEAD = 128
PROMPT = 512
EPS = 1e-05
THETA = 10000.0
MASKED = -1e30
BF = jnp.bfloat16
F32 = jnp.float32
ALL = ("dp", "ctx", "exp")
MOE = ("ctx", "exp")
ROWS = ("dp", "exp")
MESH = pl.DeviceIdType.MESH


def by_distance(me, n):
    far=[jnp.abs(me-j)*n+j for j in range(n)]
    rank=[sum(((far[i]>far[j]).astype(jnp.int32) for i in range(n) if i!=j), jnp.int32(0)) for j in range(n)]
    def at(k):
        v=jnp.int32(0)
        for j in range(n): v=v+jnp.where(rank[j]==k,j,0)
        return v
    return at


def loop(n, body):
    def step(i,_):
        body(i)
        return 0
    lax.fori_loop(0,n,step,0)


def add_into(dst, src, rows=16):
    n=dst.shape[-2]//rows
    lead=dst.shape[:-2]
    assert not lead
    def body(i,_):
        sl=pl.ds(pl.multiple_of(i*rows,rows),rows)
        dst[sl,:]=(dst[sl,:].astype(F32)+src[sl,:].astype(F32)).astype(dst.dtype)
        return 0
    lax.fori_loop(0,n,body,0)


def add3(dst,src):
    if len(dst.shape)==2: add_into(dst,src); return
    def body(i,_):
        add_into(dst.at[i],src.at[i]); return 0
    lax.fori_loop(0,dst.shape[0],body,0)

def tail_kernel(N,C,E,nrm,dr,w,go,hid,dres,gain,sm,o1,o2,o3,oo,od,osm,own_q,own_o,own_d,yq,yo,uq,uo,vq,vo,d1,d2,ld,ldd,ys,yr,zs,zu,zd,s1,r1,s2,r2,a_s,a_r,osem,hv,rv,gv,b0,b1,b2,t_s,t_r,nv,drv,wv,sq,sd,m_s):
    p=lax.axis_index("dp"); c=lax.axis_index("ctx"); e=lax.axis_index("exp")
    H=C//2; h=c//2; l=c%2
    def dpeer(j): return lax.rem(p+j,N)
    def cpeer(j): return lax.rem(c+j,C)
    def hpeer(j): return lax.rem(h+j,H)
    bar=pltpu.get_barrier_semaphore()
    def sig(**kw): pl.semaphore_signal(bar,inc=1,device_id=kw,device_id_type=MESH)
    for j in range(1,N): sig(dp=dpeer(j))
    for j in range(1,C): sig(ctx=cpeer(j))
    for j in range(1,E): sig(exp=lax.rem(e+j,E))
    order=by_distance(e,E)
    def rc(src,dst,ss,rs,**kw): return pltpu.make_async_remote_copy(src,dst,ss,rs,device_id=kw,device_id_type=MESH)
    def loads(o): return [pltpu.make_async_copy(go.at[p,o],own_o.at[o],ld.at[1,o])]
    def cy(j,o):
        q=dpeer(j)
        return [rc(sq.at[j-1,o],yq.at[j-1,o],ys.at[0,j-1,o],yr.at[0,j-1,o],dp=q), rc(go.at[q,o],yo.at[j-1,o],ys.at[1,j-1,o],yr.at[1,j-1,o],dp=q)]
    def cu(o): return [rc(own_q.at[o],uq.at[o],zs.at[0,o],zu.at[0,o],exp=e+1), rc(own_o.at[o],uo.at[o],zs.at[1,o],zu.at[1,o],exp=e+1)]
    def cd(o): return [rc(own_q.at[o],vq.at[o],zs.at[0,o],zd.at[0,o],exp=e-1), rc(own_o.at[o],vo.at[o],zs.at[1,o],zd.at[1,o],exp=e-1)]
    def c1(hh): return rc(sd.at[hh],d1.at[hh],s1.at[hh],r1.at[hh],ctx=h*2+1-l)
    def c2(j):
        hh=hpeer(j); return rc(own_d.at[hh],d2.at[j-1],s2.at[j-1],r2.at[j-1],ctx=hh*2+l)
    hs=[hpeer(j) for j in range(1,H)]+[h]
    def start_loads(k):
        for x in loads(k): x.start()
    side=[pltpu.make_async_copy(hid,hv,osem.at[3]),pltpu.make_async_copy(dres,rv,osem.at[4]),pltpu.make_async_copy(gain,gv,osem.at[5]),pltpu.make_async_copy(sm,b0.at[p],osem.at[6])]
    for x in side: x.start()
    loop(E,start_loads)
    big=[pltpu.make_async_copy(a,b,m_s.at[i]) for i,(a,b) in enumerate(((nrm,nv),(dr,drv),(w,wv)))]
    for x in big: x.start()
    Dm=wv.shape[0]; W3=wv.shape[1]; S_=own_q.shape[2]; T_=own_d.shape[1]; pc=Dm//(N*C)
    def grads(q,put):
        def chunk(cc):
            cl=pl.ds(pl.multiple_of(q*(Dm//N)+cc*pc,128),pc)
            st=W3//3
            for t in range(3):
                g=tn(nv[:,cl],drv[:,t*st:(t+1)*st]).astype(BF)
                for ee in range(E): put.at[ee][cc,:,t*st:(t+1)*st]=g[ee*S_:(ee+1)*S_]
        loop(C,chunk)
    def dnorm(cc,put):
        rw=pl.ds(pl.multiple_of(cc*T_,T_),T_)
        def chunk(n):
            cl=pl.ds(pl.multiple_of(n*512,512),512)
            put[:,cl]=nt(drv[rw,:],wv[cl,:]).astype(BF)
        loop(Dm//512,chunk)
    pl.semaphore_wait(bar,(N-1)+(C-1)+(E-1))
    def start_o(k):
        for j in range(1,N): cy(j,order(k))[1].start()
    loop(E,start_o)
    big[0].wait(); big[1].wait()
    for j in range(1,N): grads(dpeer(j),sq.at[j-1])
    def start_q(k):
        for j in range(1,N): cy(j,order(k))[0].start()
    loop(E,start_q)
    big[2].wait()
    for hh in hs:
        dnorm(hh*2+1-l,sd.at[hh]); c1(hh).start()
        dnorm(hh*2+l,own_d.at[hh])
    grads(p,own_q)
    for i,hh in enumerate(hs):
        c1(hh).wait_recv(); add_into(own_d.at[hh],d1.at[hh])
        if i<H-1: c2(i+1).start()
    def line(k):
        o=order(k)
        for x in loads(o): x.wait()
        for j in range(1,N):
            for x in cy(j,o): x.wait_recv()
            add3(own_q.at[o],yq.at[j-1,o]); add3(own_o.at[o],yo.at[j-1,o])
        if True:
            @pl.when(o>e)
            def _():
                @pl.when(e>0)
                def _():
                    for x in cu(o): x.wait_recv()
                    add3(own_q.at[o],uq.at[o]); add3(own_o.at[o],uo.at[o])
                for x in cu(o): x.start()
            @pl.when(o<e)
            def _():
                @pl.when(e<E-1)
                def _():
                    for x in cd(o): x.wait_recv()
                    add3(own_q.at[o],vq.at[o]); add3(own_o.at[o],vo.at[o])
                for x in cd(o): x.start()
    small=((b0,"dp",N,p),(b1,"ctx",C,c),(b2,"exp",E,e))
    def hop(t,j):
        b,a,n,i=small[t]
        return rc(b.at[i],b.at[i],t_s.at[t,j-1],t_r.at[t,j-1],**{a:lax.rem(i+j,n)})
    def gathered(t):
        b,a,n,i=small[t]
        for j in range(1,n):
            q=lax.rem(i+n-j,n)
            rc(b.at[q],b.at[q],t_s.at[t,j-1],t_r.at[t,j-1],**{a:q}).wait_recv()
        x=b[0]
        for j in range(1,n): x=x+b[j]
        return x
    def send(t):
        for j in range(1,small[t][2]): hop(t,j).start()
    T,D=hv.shape; RB=16
    lastrow=b0.shape[1]-1
    def epilogue(i):
        sl=pl.ds(pl.multiple_of(i*RB,RB),RB)
        d=own_d[h,sl,:].astype(F32); x=hv[sl,:].astype(F32)
        r=lax.rsqrt(jnp.mean(x*x,axis=1,keepdims=True)+EPS)
        b0[p,lastrow:,:]+=jnp.sum(d*x*r,axis=0,keepdims=True)
        w=d*gv[...]
        own_d[h,sl,:]=(rv[sl,:]+(w*r-x*(r*r*r)*jnp.mean(x*w,axis=1,keepdims=True))).astype(BF)
    def lines(k):
        line(k)
        @pl.when(k==0)
        def _():
            for j in range(1,H):
                c2(j).wait_recv(); add_into(own_d.at[h],d2.at[j-1])
            for x in side: x.wait()
            loop(T//RB,epilogue)
            send(0)
            pltpu.make_async_copy(own_d.at[h],od,osem.at[0]).start()
        @pl.when(k==1)
        def _():
            b1[c]=gathered(0); send(1)
        @pl.when(k==2)
        def _():
            b2[e]=gathered(1); send(2)
    loop(E,lines)
    @pl.when(e>0)
    def _():
        for x in cu(e): x.wait_recv()
        add3(own_q.at[e],uq.at[e]); add3(own_o.at[e],uo.at[e])
    @pl.when(e<E-1)
    def _():
        for x in cd(e): x.wait_recv()
        add3(own_q.at[e],vq.at[e]); add3(own_o.at[e],vo.at[e])
    outs=(o1,o2,o3); cols=W3//3
    TD=[(t,d) for t in range(3) for d in range(N)]
    def src(q,t,d): return own_q.at[e,q,:,pl.ds(t*cols+d*pc,pc)]
    def dst(q,t,d): return outs[t].at[:,pl.ds(pl.multiple_of(d*(Dm//N)+q*pc,128),pc)]
    def ca(j,i): q=cpeer(j); return rc(src(q,*TD[i]),dst(c,*TD[i]),a_s.at[j-1,i],a_r.at[j-1,i],ctx=q)
    def cw(j,i): q=lax.rem(c+C-j,C); return rc(src(q,*TD[i]),dst(q,*TD[i]),a_s.at[j-1,i],a_r.at[j-1,i],ctx=q)
    for j in range(1,C):
        for i in range(len(TD)): ca(j,i).start()
    l1=[pltpu.make_async_copy(src(c,*TD[i]),dst(c,*TD[i]),m_s.at[3+i]) for i in range(len(TD))]
    for x in l1: x.start()
    l2=pltpu.make_async_copy(own_o.at[e],oo,osem.at[2]); l2.start()
    def drain(k):
        for j in range(1,N):
            for x in cy(j,k): x.wait_send()
        @pl.when(k!=e)
        def _():
            for x in cu(k): x.wait_send()
    loop(E,drain)
    for hh in hs: c1(hh).wait_send()
    for j in range(1,H): c2(j).wait_send()
    for j in range(1,C):
        for i in range(len(TD)):
            ca(j,i).wait_send(); cw(j,i).wait_recv()
    for t in range(3):
        for j in range(1,small[t][2]): hop(t,j).wait_send()
    b0[0]=gathered(2)
    so=pltpu.make_async_copy(b0.at[0],osm,osem.at[7]); so.start()
    pltpu.make_async_copy(own_d.at[h],od,osem.at[0]).wait(); l2.wait(); so.wait()
    for x in l1: x.wait()

def tail(nrm,dr,w,go,hid,dres,gain,sm,C,cid=2):
    N,E,S,D=go.shape; W3=dr.shape[1]; G=nrm.shape[0]; T=G//C; H=C//2; R=sm.shape[0]
    dma=pltpu.SemaphoreType.DMA; V=lambda *s: pltpu.VMEM(s,BF); FV=lambda *s: pltpu.VMEM(s,F32)
    M=max(N,C,E)-1
    sd=jax.ShapeDtypeStruct((S,D),BF)
    return pl.pallas_call(functools.partial(tail_kernel,N,C,E),
        out_shape=[sd]*4+[jax.ShapeDtypeStruct((T,D),BF),jax.ShapeDtypeStruct((R,D),F32)],
        in_specs=[pl.BlockSpec(memory_space=pl.ANY)]*8,
        out_specs=[pl.BlockSpec(memory_space=pl.ANY)]*6,
        scratch_shapes=[V(E,C,S,W3),V(E,S,D),V(H,T,D),V(N-1,E,C,S,W3),V(N-1,E,S,D),V(E,C,S,W3),V(E,S,D),V(E,C,S,W3),V(E,S,D),V(H,T,D),V(H-1,T,D),
            dma((2,E)),dma((H,)),dma((2,N-1,E)),dma((2,N-1,E)),dma((2,E)),dma((2,E)),dma((2,E)),dma((H,)),dma((H,)),dma((H-1,)),dma((H-1,)),dma((C-1,3*N)),dma((C-1,3*N)),dma((8,)),
            V(T,D),FV(T,D),FV(1,D),FV(N,R,D),FV(C,R,D),FV(E,R,D),dma((3,M)),dma((3,M)),
            V(G,D),V(G,W3),V(D,W3),V(N-1,E,C,S,W3),V(H,T,D),dma((3+3*N,))],
        cost_estimate=pl.CostEstimate(flops=4*G*D*W3,bytes_accessed=2*(G*D+G*W3+D*W3),transcendentals=0),
        compiler_params=pltpu.CompilerParams(collective_id=cid,has_side_effects=True,vmem_limit_bytes=61*2**20),
        name="tail")(nrm,dr,w,go,hid,dres,gain,sm)

def nn(a,b): return lax.dot_general(a,b,(((1,),(0,)),((),())),preferred_element_type=F32)
def tn(a,b): return lax.dot_general(a,b,(((0,),(0,)),((),())),preferred_element_type=F32)
def nt(a,b): return lax.dot_general(a,b,(((1,),(1,)),((),())),preferred_element_type=F32)

def pick_of(slot_row, cap):
    T=slot_row.shape[1]
    return jnp.broadcast_to(slot_row,(cap,T))==lax.broadcasted_iota(jnp.int32,(cap,T),0)

def back_kernel(H,E,cap,X,slot,dgp,dup,gw,uw,*rest):
    ex_in,o_ref,ex_out=rest[:X],rest[X],rest[X+1:2*X+1]
    own,r1,r2,rz,snd,gb,ub,slv,wg,wu,ld_sem,w_sem,s1,q1,s2,q2,s3,qz,o_sem=rest[2*X+1:2*X+20]
    c=lax.axis_index("ctx"); e=lax.axis_index("exp")
    h=c//2; l=c%2
    T,W=own.shape[2:]; FF=wg.shape[1]
    sib={"ctx":h*2+1-l}
    def xpeer(j): return lax.rem(h+j,H)
    bar=pltpu.get_barrier_semaphore()
    pl.semaphore_signal(bar,inc=1,device_id=sib,device_id_type=MESH)
    for j in range(1,H):
        pl.semaphore_signal(bar,inc=1,device_id={"ctx":xpeer(j)*2+l},device_id_type=MESH)
    @pl.when(e>0)
    def _(): pl.semaphore_signal(bar,inc=1,device_id={"exp":e-1},device_id_type=MESH)
    @pl.when(e<E-1)
    def _(): pl.semaphore_signal(bar,inc=1,device_id={"exp":e+1},device_id_type=MESH)
    def ex(i):
        es,er=rest[2*X+20:]
        return pltpu.make_async_remote_copy(ex_in[i].at[:ex_out[i].shape[0]],ex_out[i],es.at[i],er.at[i],device_id={"dp":1-lax.axis_index("dp")},device_id_type=MESH)
    if X: pl.semaphore_signal(bar,inc=1,device_id={"dp":1-lax.axis_index("dp")},device_id_type=MESH)
    order=by_distance(e,E)
    wl=[pltpu.make_async_copy(gw,wg,w_sem.at[0]),pltpu.make_async_copy(uw,wu,w_sem.at[1])]
    for x in wl: x.start()
    NS=snd.shape[0]; M=H*E
    def place(m):
        return lax.rem(h+1+m//E,H),order(lax.rem(m,E))
    def loads(n):
        hh,o=place(n//2)
        s=(hh*2+jnp.where(lax.rem(n,2)==0,1-l,l))*E+o; b=lax.rem(n,2)
        return [pltpu.make_async_copy(dgp.at[s],gb.at[b],ld_sem.at[0,b]),pltpu.make_async_copy(dup.at[s],ub.at[b],ld_sem.at[1,b])],s
    for x in loads(0)[0]: x.start()
    def c1(m):
        hh,o=place(m)
        return pltpu.make_async_remote_copy(snd.at[lax.rem(m,NS)],r1.at[hh,o],s1.at[m],q1.at[hh,o],device_id=sib,device_id_type=MESH)
    def c2(j,o):
        hh=xpeer(j)
        return pltpu.make_async_remote_copy(own.at[hh,o],r2.at[j-1,o],s2.at[j-1,o],q2.at[j-1,o],device_id={"ctx":hh*2+l},device_id_type=MESH)
    def cz(o,to,slot_): return pltpu.make_async_remote_copy(own.at[h,o],rz.at[slot_],s3.at[o],qz.at[slot_],device_id={"exp":to},device_id_type=MESH)
    step=min(512,W)
    def compute(n,dst):
        x,s=loads(n); b=lax.rem(n,2)
        for y in x: y.wait()
        @pl.when(n+1<2*M)
        def _():
            for y in loads(n+1)[0]: y.start()
        low=pick_of(slv[pl.ds(s,1),:],cap).astype(F32).astype(BF)
        def body(i):
            sl=pl.ds(pl.multiple_of(i*step,step),step)
            d=(nt(gb[b],wg[sl,:])+nt(ub[b],wu[sl,:])).astype(BF)
            dst[:,sl]=tn(low,d).astype(BF)
        loop(W//step,body)
    pltpu.sync_copy(slot,slv)
    for x in wl: x.wait()
    pl.semaphore_wait(bar,H+min(X,1)+(e>0).astype(jnp.int32)+(e<E-1).astype(jnp.int32))
    for i in range(X): ex(i).start()
    def zstep(k):
        o=order(k)
        for j in range(1,H):
            c2(j,o).wait_recv()
            add_into(own.at[h,o],r2.at[j-1,o])
        @pl.when(o>e)
        def _():
            @pl.when(e>0)
            def _():
                cz(o,e-1,o).wait_recv(); add_into(own.at[h,o],rz.at[o])
            cz(o,e+1,o).start()
        @pl.when(o<e)
        def _():
            @pl.when(e<E-1)
            def _():
                cz(o,e+1,o).wait_recv(); add_into(own.at[h,o],rz.at[o])
            cz(o,e-1,jnp.where(o==e-1,E,o)).start()
    def pair(m):
        hh,o=place(m)
        @pl.when(m>=NS)
        def _(): c1(m-NS).wait_send()
        compute(2*m,snd.at[lax.rem(m,NS)])
        c1(m).start()
        compute(2*m+1,own.at[hh,o])
        c1(m).wait_recv()
        add_into(own.at[hh,o],r1.at[hh,o])
        for j in range(1,H):
            @pl.when(m//E==j-1)
            def _(): c2(j,o).start()
        @pl.when(m//E==H-1)
        def _(): zstep(lax.rem(m,E))
    loop(M,pair)
    for m in range(max(0,M-NS),M): c1(m).wait_send()
    @pl.when(e>0)
    def _():
        cz(e,e-1,e).wait_recv(); add_into(own.at[h,e],rz.at[e])
    @pl.when(e<E-1)
    def _():
        cz(e,e+1,E).wait_recv(); add_into(own.at[h,e],rz.at[E])
    out=pltpu.make_async_copy(own.at[h,e],o_ref,o_sem); out.start()
    def drain(k):
        for j in range(1,H): c2(j,order(k)).wait_send()
        @pl.when(k<E-1)
        def _(): cz(order(k),e,order(k)).wait_send()
    loop(E,drain)
    out.wait()
    for i in range(X): ex(i).wait()


def back_call(slot,dgp,dup,gw,uw,swap,C,E,T,cids):
    S,cap,FF=dgp.shape; D=gw.shape[0]; H=C//2
    dma=pltpu.SemaphoreType.DMA; V=lambda *s: pltpu.VMEM(s,BF)
    blocks=2*H*E+(H-1)*E+E+4
    parts=1
    while 2*(blocks*T*D//parts+2*D//parts*FF+4*cap*FF)>60*2**20: parts*=2
    W=D//parts
    A=pl.BlockSpec(memory_space=pl.ANY)
    def part(i):
        a,b=(gw,uw) if parts==1 else (gw[i*W:(i+1)*W],uw[i*W:(i+1)*W])
        ex=tuple(swap) if i==0 else ()
        X=len(ex)
        return pl.pallas_call(functools.partial(back_kernel,H,E,cap,X),
            out_shape=[jax.ShapeDtypeStruct((T,W),BF)]+[jax.ShapeDtypeStruct((n,g.shape[1]),g.dtype) for g,n in ex],
            in_specs=[A]*(5+X),
            out_specs=[A]*(1+X),
            scratch_shapes=[V(H,E,T,W),V(H,E,T,W),V(H-1,E,T,W),V(E+1,T,W),V(3,T,W),V(2,cap,FF),V(2,cap,FF),pltpu.VMEM((S,T),jnp.int32),V(W,FF),V(W,FF),
                dma((2,2)),dma((2,)),dma((H*E,)),dma((H,E)),dma((H-1,E)),dma((H-1,E)),dma((E,)),dma((E+1,)),dma(())]+([dma((X,)),dma((X,))] if X else []),
            cost_estimate=pl.CostEstimate(flops=2*S*cap*(2*W*FF+T*W),bytes_accessed=S*4*cap*FF,transcendentals=0),
            compiler_params=pltpu.CompilerParams(collective_id=cids[i],has_side_effects=True,vmem_limit_bytes=61*2**20),
            name="back")(slot,dgp,dup,a,b,*[g for g,_ in ex])
    out=[part(i) for i in range(parts)]
    tok=out[0][0] if parts==1 else jnp.concatenate([o[0] for o in out],axis=1)
    return tok,out[0][1:]


def fwd_kernel(H,E,T,cap,in_vmem,slot,rows,cot,gw,uw,dw,recv,hid,dout,dgp,dup,moe_a,moe_b,dg,*scr):
    if in_vmem: allr=scr[0]; scr=scr[1:]; rb=None
    else: allr=scr[0]; rb=scr[1]; scr=scr[2:]
    (slv,wg,wu,wd,cb,srecv,shid,sdout,sdgp,sdup,smoe,sdg,cr,w_sem,c_sem,l_sem,o_sem,up_s,dn_s,up_r,dn_r,x_s,x_r,b_s,b_r)=scr
    c=lax.axis_index("ctx"); e=lax.axis_index("exp")
    h=c//2; l=c%2; C=2*H; S=C*E
    D=wg.shape[0]; FF=wg.shape[1]; EXT=allr.shape[1]
    expert=c*E+e
    def xpeer(j): return lax.rem(h+j,H)
    def idx(hh,ll,ee): return (hh*2+ll)*E+ee
    bar=pltpu.get_barrier_semaphore()
    pl.semaphore_signal(bar,inc=1,device_id={"ctx":h*2+1-l},device_id_type=MESH)
    for j in range(1,H):
        pl.semaphore_signal(bar,inc=1,device_id={"ctx":xpeer(j)*2+l},device_id_type=MESH)
    @pl.when(e>0)
    def _(): pl.semaphore_signal(bar,inc=1,device_id={"exp":e-1},device_id_type=MESH)
    @pl.when(e<E-1)
    def _(): pl.semaphore_signal(bar,inc=1,device_id={"exp":e+1},device_id_type=MESH)
    order=by_distance(e,E)
    def near(k): return order(E-1-k)
    own=idx(h,l,e)
    wl=[pltpu.make_async_copy(a,b,w_sem.at[i]) for i,(a,b) in enumerate(((gw,wg),(uw,wu),(dw,wd)))]
    first=pltpu.make_async_copy(rows,allr.at[own],w_sem.at[3])
    first.start()
    for x in wl: x.start()
    def job(n):
        m=jnp.maximum(n-2,0)
        r=jnp.where(n<2,0,1+m//(2*H)); t=jnp.where(n<2,n,lax.rem(m,2*H))
        t=jnp.where(r==E,t+2,t)
        j=t//2
        return r,t,j,lax.rem(t,2),jnp.where(j==0,r,r-1)
    def hi(j): return jnp.where(j==0,h,lax.rem(h+H-j,H))
    def sender(n):
        r,t,j,s,k=job(n)
        return idx(hi(j),jnp.where(s==1,1-l,l),near(k))
    def cload(n): return pltpu.make_async_copy(cot.at[sender(n)],cb.at[lax.rem(n,2)],c_sem.at[lax.rem(n,2)])
    cload(0).start()
    def rc(i,ss,rs,**kw): return pltpu.make_async_remote_copy(allr.at[i],allr.at[i],ss,rs,device_id=kw,device_id_type=MESH)
    def up(ee): return rc(idx(h,l,ee),up_s.at[ee],up_r.at[ee],exp=e+1)
    def dn(ee): return rc(idx(h,l,ee),dn_s.at[ee],dn_r.at[ee],exp=e-1)
    def xs(j,ee): return rc(idx(h,l,ee),x_s.at[j-1,ee],x_r.at[j-1,ee],ctx=xpeer(j)*2+l)
    def xr(j,ee):
        return rc(idx(hi(j),l,ee),x_s.at[j-1,ee],x_r.at[j-1,ee],ctx=hi(j)*2+l)
    def bs(j,ee): return rc(idx(hi(j),l,ee),b_s.at[j,ee],b_r.at[j,ee],ctx=h*2+1-l)
    def br(j,ee): return rc(idx(hi(j),1-l,ee),b_s.at[j,ee],b_r.at[j,ee],ctx=h*2+1-l)
    outs=[(srecv,recv),(shid,hid),(sdout,dout),(sdgp,dgp),(sdup,dup),(smoe.at[:,:,:D//2],moe_a),(smoe.at[:,:,D//2:],moe_b),(sdg,dg)]
    def odma(n):
        s=sender(n); b=lax.rem(n,2)
        return [pltpu.make_async_copy(a.at[b],o.at[s],o_sem.at[i,b]) for i,(a,o) in enumerate(outs)]
    def compute(n):
        s=sender(n); b=lax.rem(n,2)
        if in_vmem: rw=allr.at[s]
        else:
            cp=pltpu.make_async_copy(allr.at[s],rb,l_sem); cp.start(); cp.wait(); rw=rb
        cload(n).wait()
        @pl.when(n+1<S)
        def _(): cload(n+1).start()
        @pl.when(n>=2)
        def _():
            for x in odma(n-2): x.wait()
        ct=cb.at[b]
        pk=pick_of(slv[pl.ds(s,1),:],cap); pf=pk.astype(F32); low=pf.astype(BF)
        gm=rw[T:EXT,:T].astype(F32)
        g=jnp.sum(jnp.where(lax.broadcasted_iota(jnp.int32,gm.shape,0)==expert,gm,0.0),axis=0,keepdims=True)
        gsel=jnp.where(pk,jnp.broadcast_to(g,(cap,T)),0.0)
        grow=jnp.sum(gsel,axis=1,keepdims=True)
        comb=gsel.astype(BF)
        step=512
        for m in range(0,D,step):
            srecv[b,:,m:m+step]=nn(low,rw[:T,m:m+step]).astype(BF)
            q=nn(low,ct[:,m:m+step])
            sdout[b,:,m:m+step]=(q*grow).astype(BF)
            cr[:,m:m+step]=q.astype(BF)
        half=FF//2
        for m in range(0,FF,half):
            gp=nn(srecv[b],wg[:,m:m+half]); upp=nn(srecv[b],wu[:,m:m+half])
            dh=nt(sdout[b],wd[m:m+half,:])
            sg=jax.nn.sigmoid(gp); si=gp*sg
            shid[b,:,m:m+half]=(si*upp).astype(BF)
            sdgp[b,:,m:m+half]=(dh*upp*sg*(1.0+gp*(1.0-sg))).astype(BF)
            sdup[b,:,m:m+half]=(dh*si).astype(BF)
        acc=jnp.zeros((cap,1),F32)
        for m in range(0,D,step):
            ev=nn(shid[b],wd[:,m:m+step]).astype(BF)
            acc=acc+jnp.sum(cr[:,m:m+step].astype(F32)*ev.astype(F32),axis=1,keepdims=True)
            smoe[b,:,m:m+step]=tn(comb,ev).astype(BF)
        sdg[b]=jnp.sum(pf*acc,axis=0,keepdims=True)
        for x in odma(n): x.start()
    pltpu.sync_copy(slot,slv)
    first.wait()
    pl.semaphore_wait(bar,H+(e>0).astype(jnp.int32)+(e<E-1).astype(jnp.int32))
    @pl.when(e<E-1)
    def _(): up(e).start()
    @pl.when(e>0)
    def _(): dn(e).start()
    for j in range(1,H): xs(j,e).start()
    bs(0,e).start()
    for x in wl: x.wait()
    def step_(n):
        r,t,j,sib_,k=job(n)
        @pl.when(jnp.logical_and(t==0,r>0))
        def _():
            @pl.when(e>=r)
            def _():
                up(e-r).wait_recv()
                @pl.when(e<E-1)
                def _(): up(e-r).start()
                for q in range(1,H): xs(q,e-r).start()
                bs(0,e-r).start()
            @pl.when(e+r<E)
            def _():
                dn(e+r).wait_recv()
                @pl.when(e>0)
                def _(): dn(e+r).start()
                for q in range(1,H): xs(q,e+r).start()
                bs(0,e+r).start()
        @pl.when(jnp.logical_and(sib_==0,j>0))
        def _():
            xr(j,near(k)).wait_recv(); bs(j,near(k)).start()
        @pl.when(sib_==1)
        def _(): br(j,near(k)).wait_recv()
        compute(n)
    loop(S,step_)
    for x in odma(S-2)+odma(S-1): x.wait()
    def drain(ee):
        @pl.when(jnp.logical_and(e<E-1,ee<=e))
        def _(): up(ee).wait_send()
        @pl.when(jnp.logical_and(e>0,ee>=e))
        def _(): dn(ee).wait_send()
        for j in range(1,H): xs(j,ee).wait_send()
        for j in range(H): bs(j,ee).wait_send()
    loop(E,drain)


def fwd_call(slot,rows,cot,gw,uw,dw,cap,C,E,T,cid=4):
    EXT,D=rows.shape; S=C*E; H=C//2; FF=gw.shape[1]
    dma=pltpu.SemaphoreType.DMA; V=lambda *s: pltpu.VMEM(s,BF)
    in_vmem=S*EXT*D*2<=28*2**20
    A=pl.BlockSpec(memory_space=pl.ANY)
    sd=lambda a,b,dt=BF: jax.ShapeDtypeStruct((S,a,b),dt)
    out_shape=[sd(cap,D),sd(cap,FF),sd(cap,D),sd(cap,FF),sd(cap,FF),sd(T,D//2),sd(T,D//2),sd(1,T,F32)]
    land=[V(S,EXT,D)] if in_vmem else [V(EXT,D)]
    if not in_vmem: out_shape=out_shape+[sd(EXT,D)]
    body=functools.partial(fwd_kernel,H,E,T,cap,in_vmem)
    r=pl.pallas_call(body,out_shape=out_shape,in_specs=[A]*6,out_specs=[A]*len(out_shape),
        scratch_shapes=land+[pltpu.VMEM((S,T),jnp.int32),V(D,FF),V(D,FF),V(FF,D),V(2,T,D),V(2,cap,D),V(2,cap,FF),V(2,cap,D),V(2,cap,FF),V(2,cap,FF),V(2,T,D),pltpu.VMEM((2,1,T),F32),V(cap,D),
            dma((4,)),dma((2,)),dma(()),dma((8,2)),dma((E,)),dma((E,)),dma((E,)),dma((E,)),dma((H-1,E)),dma((H-1,E)),dma((H,E)),dma((H,E))],
        cost_estimate=pl.CostEstimate(flops=2*S*cap*(4*D*FF+3*T*D),bytes_accessed=S*2*(T*D+2*cap*D+3*cap*FF+T*D)+6*D*FF,transcendentals=S*cap*FF),
        compiler_params=pltpu.CompilerParams(collective_id=cid,has_side_effects=True,vmem_limit_bytes=61*2**20),name="experts_fwd")(slot,rows,cot,gw,uw,dw)
    return r[:8]


def mask_bias(lab_r,lab_c,i0,bq,K):
    lr=lab_r[:,:K]; lc=lab_c
    row=lax.broadcasted_iota(jnp.int32,(bq,K),0)+i0; col=lax.broadcasted_iota(jnp.int32,(bq,K),1)
    ok=(col<=row)&((lr==0)|(lr==lc))
    return jnp.where(ok,0.0,-1e30).astype(F32)

def eye_mask():
    return lax.broadcasted_iota(jnp.int32,(HEAD,HEAD),0)==lax.broadcasted_iota(jnp.int32,(HEAD,HEAD),1)

def to_row(col):
    return jnp.sum(jnp.where(eye_mask(),jnp.broadcast_to(col,(HEAD,HEAD)),0.0),axis=0,keepdims=True)

def to_col(row):
    return jnp.sum(jnp.where(eye_mask(),jnp.broadcast_to(row,(HEAD,HEAD)),0.0),axis=1,keepdims=True)

def greet_ctx(C):
    c=lax.axis_index("ctx"); bar=pltpu.get_barrier_semaphore()
    for j in range(1,C): pl.semaphore_signal(bar,inc=1,device_id={"ctx":lax.rem(c+j,C)},device_id_type=MESH)

def sum_ctx(C,buf,ss,rs,others=0):
    c=lax.axis_index("ctx")
    pl.semaphore_wait(pltpu.get_barrier_semaphore(),C-1+others)
    def cp(j): return pltpu.make_async_remote_copy(buf.at[c],buf.at[c],ss.at[j-1],rs.at[j-1],device_id={"ctx":lax.rem(c+j,C)},device_id_type=MESH)
    for j in range(1,C): cp(j).start()
    for j in range(1,C):
        q=lax.rem(c+C-j,C)
        pltpu.make_async_remote_copy(buf.at[q],buf.at[q],ss.at[j-1],rs.at[j-1],device_id={"ctx":q},device_id_type=MESH).wait_recv()
    acc=buf[0]
    for j in range(1,C): acc=acc+buf[j]
    for j in range(1,C): cp(j).wait_send()
    return acc

class Rows:
    def __init__(self,N,E,x,o,ls,us,ur,ds_,dr_,ys,yr):
        self.N,self.E,self.x,self.o=N,E,x,o
        self.ls,self.us,self.ur,self.ds,self.dr,self.ys,self.yr=ls,us,ur,ds_,dr_,ys,yr
        self.p=lax.axis_index("dp"); self.e=lax.axis_index("exp")
        self.peers=(N-1)+(self.e>0).astype(jnp.int32)+(self.e<E-1).astype(jnp.int32)
    def greet(self):
        bar=pltpu.get_barrier_semaphore()
        def sig(**kw): pl.semaphore_signal(bar,inc=1,device_id=kw,device_id_type=MESH)
        for j in range(1,self.N): sig(dp=lax.rem(self.p+j,self.N))
        @pl.when(self.e>0)
        def _(): sig(exp=self.e-1)
        @pl.when(self.e<self.E-1)
        def _(): sig(exp=self.e+1)
        self.local=pltpu.make_async_copy(self.x,self.o.at[self.p,self.e],self.ls)
        self.local.start()
    def rc(self,q,ee,s,r,**kw): return pltpu.make_async_remote_copy(self.o.at[q,ee],self.o.at[q,ee],s,r,device_id=kw,device_id_type=MESH)
    def up(self,ee): return self.rc(self.p,ee,self.us.at[ee],self.ur.at[ee],exp=self.e+1)
    def dn(self,ee): return self.rc(self.p,ee,self.ds.at[ee],self.dr.at[ee],exp=self.e-1)
    def across(self,j,ee): return self.rc(self.p,ee,self.ys.at[j-1,ee],self.yr.at[j-1,ee],dp=lax.rem(self.p+j,self.N))
    def came(self,j,ee):
        q=lax.rem(self.p+self.N-j,self.N)
        return self.rc(q,ee,self.ys.at[j-1,ee],self.yr.at[j-1,ee],dp=q)
    def begin(self):
        e,E=self.e,self.E
        self.local.wait()
        for j in range(1,self.N): self.across(j,e).start()
        @pl.when(e<E-1)
        def _(): self.up(e).start()
        @pl.when(e>0)
        def _(): self.dn(e).start()
    def round(self,r):
        e,E=self.e,self.E
        @pl.when(e>=r)
        def _():
            self.up(e-r).wait_recv()
            @pl.when(e<E-1)
            def _(): self.up(e-r).start()
            for j in range(1,self.N): self.across(j,e-r).start()
        @pl.when(e+r<E)
        def _():
            self.dn(e+r).wait_recv()
            @pl.when(e>0)
            def _(): self.dn(e+r).start()
            for j in range(1,self.N): self.across(j,e+r).start()
    def finish(self):
        e,E=self.e,self.E
        def one(ee):
            for j in range(1,self.N):
                self.came(j,ee).wait_recv(); self.across(j,ee).wait_send()
            @pl.when(jnp.logical_and(e<E-1,ee<=e))
            def _(): self.up(ee).wait_send()
            @pl.when(jnp.logical_and(e>0,ee>=e))
            def _(): self.dn(ee).wait_send()
        loop(E,one)


def attn_fwd_kernel(N,C,E,heads,bq,scale,raw,cos,sin,lab_r,lab_c,gains,wo,qo,ko,vo,mix,inv,ow,bias,buf,ss,rs,*gs):
    G=raw.shape[0]; cols=heads*HEAD; nb=G//HEAD
    c=lax.axis_index("ctx")
    greet_ctx(C)
    rows_w=Rows(N,E,wo,ow,*gs)
    rows_w.greet()
    def squares(i):
        sl=pl.ds(pl.multiple_of(i*HEAD,HEAD),HEAD)
        for t in range(2):
            v=raw[sl,t*cols:(t+1)*cols]
            buf[c,pl.ds(t*nb+i,1),:]=to_row(jnp.sum(v*v,axis=1,keepdims=True))
        vo[sl,:]=raw[sl,2*cols:].astype(BF)
    loop(nb,squares)
    inv[...]=lax.rsqrt(sum_ctx(C,buf,ss,rs,rows_w.peers)/(C*cols)+EPS)
    rows_w.begin()
    def prep(i):
        sl=pl.ds(pl.multiple_of(i*HEAD,HEAD),HEAD)
        cs,sn=cos[sl,:],sin[sl,:]
        for t,o in ((0,qo),(1,ko)):
            r=to_col(inv[pl.ds(t*nb+i,1),:])
            for hd in range(heads):
                a=hd*HEAD
                v=raw[sl,t*cols+a:t*cols+a+HEAD]*r*gains[t:t+1,a:a+HEAD]
                o[sl,a:a+HEAD]=(v*cs+pltpu.roll(v,HEAD//2,1)*sn).astype(BF)
    loop(nb,prep)
    def block(i,K):
        rows=pl.ds(pl.multiple_of(i*bq,bq),bq)
        bias[:,:K]=mask_bias(lab_r,lab_c[rows,:],i*bq,bq,K)
        def head(hd):
            ln=pl.ds(pl.multiple_of(hd*HEAD,HEAD),HEAD)
            s=nt(qo[rows,ln],ko[:K,ln])*scale+bias[:,:K]
            p=jnp.exp(s-jnp.max(s,axis=1,keepdims=True))
            pr=(p*(1.0/jnp.sum(p,axis=1,keepdims=True))).astype(BF)
            mix[rows,ln]=nn(pr,vo[:K,ln]).astype(BF)
        loop(heads,head)
    per=G//bq//3
    for g in range(3):
        loop(per,lambda i,g=g: block(i+g*per,(g+1)*per*bq))
        if g+1<E: rows_w.round(g+1)
    for r in range(4,E): rows_w.round(r)
    rows_w.finish()

def attn_fwd(raw,cos,sin,lab_r,lab_c,gains,wo,N,C,E,heads,cid,bq=256):
    G=raw.shape[0]; cols=heads*HEAD; R=2*G//HEAD; dma=pltpu.SemaphoreType.DMA
    o=jax.ShapeDtypeStruct((G,cols),BF)
    V=pl.BlockSpec(memory_space=pltpu.VMEM); A=pl.BlockSpec(memory_space=pl.ANY)
    return pl.pallas_call(functools.partial(attn_fwd_kernel,N,C,E,heads,bq,HEAD**-0.5),out_shape=[o]*4+[jax.ShapeDtypeStruct((R,HEAD),F32),jax.ShapeDtypeStruct((N,E)+wo.shape,BF)],in_specs=[V]*6+[A],out_specs=[V]*5+[A],
        scratch_shapes=[pltpu.VMEM((bq,G),F32),pltpu.VMEM((C,R,HEAD),F32),dma((C-1,)),dma((C-1,)),dma(()),dma((E,)),dma((E,)),dma((E,)),dma((E,)),dma((N-1,E)),dma((N-1,E))],
        cost_estimate=pl.CostEstimate(flops=2*2*heads*G*G*HEAD,bytes_accessed=G*cols*20,transcendentals=heads*G*G),
        compiler_params=pltpu.CompilerParams(collective_id=cid,has_side_effects=True,vmem_limit_bytes=48*2**20),name="attn_fwd")(raw,cos,sin,lab_r,lab_c,gains,wo)

def attn_bwd_kernel(C,heads,bq,scale,q,k,v,dm,raw,inv,cos,sin,lab_r,lab_c,gains,draw,gsum,bias,aq,ak,av,buf,ss,rs):
    G=q.shape[0]; cols=heads*HEAD; nb=G//HEAD
    c=lax.axis_index("ctx")
    greet_ctx(C)
    ak[...]=jnp.zeros_like(ak); av[...]=jnp.zeros_like(av)
    def block(i,K):
        rows=pl.ds(pl.multiple_of(i*bq,bq),bq)
        bias[:,:K]=mask_bias(lab_r,lab_c[rows,:],i*bq,bq,K)
        def head(hd):
            ln=pl.ds(pl.multiple_of(hd*HEAD,HEAD),HEAD)
            qb=q[rows,ln]; kb=k[:K,ln]; db=dm[rows,ln]
            s=nt(qb,kb)*scale+bias[:,:K]
            p=jnp.exp(s-jnp.max(s,axis=1,keepdims=True))
            p=p*(1.0/jnp.sum(p,axis=1,keepdims=True))
            dp=nt(db,v[:K,ln])
            ds=(p*(dp-jnp.sum(p*dp,axis=1,keepdims=True))).astype(BF)
            aq[rows,ln]=nn(ds,kb)
            ak[:K,ln]+=tn(ds,qb)
            av[:K,ln]+=tn(p.astype(BF),db)
        loop(heads,head)
    per=G//bq//3
    for g in range(3):
        loop(per,lambda i,g=g: block(i+g*per,(g+1)*per*bq))
    gsum[...]=jnp.zeros_like(gsum)
    def unrope(i):
        sl=pl.ds(pl.multiple_of(i*HEAD,HEAD),HEAD)
        for t,a in ((0,aq),(1,ak)):
            r=to_col(inv[pl.ds(t*nb+i,1),:])
            dot=jnp.zeros((HEAD,1),F32)
            for hd in range(heads):
                b=hd*HEAD
                g=a[sl,b:b+HEAD]*scale
                g=g*cos[sl,:]-pltpu.roll(g,HEAD//2,1)*sin[sl,:]
                x=raw[sl,t*cols+b:t*cols+b+HEAD]
                gsum[t:t+1,b:b+HEAD]+=jnp.sum(g*x*r,axis=0,keepdims=True)
                g=g*gains[t:t+1,b:b+HEAD]
                a[sl,b:b+HEAD]=g
                dot=dot+jnp.sum(g*x,axis=1,keepdims=True)
            buf[c,pl.ds(t*nb+i,1),:]=to_row(dot)
        draw[sl,2*cols:]=av[sl,:].astype(BF)
    loop(nb,unrope)
    buf[0]=sum_ctx(C,buf,ss,rs)/(C*cols)
    def fin(i):
        sl=pl.ds(pl.multiple_of(i*HEAD,HEAD),HEAD)
        for t,a in ((0,aq),(1,ak)):
            r=to_col(inv[pl.ds(t*nb+i,1),:]); dot=to_col(buf[0,pl.ds(t*nb+i,1),:])
            m=r*r*r*dot
            draw[sl,t*cols:(t+1)*cols]=(a[sl,:]*r-raw[sl,t*cols:(t+1)*cols]*m).astype(BF)
    loop(nb,fin)

def attn_bwd(q,k,v,dm,raw,inv,cos,sin,lab_r,lab_c,gains,C,heads,cid,bq=256):
    G,cols=q.shape; R=2*G//HEAD; dma=pltpu.SemaphoreType.DMA
    V=pl.BlockSpec(memory_space=pltpu.VMEM)
    acc=pltpu.VMEM((G,cols),F32)
    return pl.pallas_call(functools.partial(attn_bwd_kernel,C,heads,bq,HEAD**-0.5),out_shape=[jax.ShapeDtypeStruct((G,3*cols),BF),jax.ShapeDtypeStruct((2,cols),F32)],in_specs=[V]*11,out_specs=[V]*2,
        scratch_shapes=[pltpu.VMEM((bq,G),F32),acc,acc,acc,pltpu.VMEM((C,R,HEAD),F32),dma((C-1,)),dma((C-1,))],
        cost_estimate=pl.CostEstimate(flops=5*2*heads*G*G*HEAD,bytes_accessed=G*cols*20,transcendentals=heads*G*G),
        compiler_params=pltpu.CompilerParams(collective_id=cid,has_side_effects=True,vmem_limit_bytes=56*2**20),name="attn_bwd")(q,k,v,dm,raw,inv,cos,sin,lab_r,lab_c,gains)

def ctx_barrier(H,c,h,l):
    bar=pltpu.get_barrier_semaphore()
    pl.semaphore_signal(bar,inc=1,device_id={"ctx":h*2+1-l},device_id_type=MESH)
    for j in range(1,H):
        pl.semaphore_signal(bar,inc=1,device_id={"ctx":lax.rem(h+j,H)*2+l},device_id_type=MESH)
    pl.semaphore_wait(bar,H)

def ag_ctx_kernel(H,Q,x,o,xs,xr,bs,br,lsem):
    c=lax.axis_index("ctx"); h=c//2; l=c%2
    T=x.shape[0]; R=T//Q
    loc=pltpu.make_async_copy(x,o.at[c],lsem); loc.start()
    ctx_barrier(H,c,h,l)
    sib=h*2+1-l
    def sl(q): return pl.ds(q*R,R)
    def rc(a,b,s,r,to): return pltpu.make_async_remote_copy(a,b,s,r,device_id={"ctx":to},device_id_type=MESH)
    def xc(j,q): return rc(x.at[sl(q)],o.at[c,sl(q)],xs.at[j-1,q],xr.at[j-1,q],lax.rem(h+j,H)*2+l)
    def xw(j,q):
        p=lax.rem(h+H-j,H)*2+l; return rc(x.at[sl(q)],o.at[p,sl(q)],xs.at[j-1,q],xr.at[j-1,q],p)
    def bc(j,q):
        p=c if j==0 else lax.rem(h+H-j,H)*2+l
        src=x if j==0 else o.at[p]
        return rc(src.at[sl(q)],o.at[p,sl(q)],bs.at[j,q],br.at[j,q],sib)
    def bw(j,q):
        p=sib if j==0 else lax.rem(h+H-j,H)*2+1-l
        return rc(x.at[sl(q)],o.at[p,sl(q)],bs.at[j,q],br.at[j,q],sib)
    for q in range(Q):
        for j in range(1,H): xc(j,q).start()
    for q in range(Q): bc(0,q).start()
    for q in range(Q):
        for j in range(1,H):
            xw(j,q).wait_recv(); bc(j,q).start()
    for j in range(H):
        for q in range(Q):
            bw(j,q).wait_recv(); bc(j,q).wait_send()
            if j>0: xc(j,q).wait_send()
    loc.wait()

def ag_ctx(x,C,cid,Q=4):
    T,D=x.shape; H=C//2; dma=pltpu.SemaphoreType.DMA
    A=pl.BlockSpec(memory_space=pl.ANY)
    return pl.pallas_call(functools.partial(ag_ctx_kernel,H,Q),out_shape=jax.ShapeDtypeStruct((C,T,D),x.dtype),in_specs=[A],out_specs=A,
        scratch_shapes=[dma((H-1,Q)),dma((H-1,Q)),dma((H,Q)),dma((H,Q)),dma(())],
        compiler_params=pltpu.CompilerParams(collective_id=cid,has_side_effects=True),name="ag_ctx")(x)

def rs_ctx_kernel(H,Q,x,o,own,r1,r2,ld,s1,q1,s2,q2,osem):
    c=lax.axis_index("ctx"); h=c//2; l=c%2
    T=own.shape[1]; R=T//Q
    def sl(q): return pl.ds(q*R,R)
    hs=[lax.rem(h+j,H) for j in range(1,H)]+[h]
    def load(i): return pltpu.make_async_copy(x.at[hs[i]*2+l],own.at[hs[i]],ld.at[i])
    for i in range(H): load(i).start()
    ctx_barrier(H,c,h,l)
    def c1(i,q): return pltpu.make_async_remote_copy(x.at[hs[i]*2+1-l,sl(q)],r1.at[hs[i],sl(q)],s1.at[hs[i],q],q1.at[hs[i],q],device_id={"ctx":h*2+1-l},device_id_type=MESH)
    def c2(j,q): return pltpu.make_async_remote_copy(own.at[hs[j-1],sl(q)],r2.at[j-1,sl(q)],s2.at[j-1,q],q2.at[j-1,q],device_id={"ctx":hs[j-1]*2+l},device_id_type=MESH)
    for i in range(H):
        for q in range(Q): c1(i,q).start()
    for i in range(H):
        load(i).wait()
        for q in range(Q):
            c1(i,q).wait_recv()
            add_into(own.at[hs[i],sl(q)],r1.at[hs[i],sl(q)])
            if i<H-1: c2(i+1,q).start()
    for q in range(Q):
        for j in range(1,H):
            c2(j,q).wait_recv()
            add_into(own.at[h,sl(q)],r2.at[j-1,sl(q)])
    out=pltpu.make_async_copy(own.at[h],o,osem); out.start()
    for q in range(Q):
        for i in range(H): c1(i,q).wait_send()
        for j in range(1,H): c2(j,q).wait_send()
    out.wait()

def rs_ctx(x,cid,Q=4):
    C,T,D=x.shape; H=C//2; dma=pltpu.SemaphoreType.DMA
    A=pl.BlockSpec(memory_space=pl.ANY)
    return pl.pallas_call(functools.partial(rs_ctx_kernel,H,Q),out_shape=jax.ShapeDtypeStruct((T,D),x.dtype),in_specs=[A],out_specs=A,
        scratch_shapes=[pltpu.VMEM((H,T,D),BF),pltpu.VMEM((H,T,D),BF),pltpu.VMEM((H-1,T,D),BF),dma((H,)),dma((H,Q)),dma((H,Q)),dma((H-1,Q)),dma((H-1,Q)),dma(())],
        compiler_params=pltpu.CompilerParams(collective_id=cid,has_side_effects=True,vmem_limit_bytes=40*2**20),name="rs_ctx")(x)


def front_kernel(N,C,E,Q,wq,wk,wv,nx,qkv,na,a_s,a_r,up_s,up_r,dn_s,dn_r,y_s,y_r,xs_,xr_,bs_,br_,lsem):
    p=lax.axis_index("dp"); c=lax.axis_index("ctx"); e=lax.axis_index("exp")
    H=C//2; h=c//2; l=c%2; sib=h*2+1-l
    D=wq.shape[1]; cols=D//C; piece=cols//N; T=nx.shape[0]; R=T//Q
    def dpeer(j): return lax.rem(p+j,N)
    def cpeer(j): return lax.rem(c+j,C)
    bar=pltpu.get_barrier_semaphore()
    def sig(**kw): pl.semaphore_signal(bar,inc=1,device_id=kw,device_id_type=MESH)
    for j in range(1,N): sig(dp=dpeer(j))
    for j in range(1,C): sig(ctx=cpeer(j))
    @pl.when(e>0)
    def _(): sig(exp=e-1)
    @pl.when(e<E-1)
    def _(): sig(exp=e+1)
    def rc(a,b,s,r,**kw): return pltpu.make_async_remote_copy(a,b,s,r,device_id=kw,device_id_type=MESH)
    W=(wq,wk,wv)
    def src(t,d,q): return W[t].at[:,pl.ds(pl.multiple_of(d*(D//N)+q*piece,128),piece)]
    def dst(t,d,q): return qkv.at[p,q,e,:,pl.ds(t*cols+d*piece,piece)]
    TD=[(t,d) for t in range(3) for d in range(N)]
    local=[pltpu.make_async_copy(src(t,d,c),dst(t,d,c),lsem.at[i]) for i,(t,d) in enumerate(TD)]
    local_n=pltpu.make_async_copy(nx,na.at[c],lsem.at[len(TD)+1])
    for x in local+[local_n]: x.start()
    def away(j,i):
        t,d=TD[i]; q=cpeer(j)
        return rc(src(t,d,q),dst(t,d,c),a_s.at[j-1,i],a_r.at[j-1,i],ctx=q)
    def home(j,i):
        t,d=TD[i]; q=lax.rem(c+C-j,C)
        return rc(src(t,d,q),dst(t,d,q),a_s.at[j-1,i],a_r.at[j-1,i],ctx=q)
    def both(q,ee): return ((0,qkv.at[q,:,ee]),)
    def up(i,ee): b=both(p,ee)[i][1]; return rc(b,b,up_s.at[i,ee],up_r.at[i,ee],exp=e+1)
    def dn(i,ee): b=both(p,ee)[i][1]; return rc(b,b,dn_s.at[i,ee],dn_r.at[i,ee],exp=e-1)
    def ys(i,j,ee): b=both(p,ee)[i][1]; return rc(b,b,y_s.at[i,j-1,ee],y_r.at[i,j-1,ee],dp=dpeer(j))
    def yr(i,j,ee): q=lax.rem(p+N-j,N); b=both(q,ee)[i][1]; return rc(b,b,y_s.at[i,j-1,ee],y_r.at[i,j-1,ee],dp=q)
    def sl(q): return pl.ds(q*R,R)
    def xc(j,q): return rc(nx.at[sl(q)],na.at[c,sl(q)],xs_.at[j-1,q],xr_.at[j-1,q],ctx=lax.rem(h+j,H)*2+l)
    def xw(j,q):
        s=lax.rem(h+H-j,H)*2+l; return rc(nx.at[sl(q)],na.at[s,sl(q)],xs_.at[j-1,q],xr_.at[j-1,q],ctx=s)
    def bc(j,q):
        s=c if j==0 else lax.rem(h+H-j,H)*2+l
        a=nx if j==0 else na.at[s]
        return rc(a.at[sl(q)],na.at[s,sl(q)],bs_.at[j,q],br_.at[j,q],ctx=sib)
    def bw(j,q):
        s=sib if j==0 else lax.rem(h+H-j,H)*2+1-l
        return rc(nx.at[sl(q)],na.at[s,sl(q)],bs_.at[j,q],br_.at[j,q],ctx=sib)
    pl.semaphore_wait(bar,(N-1)+(C-1)+(e>0).astype(jnp.int32)+(e<E-1).astype(jnp.int32))
    for j in range(1,C):
        for i in range(len(TD)): away(j,i).start()
    for q in range(Q):
        for j in range(1,H): xc(j,q).start()
    for q in range(Q): bc(0,q).start()
    for x in local: x.wait()
    for j in range(1,C):
        for i in range(len(TD)): home(j,i).wait_recv()
    for i in range(1):
        for j in range(1,N): ys(i,j,e).start()
        @pl.when(e<E-1)
        def _(): up(i,e).start()
        @pl.when(e>0)
        def _(): dn(i,e).start()
    def rounds(r0):
        r=r0+1
        for i in range(1):
            @pl.when(e>=r)
            def _():
                up(i,e-r).wait_recv()
                @pl.when(e<E-1)
                def _(): up(i,e-r).start()
                for j in range(1,N): ys(i,j,e-r).start()
            @pl.when(e+r<E)
            def _():
                dn(i,e+r).wait_recv()
                @pl.when(e>0)
                def _(): dn(i,e+r).start()
                for j in range(1,N): ys(i,j,e+r).start()
        @pl.when(r0==0)
        def _():
            for q in range(Q):
                for j in range(1,H):
                    xw(j,q).wait_recv(); bc(j,q).start()
    loop(E-1,rounds)
    def finish(ee):
        for i in range(1):
            for j in range(1,N):
                yr(i,j,ee).wait_recv(); ys(i,j,ee).wait_send()
            @pl.when(jnp.logical_and(e<E-1,ee<=e))
            def _(): up(i,ee).wait_send()
            @pl.when(jnp.logical_and(e>0,ee>=e))
            def _(): dn(i,ee).wait_send()
    loop(E,finish)
    for j in range(1,C):
        for i in range(len(TD)): away(j,i).wait_send()
    for q in range(Q):
        for j in range(1,H): xc(j,q).wait_send()
        for j in range(H):
            bc(j,q).wait_send(); bw(j,q).wait_recv()
    local_n.wait()


def front(wq,wk,wv,nx,N,C,E,cid,Q=2):
    S,D=wq.shape; T=nx.shape[0]; H=C//2; dma=pltpu.SemaphoreType.DMA
    A=pl.BlockSpec(memory_space=pl.ANY)
    return pl.pallas_call(functools.partial(front_kernel,N,C,E,Q),
        out_shape=[jax.ShapeDtypeStruct((N,C,E,S,3*D//C),BF),jax.ShapeDtypeStruct((C,T,D),BF)],
        in_specs=[A]*4,out_specs=[A]*2,
        scratch_shapes=[dma((C-1,3*N)),dma((C-1,3*N)),dma((2,E)),dma((2,E)),dma((2,E)),dma((2,E)),dma((2,N-1,E)),dma((2,N-1,E)),dma((H-1,Q)),dma((H-1,Q)),dma((H,Q)),dma((H,Q)),dma((3*N+2,))],
        compiler_params=pltpu.CompilerParams(collective_id=cid,has_side_effects=True),name="front")(wq,wk,wv,nx)


def dot_nn(a, b):
    return lax.dot_general(a, b, (((1,), (0,)), ((), ())), preferred_element_type=F32)


def dot_tn(a, b):
    return lax.dot_general(a, b, (((0,), (0,)), ((), ())), preferred_element_type=F32)


def dot_nt(a, b):
    return lax.dot_general(a, b, (((1,), (1,)), ((), ())), preferred_element_type=F32)


def low_dp(grad, n_dp):
    low = grad.astype(BF)
    if n_dp != 2:
        return (lax.psum(low, "dp"),)
    return low, lax.ppermute(low, "dp", [(0, 1), (1, 0)])


def per_device(
    hidden_in,
    segments,
    routes,
    attn_gain,
    query_weight,
    key_weight,
    value_weight,
    query_gain,
    key_gain,
    output_weight,
    ffn_gain,
    router_weight,
    gate_weight,
    up_weight,
    down_weight,
    cotangent,
):
    n_dp, n_ctx, n_exp = (lax.axis_size(a) for a in ALL)
    tok, width = hidden_in.shape[2:]
    topk = routes.shape[3]
    experts = n_ctx * n_exp
    cap = (5 * tok * topk + 4 * experts - 1) // (4 * experts)
    cap = -(-cap // 16) * 16
    group = segments.shape[2]
    shard = query_weight.shape[0]
    cols = width // n_ctx
    piece = cols // n_dp
    heads = cols // HEAD
    ctx_me = lax.axis_index("ctx")
    exp_me = lax.axis_index("exp")
    expert_me = ctx_me * n_exp + exp_me

    def own_cols(vec):
        return lax.dynamic_index_in_dim(
            vec.reshape(n_dp, n_ctx, piece), ctx_me, 1, keepdims=False
        ).reshape(cols)

    own_routes = routes[0, 0]
    expert_ids = jnp.arange(experts, dtype=jnp.int32)
    hits = jnp.sum((own_routes[:, :, None] == expert_ids).astype(jnp.int32), axis=1)
    tokens = jnp.arange(tok, dtype=jnp.int32)
    lower = (tokens[:, None] > tokens[None, :]).astype(BF)
    earlier = dot_nn(lower, hits.astype(BF)).astype(jnp.int32)
    slot_local = jnp.where(hits > 0, earlier, -1).T
    slot = lax.all_to_all(slot_local, MOE, split_axis=0, concat_axis=0, tiled=True)
    slot = slot.reshape(experts, tok)
    cot = cotangent[0, 0]

    hidden = hidden_in[0, 0].astype(F32)
    labels = segments[0, 0]
    index = jnp.arange(group, dtype=jnp.int32)
    before = jnp.sum((labels[None, :] < labels[:, None]).astype(jnp.int32), axis=1)
    positions = index - before + jnp.where(labels > 0, PROMPT, 0).astype(jnp.int32)
    half = HEAD // 2
    frequency = THETA ** (-(jnp.arange(half, dtype=F32) * 2.0 / HEAD))
    angles = positions.astype(F32)[:, None] * frequency[None, :]
    cos, sin = jnp.cos(angles), jnp.sin(angles)
    cos = jnp.concatenate([cos, cos], axis=1)
    sin = jnp.concatenate([-sin, sin], axis=1)
    label_row, label_col = labels[None, :], labels[:, None]
    attn_gain_f = attn_gain.astype(F32)
    ffn_gain_f = ffn_gain.astype(F32)
    q_gain = own_cols(query_gain.astype(F32))
    k_gain = own_cols(key_gain.astype(F32))

    attn_r = lax.rsqrt(jnp.mean(hidden * hidden, axis=-1, keepdims=True) + EPS)
    normed = (hidden * attn_r * attn_gain_f).astype(BF)
    qkv_w, normed_g = front(query_weight, key_weight, value_weight, normed, n_dp, n_ctx, n_exp, 5)
    qkv_w = qkv_w.reshape(width, 3 * cols)
    normed_g = normed_g.reshape(group, width)
    cot, normed_g = lax.optimization_barrier((cot, normed_g))
    cot_all = lax.all_gather(cot, MOE, axis=0, tiled=False)
    raw = dot_nn(normed_g, qkv_w)
    gains = jnp.stack([q_gain, k_gain])
    q_rot, k_rot, v_low, mix, inv, out_w = attn_fwd(
        raw, cos, sin, label_row, label_col, gains, output_weight, n_dp, n_ctx, n_exp, heads, 9
    )
    out_w = out_w.reshape(cols, width)
    branch = rs_ctx(dot_nn(mix, out_w).astype(BF).reshape(n_ctx, tok, width), 6)
    residual = hidden + branch.astype(F32)

    ffn_r = lax.rsqrt(jnp.mean(residual * residual, axis=-1, keepdims=True) + EPS)
    ffn_normed = (residual * ffn_r * ffn_gain_f).astype(BF)
    logits = dot_nn(ffn_normed, router_weight)
    router_prob = jax.nn.softmax(logits, axis=-1)
    gates = jnp.where(hits > 0, router_prob, 0.0).astype(BF)
    padded = jnp.zeros((experts, width), BF).at[:, :tok].set(gates.T)
    rows_ext = jnp.concatenate([ffn_normed, padded], axis=0)
    gate_mat, up_mat, down_mat = gate_weight[0], up_weight[0], down_weight[0]
    received, expert_hidden, d_out, d_gate_pre, d_up_pre, moe_a, moe_b, d_gate_at = fwd_call(
        slot, rows_ext, cot_all, gate_mat, up_mat, down_mat, cap, n_ctx, n_exp, tok
    )
    total = experts * cap

    d_gate = lax.all_to_all(
        d_gate_at.reshape(experts, tok), MOE, split_axis=0, concat_axis=0, tiled=True
    ).T
    received = received.reshape(total, width)
    gate_low = dot_tn(received, d_gate_pre.reshape(total, -1)).astype(BF)
    moe_a = lax.psum_scatter(
        moe_a.reshape(experts * tok, width // 2), MOE, scatter_dimension=0, tiled=True
    )
    up_low = dot_tn(received, d_up_pre.reshape(total, -1)).astype(BF)
    down_low = dot_tn(expert_hidden.reshape(total, -1), d_out.reshape(total, width)).astype(BF)
    most = width * 3 // 4
    swap = ((gate_low, width), (up_low, most)) if n_dp == 2 else ()
    d_gate_pre, down_low = lax.optimization_barrier((d_gate_pre, down_low))
    d_tokens, others = back_call(
        slot, d_gate_pre, d_up_pre, gate_mat, up_mat, swap, n_ctx, n_exp, tok, (1, 8)
    )
    down_low, d_tokens = lax.optimization_barrier((down_low, d_tokens))
    if swap:
        wide = [(gate_low, others[0]), (up_low[:most], others[1])]
        rest_up = low_dp(up_low[most:], n_dp)
    else:
        wide = [low_dp(gate_low, n_dp), low_dp(up_low[:most], n_dp)]
        rest_up = low_dp(up_low[most:], n_dp)
    wide = wide + [rest_up, low_dp(down_low, n_dp)]

    d_router = d_gate
    d_logits = (
        router_prob * (d_router - jnp.sum(router_prob * d_router, axis=-1, keepdims=True))
    ).astype(BF)
    router_grad = dot_tn(d_logits, ffn_normed)
    d_ffn = d_tokens.astype(F32) + dot_nt(d_logits, router_weight)
    ffn_gain_grad = jnp.sum(d_ffn * residual * ffn_r, axis=0)
    weighted = d_ffn * ffn_gain_f
    d_residual = cot.astype(F32) + (
        weighted * ffn_r
        - residual * ffn_r**3 * jnp.mean(residual * weighted, axis=-1, keepdims=True)
    )
    d_branch = d_residual.astype(BF)

    moe_b, d_branch = lax.optimization_barrier((moe_b, d_branch))
    moe_b = lax.psum_scatter(
        moe_b.reshape(experts * tok, width // 2), MOE, scatter_dimension=0, tiled=True
    )
    moe_out = jnp.concatenate([moe_a, moe_b], axis=1)
    d_branch_g = ag_ctx(d_branch, n_ctx, 7).reshape(group, width)
    out_grad = dot_tn(mix, d_branch_g)
    d_mix = dot_nt(d_branch_g, out_w).astype(BF)
    d_raw, gain_parts = attn_bwd(
        q_rot, k_rot, v_low, d_mix, raw, inv, cos, sin, label_row, label_col, gains, n_ctx, heads, 10
    )
    spread = jnp.zeros((2, n_dp, n_ctx, piece), F32)
    spread = lax.dynamic_update_slice(
        spread, gain_parts.reshape(2, n_dp, 1, piece), (0, 0, ctx_me, 0)
    ).reshape(2, width)
    small = jnp.concatenate([router_grad, spread, ffn_gain_grad[None]], axis=0)
    small = jnp.pad(small, ((0, 8 - small.shape[0] % 8), (0, 0)))
    out_part = out_grad.astype(BF).reshape(n_dp, n_exp, shard, width)
    query_sum, key_sum, value_sum, out_sum, hidden_grad, small = tail(
        normed_g, d_raw, qkv_w, out_part, hidden_in[0, 0], d_residual, attn_gain_f[None], small, n_ctx
    )
    query_sum, key_sum, value_sum, out_sum = (
        x.astype(F32) for x in (query_sum, key_sum, value_sum, out_sum)
    )
    wide, moe_out, small = lax.optimization_barrier((wide, moe_out, small))
    output = (residual + moe_out.astype(F32)).astype(BF)
    gate_sum, up_a, up_b, down_sum = (sum(x.astype(F32) for x in pair) for pair in wide)
    up_sum = jnp.concatenate([up_a, up_b], axis=0)

    return (
        output[None, None],
        hidden_grad[None, None],
        small[-1],
        query_sum,
        key_sum,
        value_sum,
        small[experts],
        small[experts + 1],
        out_sum,
        small[experts + 2],
        small[:experts].T,
        gate_sum[None],
        up_sum[None],
        down_sum[None],
    )


def solution(mesh):
    tokens = P("dp", "exp", "ctx", None)
    rows = P(ALL, None)
    expert = P(MOE, None, None)
    return jax.shard_map(
        per_device,
        mesh=mesh,
        in_specs=(
            tokens,
            P("dp", "exp", None),
            tokens,
            P(),
            rows,
            rows,
            rows,
            P(),
            P(),
            rows,
            P(),
            P(),
            expert,
            expert,
            expert,
            tokens,
        ),
        out_specs=(
            tokens,
            tokens,
            P(),
            rows,
            rows,
            rows,
            P(),
            P(),
            rows,
            P(),
            P(),
            expert,
            expert,
            expert,
        ),
        check_vma=False,
    )
```

```python
import functools

import jax
import jax.numpy as jnp
from jax import lax
from jax.experimental import pallas as pl
from jax.experimental.pallas import tpu as pltpu
from jax.sharding import PartitionSpec as P

HEAD = 128
PROMPT = 512
EPS = 1e-05
THETA = 10000.0
MASKED = -1e30
BF = jnp.bfloat16
F32 = jnp.float32
ALL = ("dp", "ctx", "exp")
MOE = ("ctx", "exp")
ROWS = ("dp", "exp")
MESH = pl.DeviceIdType.MESH


def by_distance(me, n):
    far=[jnp.abs(me-j)*n+j for j in range(n)]
    rank=[sum(((far[i]>far[j]).astype(jnp.int32) for i in range(n) if i!=j), jnp.int32(0)) for j in range(n)]
    def at(k):
        v=jnp.int32(0)
        for j in range(n): v=v+jnp.where(rank[j]==k,j,0)
        return v
    return at


def loop(n, body):
    def step(i,_):
        body(i)
        return 0
    lax.fori_loop(0,n,step,0)


def add_into(dst, src, rows=16):
    n=dst.shape[-2]//rows
    lead=dst.shape[:-2]
    assert not lead
    def body(i,_):
        sl=pl.ds(pl.multiple_of(i*rows,rows),rows)
        dst[sl,:]=dst[sl,:]+src[sl,:]
        return 0
    lax.fori_loop(0,n,body,0)


def add3(dst,src):
    if len(dst.shape)==2: add_into(dst,src); return
    def body(i,_):
        add_into(dst.at[i],src.at[i]); return 0
    lax.fori_loop(0,dst.shape[0],body,0)

def tail_kernel(N,C,E,nrm,dr,w,go,hid,dres,gain,sm,o1,o2,o3,oo,od,osm,own_q,own_o,own_d,yq,yo,uq,uo,vq,vo,d1,d2,ld,ldd,ys,yr,zs,zu,zd,s1,r1,s2,r2,a_s,a_r,osem,hv,rv,gv,b0,b1,b2,t_s,t_r,nv,drv,wv,sq,sd,m_s):
    p=lax.axis_index("dp"); c=lax.axis_index("ctx"); e=lax.axis_index("exp")
    H=C//2; h=c//2; l=c%2
    def dpeer(j): return lax.rem(p+j,N)
    def cpeer(j): return lax.rem(c+j,C)
    def hpeer(j): return lax.rem(h+j,H)
    bar=pltpu.get_barrier_semaphore()
    def sig(**kw): pl.semaphore_signal(bar,inc=1,device_id=kw,device_id_type=MESH)
    for j in range(1,N): sig(dp=dpeer(j))
    for j in range(1,C): sig(ctx=cpeer(j))
    for j in range(1,E): sig(exp=lax.rem(e+j,E))
    order=by_distance(e,E)
    def rc(src,dst,ss,rs,**kw): return pltpu.make_async_remote_copy(src,dst,ss,rs,device_id=kw,device_id_type=MESH)
    def loads(o): return [pltpu.make_async_copy(go.at[p,o],own_o.at[o],ld.at[1,o])]
    def cy(j,o):
        q=dpeer(j)
        return [rc(sq.at[j-1,o],yq.at[j-1,o],ys.at[0,j-1,o],yr.at[0,j-1,o],dp=q), rc(go.at[q,o],yo.at[j-1,o],ys.at[1,j-1,o],yr.at[1,j-1,o],dp=q)]
    def cu(o): return [rc(own_q.at[o],uq.at[o],zs.at[0,o],zu.at[0,o],exp=e+1), rc(own_o.at[o],uo.at[o],zs.at[1,o],zu.at[1,o],exp=e+1)]
    def cd(o): return [rc(own_q.at[o],vq.at[o],zs.at[0,o],zd.at[0,o],exp=e-1), rc(own_o.at[o],vo.at[o],zs.at[1,o],zd.at[1,o],exp=e-1)]
    def c1(hh): return rc(sd.at[hh],d1.at[hh],s1.at[hh],r1.at[hh],ctx=h*2+1-l)
    def c2(j):
        hh=hpeer(j); return rc(own_d.at[hh],d2.at[j-1],s2.at[j-1],r2.at[j-1],ctx=hh*2+l)
    hs=[hpeer(j) for j in range(1,H)]+[h]
    def start_loads(k):
        for x in loads(k): x.start()
    side=[pltpu.make_async_copy(hid,hv,osem.at[3]),pltpu.make_async_copy(dres,rv,osem.at[4]),pltpu.make_async_copy(gain,gv,osem.at[5]),pltpu.make_async_copy(sm,b0.at[p],osem.at[6])]
    for x in side: x.start()
    loop(E,start_loads)
    big=[pltpu.make_async_copy(a,b,m_s.at[i]) for i,(a,b) in enumerate(((nrm,nv),(dr,drv),(w,wv)))]
    for x in big: x.start()
    Dm=wv.shape[0]; W3=wv.shape[1]; S_=own_q.shape[2]; T_=own_d.shape[1]; pc=Dm//(N*C)
    def grads(q,put):
        def chunk(cc):
            cl=pl.ds(pl.multiple_of(q*(Dm//N)+cc*pc,128),pc)
            st=W3//3
            for t in range(3):
                g=tn(nv[:,cl],drv[:,t*st:(t+1)*st]).astype(BF)
                for ee in range(E): put.at[ee][cc,:,t*st:(t+1)*st]=g[ee*S_:(ee+1)*S_]
        loop(C,chunk)
    def dnorm(cc,put):
        rw=pl.ds(pl.multiple_of(cc*T_,T_),T_)
        def chunk(n):
            cl=pl.ds(pl.multiple_of(n*512,512),512)
            put[:,cl]=nt(drv[rw,:],wv[cl,:]).astype(BF)
        loop(Dm//512,chunk)
    pl.semaphore_wait(bar,(N-1)+(C-1)+(E-1))
    def start_o(k):
        for j in range(1,N): cy(j,order(k))[1].start()
    loop(E,start_o)
    big[0].wait(); big[1].wait()
    for j in range(1,N): grads(dpeer(j),sq.at[j-1])
    def start_q(k):
        for j in range(1,N): cy(j,order(k))[0].start()
    loop(E,start_q)
    big[2].wait()
    for hh in hs:
        dnorm(hh*2+1-l,sd.at[hh]); c1(hh).start()
        dnorm(hh*2+l,own_d.at[hh])
    grads(p,own_q)
    for i,hh in enumerate(hs):
        c1(hh).wait_recv(); add_into(own_d.at[hh],d1.at[hh])
        if i<H-1: c2(i+1).start()
    def line(k):
        o=order(k)
        for x in loads(o): x.wait()
        for j in range(1,N):
            for x in cy(j,o): x.wait_recv()
            add3(own_q.at[o],yq.at[j-1,o]); add3(own_o.at[o],yo.at[j-1,o])
        if True:
            @pl.when(o>e)
            def _():
                @pl.when(e>0)
                def _():
                    for x in cu(o): x.wait_recv()
                    add3(own_q.at[o],uq.at[o]); add3(own_o.at[o],uo.at[o])
                for x in cu(o): x.start()
            @pl.when(o<e)
            def _():
                @pl.when(e<E-1)
                def _():
                    for x in cd(o): x.wait_recv()
                    add3(own_q.at[o],vq.at[o]); add3(own_o.at[o],vo.at[o])
                for x in cd(o): x.start()
    small=((b0,"dp",N,p),(b1,"ctx",C,c),(b2,"exp",E,e))
    def hop(t,j):
        b,a,n,i=small[t]
        return rc(b.at[i],b.at[i],t_s.at[t,j-1],t_r.at[t,j-1],**{a:lax.rem(i+j,n)})
    def gathered(t):
        b,a,n,i=small[t]
        for j in range(1,n):
            q=lax.rem(i+n-j,n)
            rc(b.at[q],b.at[q],t_s.at[t,j-1],t_r.at[t,j-1],**{a:q}).wait_recv()
        x=b[0]
        for j in range(1,n): x=x+b[j]
        return x
    def send(t):
        for j in range(1,small[t][2]): hop(t,j).start()
    T,D=hv.shape; RB=16
    lastrow=b0.shape[1]-1
    def epilogue(i):
        sl=pl.ds(pl.multiple_of(i*RB,RB),RB)
        d=own_d[h,sl,:].astype(F32); x=hv[sl,:].astype(F32)
        r=lax.rsqrt(jnp.mean(x*x,axis=1,keepdims=True)+EPS)
        b0[p,lastrow:,:]+=jnp.sum(d*x*r,axis=0,keepdims=True)
        w=d*gv[...]
        own_d[h,sl,:]=(rv[sl,:]+(w*r-x*(r*r*r)*jnp.mean(x*w,axis=1,keepdims=True))).astype(BF)
    def lines(k):
        line(k)
        @pl.when(k==0)
        def _():
            for j in range(1,H):
                c2(j).wait_recv(); add_into(own_d.at[h],d2.at[j-1])
            for x in side: x.wait()
            loop(T//RB,epilogue)
            send(0)
            pltpu.make_async_copy(own_d.at[h],od,osem.at[0]).start()
        @pl.when(k==1)
        def _():
            b1[c]=gathered(0); send(1)
        @pl.when(k==2)
        def _():
            b2[e]=gathered(1); send(2)
    loop(E,lines)
    @pl.when(e>0)
    def _():
        for x in cu(e): x.wait_recv()
        add3(own_q.at[e],uq.at[e]); add3(own_o.at[e],uo.at[e])
    @pl.when(e<E-1)
    def _():
        for x in cd(e): x.wait_recv()
        add3(own_q.at[e],vq.at[e]); add3(own_o.at[e],vo.at[e])
    outs=(o1,o2,o3); cols=W3//3
    TD=[(t,d) for t in range(3) for d in range(N)]
    def src(q,t,d): return own_q.at[e,q,:,pl.ds(t*cols+d*pc,pc)]
    def dst(q,t,d): return outs[t].at[:,pl.ds(pl.multiple_of(d*(Dm//N)+q*pc,128),pc)]
    def ca(j,i): q=cpeer(j); return rc(src(q,*TD[i]),dst(c,*TD[i]),a_s.at[j-1,i],a_r.at[j-1,i],ctx=q)
    def cw(j,i): q=lax.rem(c+C-j,C); return rc(src(q,*TD[i]),dst(q,*TD[i]),a_s.at[j-1,i],a_r.at[j-1,i],ctx=q)
    for j in range(1,C):
        for i in range(len(TD)): ca(j,i).start()
    l1=[pltpu.make_async_copy(src(c,*TD[i]),dst(c,*TD[i]),m_s.at[3+i]) for i in range(len(TD))]
    for x in l1: x.start()
    l2=pltpu.make_async_copy(own_o.at[e],oo,osem.at[2]); l2.start()
    def drain(k):
        for j in range(1,N):
            for x in cy(j,k): x.wait_send()
        @pl.when(k!=e)
        def _():
            for x in cu(k): x.wait_send()
    loop(E,drain)
    for hh in hs: c1(hh).wait_send()
    for j in range(1,H): c2(j).wait_send()
    for j in range(1,C):
        for i in range(len(TD)):
            ca(j,i).wait_send(); cw(j,i).wait_recv()
    for t in range(3):
        for j in range(1,small[t][2]): hop(t,j).wait_send()
    b0[0]=gathered(2)
    so=pltpu.make_async_copy(b0.at[0],osm,osem.at[7]); so.start()
    pltpu.make_async_copy(own_d.at[h],od,osem.at[0]).wait(); l2.wait(); so.wait()
    for x in l1: x.wait()

def tail(nrm,dr,w,go,hid,dres,gain,sm,C,cid=2):
    N,E,S,D=go.shape; W3=dr.shape[1]; G=nrm.shape[0]; T=G//C; H=C//2; R=sm.shape[0]
    dma=pltpu.SemaphoreType.DMA; V=lambda *s: pltpu.VMEM(s,BF); FV=lambda *s: pltpu.VMEM(s,F32)
    M=max(N,C,E)-1
    sd=jax.ShapeDtypeStruct((S,D),BF)
    return pl.pallas_call(functools.partial(tail_kernel,N,C,E),
        out_shape=[sd]*4+[jax.ShapeDtypeStruct((T,D),BF),jax.ShapeDtypeStruct((R,D),F32)],
        in_specs=[pl.BlockSpec(memory_space=pl.ANY)]*8,
        out_specs=[pl.BlockSpec(memory_space=pl.ANY)]*6,
        scratch_shapes=[V(E,C,S,W3),V(E,S,D),V(H,T,D),V(N-1,E,C,S,W3),V(N-1,E,S,D),V(E,C,S,W3),V(E,S,D),V(E,C,S,W3),V(E,S,D),V(H,T,D),V(H-1,T,D),
            dma((2,E)),dma((H,)),dma((2,N-1,E)),dma((2,N-1,E)),dma((2,E)),dma((2,E)),dma((2,E)),dma((H,)),dma((H,)),dma((H-1,)),dma((H-1,)),dma((C-1,3*N)),dma((C-1,3*N)),dma((8,)),
            V(T,D),FV(T,D),FV(1,D),FV(N,R,D),FV(C,R,D),FV(E,R,D),dma((3,M)),dma((3,M)),
            V(G,D),V(G,W3),V(D,W3),V(N-1,E,C,S,W3),V(H,T,D),dma((3+3*N,))],
        cost_estimate=pl.CostEstimate(flops=4*G*D*W3,bytes_accessed=2*(G*D+G*W3+D*W3),transcendentals=0),
        compiler_params=pltpu.CompilerParams(collective_id=cid,has_side_effects=True,vmem_limit_bytes=61*2**20),
        name="tail")(nrm,dr,w,go,hid,dres,gain,sm)

def nn(a,b): return lax.dot_general(a,b,(((1,),(0,)),((),())),preferred_element_type=F32)
def tn(a,b): return lax.dot_general(a,b,(((0,),(0,)),((),())),preferred_element_type=F32)
def nt(a,b): return lax.dot_general(a,b,(((1,),(1,)),((),())),preferred_element_type=F32)

def pick_of(slot_row, cap):
    T=slot_row.shape[1]
    return jnp.broadcast_to(slot_row,(cap,T))==lax.broadcasted_iota(jnp.int32,(cap,T),0)

def back_kernel(H,E,cap,X,slot,dgp,dup,gw,uw,*rest):
    ex_in,o_ref,ex_out=rest[:X],rest[X],rest[X+1:2*X+1]
    own,r1,r2,rz,snd,gb,ub,slv,wg,wu,ld_sem,w_sem,s1,q1,s2,q2,s3,qz,o_sem=rest[2*X+1:2*X+20]
    c=lax.axis_index("ctx"); e=lax.axis_index("exp")
    h=c//2; l=c%2
    T,W=own.shape[2:]; FF=wg.shape[1]
    sib={"ctx":h*2+1-l}
    def xpeer(j): return lax.rem(h+j,H)
    bar=pltpu.get_barrier_semaphore()
    pl.semaphore_signal(bar,inc=1,device_id=sib,device_id_type=MESH)
    for j in range(1,H):
        pl.semaphore_signal(bar,inc=1,device_id={"ctx":xpeer(j)*2+l},device_id_type=MESH)
    @pl.when(e>0)
    def _(): pl.semaphore_signal(bar,inc=1,device_id={"exp":e-1},device_id_type=MESH)
    @pl.when(e<E-1)
    def _(): pl.semaphore_signal(bar,inc=1,device_id={"exp":e+1},device_id_type=MESH)
    def ex(i):
        es,er=rest[2*X+20:]
        return pltpu.make_async_remote_copy(ex_in[i].at[:ex_out[i].shape[0]],ex_out[i],es.at[i],er.at[i],device_id={"dp":1-lax.axis_index("dp")},device_id_type=MESH)
    if X: pl.semaphore_signal(bar,inc=1,device_id={"dp":1-lax.axis_index("dp")},device_id_type=MESH)
    order=by_distance(e,E)
    wl=[pltpu.make_async_copy(gw,wg,w_sem.at[0]),pltpu.make_async_copy(uw,wu,w_sem.at[1])]
    for x in wl: x.start()
    NS=snd.shape[0]; M=H*E
    def place(m):
        return lax.rem(h+1+m//E,H),order(lax.rem(m,E))
    def loads(n):
        hh,o=place(n//2)
        s=(hh*2+jnp.where(lax.rem(n,2)==0,1-l,l))*E+o; b=lax.rem(n,2)
        return [pltpu.make_async_copy(dgp.at[s],gb.at[b],ld_sem.at[0,b]),pltpu.make_async_copy(dup.at[s],ub.at[b],ld_sem.at[1,b])],s
    for x in loads(0)[0]: x.start()
    def c1(m):
        hh,o=place(m)
        return pltpu.make_async_remote_copy(snd.at[lax.rem(m,NS)],r1.at[hh,o],s1.at[m],q1.at[hh,o],device_id=sib,device_id_type=MESH)
    def c2(j,o):
        hh=xpeer(j)
        return pltpu.make_async_remote_copy(own.at[hh,o],r2.at[j-1,o],s2.at[j-1,o],q2.at[j-1,o],device_id={"ctx":hh*2+l},device_id_type=MESH)
    def cz(o,to,slot_): return pltpu.make_async_remote_copy(own.at[h,o],rz.at[slot_],s3.at[o],qz.at[slot_],device_id={"exp":to},device_id_type=MESH)
    step=min(512,W)
    def compute(n,dst):
        x,s=loads(n); b=lax.rem(n,2)
        for y in x: y.wait()
        @pl.when(n+1<2*M)
        def _():
            for y in loads(n+1)[0]: y.start()
        low=pick_of(slv[pl.ds(s,1),:],cap).astype(F32).astype(BF)
        def body(i):
            sl=pl.ds(pl.multiple_of(i*step,step),step)
            d=(nt(gb[b],wg[sl,:])+nt(ub[b],wu[sl,:])).astype(BF)
            dst[:,sl]=tn(low,d).astype(BF)
        loop(W//step,body)
    pltpu.sync_copy(slot,slv)
    for x in wl: x.wait()
    pl.semaphore_wait(bar,H+min(X,1)+(e>0).astype(jnp.int32)+(e<E-1).astype(jnp.int32))
    for i in range(X): ex(i).start()
    def zstep(k):
        o=order(k)
        for j in range(1,H):
            c2(j,o).wait_recv()
            add_into(own.at[h,o],r2.at[j-1,o])
        @pl.when(o>e)
        def _():
            @pl.when(e>0)
            def _():
                cz(o,e-1,o).wait_recv(); add_into(own.at[h,o],rz.at[o])
            cz(o,e+1,o).start()
        @pl.when(o<e)
        def _():
            @pl.when(e<E-1)
            def _():
                cz(o,e+1,o).wait_recv(); add_into(own.at[h,o],rz.at[o])
            cz(o,e-1,jnp.where(o==e-1,E,o)).start()
    def pair(m):
        hh,o=place(m)
        @pl.when(m>=NS)
        def _(): c1(m-NS).wait_send()
        compute(2*m,snd.at[lax.rem(m,NS)])
        c1(m).start()
        compute(2*m+1,own.at[hh,o])
        c1(m).wait_recv()
        add_into(own.at[hh,o],r1.at[hh,o])
        for j in range(1,H):
            @pl.when(m//E==j-1)
            def _(): c2(j,o).start()
        @pl.when(m//E==H-1)
        def _(): zstep(lax.rem(m,E))
    loop(M,pair)
    for m in range(max(0,M-NS),M): c1(m).wait_send()
    @pl.when(e>0)
    def _():
        cz(e,e-1,e).wait_recv(); add_into(own.at[h,e],rz.at[e])
    @pl.when(e<E-1)
    def _():
        cz(e,e+1,E).wait_recv(); add_into(own.at[h,e],rz.at[E])
    out=pltpu.make_async_copy(own.at[h,e],o_ref,o_sem); out.start()
    def drain(k):
        for j in range(1,H): c2(j,order(k)).wait_send()
        @pl.when(k<E-1)
        def _(): cz(order(k),e,order(k)).wait_send()
    loop(E,drain)
    out.wait()
    for i in range(X): ex(i).wait()


def back_call(slot,dgp,dup,gw,uw,swap,C,E,T,cids):
    S,cap,FF=dgp.shape; D=gw.shape[0]; H=C//2
    dma=pltpu.SemaphoreType.DMA; V=lambda *s: pltpu.VMEM(s,BF)
    blocks=2*H*E+(H-1)*E+E+4
    parts=1
    while 2*(blocks*T*D//parts+2*D//parts*FF+4*cap*FF)>60*2**20: parts*=2
    W=D//parts
    A=pl.BlockSpec(memory_space=pl.ANY)
    def part(i):
        a,b=(gw,uw) if parts==1 else (gw[i*W:(i+1)*W],uw[i*W:(i+1)*W])
        ex=tuple(swap) if i==0 else ()
        X=len(ex)
        return pl.pallas_call(functools.partial(back_kernel,H,E,cap,X),
            out_shape=[jax.ShapeDtypeStruct((T,W),BF)]+[jax.ShapeDtypeStruct((n,g.shape[1]),g.dtype) for g,n in ex],
            in_specs=[A]*(5+X),
            out_specs=[A]*(1+X),
            scratch_shapes=[V(H,E,T,W),V(H,E,T,W),V(H-1,E,T,W),V(E+1,T,W),V(3,T,W),V(2,cap,FF),V(2,cap,FF),pltpu.VMEM((S,T),jnp.int32),V(W,FF),V(W,FF),
                dma((2,2)),dma((2,)),dma((H*E,)),dma((H,E)),dma((H-1,E)),dma((H-1,E)),dma((E,)),dma((E+1,)),dma(())]+([dma((X,)),dma((X,))] if X else []),
            cost_estimate=pl.CostEstimate(flops=2*S*cap*(2*W*FF+T*W),bytes_accessed=S*4*cap*FF,transcendentals=0),
            compiler_params=pltpu.CompilerParams(collective_id=cids[i],has_side_effects=True,vmem_limit_bytes=61*2**20),
            name="back")(slot,dgp,dup,a,b,*[g for g,_ in ex])
    out=[part(i) for i in range(parts)]
    tok=out[0][0] if parts==1 else jnp.concatenate([o[0] for o in out],axis=1)
    return tok,out[0][1:]


def fwd_kernel(H,E,T,cap,in_vmem,slot,rows,cot,gw,uw,dw,recv,hid,dout,dgp,dup,moe_a,moe_b,dg,*scr):
    if in_vmem: allr=scr[0]; scr=scr[1:]; rb=None
    else: allr=scr[0]; rb=scr[1]; scr=scr[2:]
    (slv,wg,wu,wd,cb,srecv,shid,sdout,sdgp,sdup,smoe,sdg,cr,w_sem,c_sem,l_sem,o_sem,up_s,dn_s,up_r,dn_r,x_s,x_r,b_s,b_r)=scr
    c=lax.axis_index("ctx"); e=lax.axis_index("exp")
    h=c//2; l=c%2; C=2*H; S=C*E
    D=wg.shape[0]; FF=wg.shape[1]; EXT=allr.shape[1]
    expert=c*E+e
    def xpeer(j): return lax.rem(h+j,H)
    def idx(hh,ll,ee): return (hh*2+ll)*E+ee
    bar=pltpu.get_barrier_semaphore()
    pl.semaphore_signal(bar,inc=1,device_id={"ctx":h*2+1-l},device_id_type=MESH)
    for j in range(1,H):
        pl.semaphore_signal(bar,inc=1,device_id={"ctx":xpeer(j)*2+l},device_id_type=MESH)
    @pl.when(e>0)
    def _(): pl.semaphore_signal(bar,inc=1,device_id={"exp":e-1},device_id_type=MESH)
    @pl.when(e<E-1)
    def _(): pl.semaphore_signal(bar,inc=1,device_id={"exp":e+1},device_id_type=MESH)
    order=by_distance(e,E)
    def near(k): return order(E-1-k)
    own=idx(h,l,e)
    wl=[pltpu.make_async_copy(a,b,w_sem.at[i]) for i,(a,b) in enumerate(((gw,wg),(uw,wu),(dw,wd)))]
    first=pltpu.make_async_copy(rows,allr.at[own],w_sem.at[3])
    first.start()
    for x in wl: x.start()
    def job(n):
        m=jnp.maximum(n-2,0)
        r=jnp.where(n<2,0,1+m//(2*H)); t=jnp.where(n<2,n,lax.rem(m,2*H))
        t=jnp.where(r==E,t+2,t)
        j=t//2
        return r,t,j,lax.rem(t,2),jnp.where(j==0,r,r-1)
    def hi(j): return jnp.where(j==0,h,lax.rem(h+H-j,H))
    def sender(n):
        r,t,j,s,k=job(n)
        return idx(hi(j),jnp.where(s==1,1-l,l),near(k))
    def cload(n): return pltpu.make_async_copy(cot.at[sender(n)],cb.at[lax.rem(n,2)],c_sem.at[lax.rem(n,2)])
    cload(0).start()
    def rc(i,ss,rs,**kw): return pltpu.make_async_remote_copy(allr.at[i],allr.at[i],ss,rs,device_id=kw,device_id_type=MESH)
    def up(ee): return rc(idx(h,l,ee),up_s.at[ee],up_r.at[ee],exp=e+1)
    def dn(ee): return rc(idx(h,l,ee),dn_s.at[ee],dn_r.at[ee],exp=e-1)
    def xs(j,ee): return rc(idx(h,l,ee),x_s.at[j-1,ee],x_r.at[j-1,ee],ctx=xpeer(j)*2+l)
    def xr(j,ee):
        return rc(idx(hi(j),l,ee),x_s.at[j-1,ee],x_r.at[j-1,ee],ctx=hi(j)*2+l)
    def bs(j,ee): return rc(idx(hi(j),l,ee),b_s.at[j,ee],b_r.at[j,ee],ctx=h*2+1-l)
    def br(j,ee): return rc(idx(hi(j),1-l,ee),b_s.at[j,ee],b_r.at[j,ee],ctx=h*2+1-l)
    outs=[(srecv,recv),(shid,hid),(sdout,dout),(sdgp,dgp),(sdup,dup),(smoe.at[:,:,:D//2],moe_a),(smoe.at[:,:,D//2:],moe_b),(sdg,dg)]
    def odma(n):
        s=sender(n); b=lax.rem(n,2)
        return [pltpu.make_async_copy(a.at[b],o.at[s],o_sem.at[i,b]) for i,(a,o) in enumerate(outs)]
    def compute(n):
        s=sender(n); b=lax.rem(n,2)
        if in_vmem: rw=allr.at[s]
        else:
            cp=pltpu.make_async_copy(allr.at[s],rb,l_sem); cp.start(); cp.wait(); rw=rb
        cload(n).wait()
        @pl.when(n+1<S)
        def _(): cload(n+1).start()
        @pl.when(n>=2)
        def _():
            for x in odma(n-2): x.wait()
        ct=cb.at[b]
        pk=pick_of(slv[pl.ds(s,1),:],cap); pf=pk.astype(F32); low=pf.astype(BF)
        gm=rw[T:EXT,:T].astype(F32)
        g=jnp.sum(jnp.where(lax.broadcasted_iota(jnp.int32,gm.shape,0)==expert,gm,0.0),axis=0,keepdims=True)
        gsel=jnp.where(pk,jnp.broadcast_to(g,(cap,T)),0.0)
        grow=jnp.sum(gsel,axis=1,keepdims=True)
        comb=gsel.astype(BF)
        step=512
        for m in range(0,D,step):
            srecv[b,:,m:m+step]=nn(low,rw[:T,m:m+step]).astype(BF)
            q=nn(low,ct[:,m:m+step])
            sdout[b,:,m:m+step]=(q*grow).astype(BF)
            cr[:,m:m+step]=q.astype(BF)
        half=FF//2
        for m in range(0,FF,half):
            gp=nn(srecv[b],wg[:,m:m+half]); upp=nn(srecv[b],wu[:,m:m+half])
            dh=nt(sdout[b],wd[m:m+half,:])
            sg=jax.nn.sigmoid(gp); si=gp*sg
            shid[b,:,m:m+half]=(si*upp).astype(BF)
            sdgp[b,:,m:m+half]=(dh*upp*sg*(1.0+gp*(1.0-sg))).astype(BF)
            sdup[b,:,m:m+half]=(dh*si).astype(BF)
        acc=jnp.zeros((cap,1),F32)
        for m in range(0,D,step):
            ev=nn(shid[b],wd[:,m:m+step]).astype(BF)
            acc=acc+jnp.sum(cr[:,m:m+step].astype(F32)*ev.astype(F32),axis=1,keepdims=True)
            smoe[b,:,m:m+step]=tn(comb,ev).astype(BF)
        sdg[b]=jnp.sum(pf*acc,axis=0,keepdims=True)
        for x in odma(n): x.start()
    pltpu.sync_copy(slot,slv)
    first.wait()
    pl.semaphore_wait(bar,H+(e>0).astype(jnp.int32)+(e<E-1).astype(jnp.int32))
    @pl.when(e<E-1)
    def _(): up(e).start()
    @pl.when(e>0)
    def _(): dn(e).start()
    for j in range(1,H): xs(j,e).start()
    bs(0,e).start()
    for x in wl: x.wait()
    def step_(n):
        r,t,j,sib_,k=job(n)
        @pl.when(jnp.logical_and(t==0,r>0))
        def _():
            @pl.when(e>=r)
            def _():
                up(e-r).wait_recv()
                @pl.when(e<E-1)
                def _(): up(e-r).start()
                for q in range(1,H): xs(q,e-r).start()
                bs(0,e-r).start()
            @pl.when(e+r<E)
            def _():
                dn(e+r).wait_recv()
                @pl.when(e>0)
                def _(): dn(e+r).start()
                for q in range(1,H): xs(q,e+r).start()
                bs(0,e+r).start()
        @pl.when(jnp.logical_and(sib_==0,j>0))
        def _():
            xr(j,near(k)).wait_recv(); bs(j,near(k)).start()
        @pl.when(sib_==1)
        def _(): br(j,near(k)).wait_recv()
        compute(n)
    loop(S,step_)
    for x in odma(S-2)+odma(S-1): x.wait()
    def drain(ee):
        @pl.when(jnp.logical_and(e<E-1,ee<=e))
        def _(): up(ee).wait_send()
        @pl.when(jnp.logical_and(e>0,ee>=e))
        def _(): dn(ee).wait_send()
        for j in range(1,H): xs(j,ee).wait_send()
        for j in range(H): bs(j,ee).wait_send()
    loop(E,drain)


def fwd_call(slot,rows,cot,gw,uw,dw,cap,C,E,T,cid=4):
    EXT,D=rows.shape; S=C*E; H=C//2; FF=gw.shape[1]
    dma=pltpu.SemaphoreType.DMA; V=lambda *s: pltpu.VMEM(s,BF)
    in_vmem=S*EXT*D*2<=28*2**20
    A=pl.BlockSpec(memory_space=pl.ANY)
    sd=lambda a,b,dt=BF: jax.ShapeDtypeStruct((S,a,b),dt)
    out_shape=[sd(cap,D),sd(cap,FF),sd(cap,D),sd(cap,FF),sd(cap,FF),sd(T,D//2),sd(T,D//2),sd(1,T,F32)]
    land=[V(S,EXT,D)] if in_vmem else [V(EXT,D)]
    if not in_vmem: out_shape=out_shape+[sd(EXT,D)]
    body=functools.partial(fwd_kernel,H,E,T,cap,in_vmem)
    r=pl.pallas_call(body,out_shape=out_shape,in_specs=[A]*6,out_specs=[A]*len(out_shape),
        scratch_shapes=land+[pltpu.VMEM((S,T),jnp.int32),V(D,FF),V(D,FF),V(FF,D),V(2,T,D),V(2,cap,D),V(2,cap,FF),V(2,cap,D),V(2,cap,FF),V(2,cap,FF),V(2,T,D),pltpu.VMEM((2,1,T),F32),V(cap,D),
            dma((4,)),dma((2,)),dma(()),dma((8,2)),dma((E,)),dma((E,)),dma((E,)),dma((E,)),dma((H-1,E)),dma((H-1,E)),dma((H,E)),dma((H,E))],
        cost_estimate=pl.CostEstimate(flops=2*S*cap*(4*D*FF+3*T*D),bytes_accessed=S*2*(T*D+2*cap*D+3*cap*FF+T*D)+6*D*FF,transcendentals=S*cap*FF),
        compiler_params=pltpu.CompilerParams(collective_id=cid,has_side_effects=True,vmem_limit_bytes=61*2**20),name="experts_fwd")(slot,rows,cot,gw,uw,dw)
    return r[:8]


def mask_bias(lab_r,lab_c,i0,bq,K):
    lr=lab_r[:,:K]; lc=lab_c
    row=lax.broadcasted_iota(jnp.int32,(bq,K),0)+i0; col=lax.broadcasted_iota(jnp.int32,(bq,K),1)
    ok=(col<=row)&((lr==0)|(lr==lc))
    return jnp.where(ok,0.0,-1e30).astype(F32)

def eye_mask():
    return lax.broadcasted_iota(jnp.int32,(HEAD,HEAD),0)==lax.broadcasted_iota(jnp.int32,(HEAD,HEAD),1)

def to_row(col):
    return jnp.sum(jnp.where(eye_mask(),jnp.broadcast_to(col,(HEAD,HEAD)),0.0),axis=0,keepdims=True)

def to_col(row):
    return jnp.sum(jnp.where(eye_mask(),jnp.broadcast_to(row,(HEAD,HEAD)),0.0),axis=1,keepdims=True)

def greet_ctx(C):
    c=lax.axis_index("ctx"); bar=pltpu.get_barrier_semaphore()
    for j in range(1,C): pl.semaphore_signal(bar,inc=1,device_id={"ctx":lax.rem(c+j,C)},device_id_type=MESH)

def sum_ctx(C,buf,ss,rs,others=0):
    c=lax.axis_index("ctx")
    pl.semaphore_wait(pltpu.get_barrier_semaphore(),C-1+others)
    def cp(j): return pltpu.make_async_remote_copy(buf.at[c],buf.at[c],ss.at[j-1],rs.at[j-1],device_id={"ctx":lax.rem(c+j,C)},device_id_type=MESH)
    for j in range(1,C): cp(j).start()
    for j in range(1,C):
        q=lax.rem(c+C-j,C)
        pltpu.make_async_remote_copy(buf.at[q],buf.at[q],ss.at[j-1],rs.at[j-1],device_id={"ctx":q},device_id_type=MESH).wait_recv()
    acc=buf[0]
    for j in range(1,C): acc=acc+buf[j]
    for j in range(1,C): cp(j).wait_send()
    return acc

class Rows:
    def __init__(self,N,E,x,o,ls,us,ur,ds_,dr_,ys,yr):
        self.N,self.E,self.x,self.o=N,E,x,o
        self.ls,self.us,self.ur,self.ds,self.dr,self.ys,self.yr=ls,us,ur,ds_,dr_,ys,yr
        self.p=lax.axis_index("dp"); self.e=lax.axis_index("exp")
        self.peers=(N-1)+(self.e>0).astype(jnp.int32)+(self.e<E-1).astype(jnp.int32)
    def greet(self):
        bar=pltpu.get_barrier_semaphore()
        def sig(**kw): pl.semaphore_signal(bar,inc=1,device_id=kw,device_id_type=MESH)
        for j in range(1,self.N): sig(dp=lax.rem(self.p+j,self.N))
        @pl.when(self.e>0)
        def _(): sig(exp=self.e-1)
        @pl.when(self.e<self.E-1)
        def _(): sig(exp=self.e+1)
        self.local=pltpu.make_async_copy(self.x,self.o.at[self.p,self.e],self.ls)
        self.local.start()
    def rc(self,q,ee,s,r,**kw): return pltpu.make_async_remote_copy(self.o.at[q,ee],self.o.at[q,ee],s,r,device_id=kw,device_id_type=MESH)
    def up(self,ee): return self.rc(self.p,ee,self.us.at[ee],self.ur.at[ee],exp=self.e+1)
    def dn(self,ee): return self.rc(self.p,ee,self.ds.at[ee],self.dr.at[ee],exp=self.e-1)
    def across(self,j,ee): return self.rc(self.p,ee,self.ys.at[j-1,ee],self.yr.at[j-1,ee],dp=lax.rem(self.p+j,self.N))
    def came(self,j,ee):
        q=lax.rem(self.p+self.N-j,self.N)
        return self.rc(q,ee,self.ys.at[j-1,ee],self.yr.at[j-1,ee],dp=q)
    def begin(self):
        e,E=self.e,self.E
        self.local.wait()
        for j in range(1,self.N): self.across(j,e).start()
        @pl.when(e<E-1)
        def _(): self.up(e).start()
        @pl.when(e>0)
        def _(): self.dn(e).start()
    def round(self,r):
        e,E=self.e,self.E
        @pl.when(e>=r)
        def _():
            self.up(e-r).wait_recv()
            @pl.when(e<E-1)
            def _(): self.up(e-r).start()
            for j in range(1,self.N): self.across(j,e-r).start()
        @pl.when(e+r<E)
        def _():
            self.dn(e+r).wait_recv()
            @pl.when(e>0)
            def _(): self.dn(e+r).start()
            for j in range(1,self.N): self.across(j,e+r).start()
    def finish(self):
        e,E=self.e,self.E
        def one(ee):
            for j in range(1,self.N):
                self.came(j,ee).wait_recv(); self.across(j,ee).wait_send()
            @pl.when(jnp.logical_and(e<E-1,ee<=e))
            def _(): self.up(ee).wait_send()
            @pl.when(jnp.logical_and(e>0,ee>=e))
            def _(): self.dn(ee).wait_send()
        loop(E,one)


def attn_fwd_kernel(N,C,E,heads,bq,scale,raw,cos,sin,lab_r,lab_c,gains,wo,qo,ko,vo,mix,inv,ow,bias,buf,ss,rs,*gs):
    G=raw.shape[0]; cols=heads*HEAD; nb=G//HEAD
    c=lax.axis_index("ctx")
    greet_ctx(C)
    rows_w=Rows(N,E,wo,ow,*gs)
    rows_w.greet()
    def squares(i):
        sl=pl.ds(pl.multiple_of(i*HEAD,HEAD),HEAD)
        for t in range(2):
            v=raw[sl,t*cols:(t+1)*cols]
            buf[c,pl.ds(t*nb+i,1),:]=to_row(jnp.sum(v*v,axis=1,keepdims=True))
        vo[sl,:]=raw[sl,2*cols:].astype(BF)
    loop(nb,squares)
    inv[...]=lax.rsqrt(sum_ctx(C,buf,ss,rs,rows_w.peers)/(C*cols)+EPS)
    rows_w.begin()
    def prep(i):
        sl=pl.ds(pl.multiple_of(i*HEAD,HEAD),HEAD)
        cs,sn=cos[sl,:],sin[sl,:]
        for t,o in ((0,qo),(1,ko)):
            r=to_col(inv[pl.ds(t*nb+i,1),:])
            for hd in range(heads):
                a=hd*HEAD
                v=raw[sl,t*cols+a:t*cols+a+HEAD]*r*gains[t:t+1,a:a+HEAD]
                o[sl,a:a+HEAD]=(v*cs+pltpu.roll(v,HEAD//2,1)*sn).astype(BF)
    loop(nb,prep)
    def block(i,K):
        rows=pl.ds(pl.multiple_of(i*bq,bq),bq)
        bias[:,:K]=mask_bias(lab_r,lab_c[rows,:],i*bq,bq,K)
        def head(hd):
            ln=pl.ds(pl.multiple_of(hd*HEAD,HEAD),HEAD)
            s=nt(qo[rows,ln],ko[:K,ln])*scale+bias[:,:K]
            p=jnp.exp(s-jnp.max(s,axis=1,keepdims=True))
            pr=(p*(1.0/jnp.sum(p,axis=1,keepdims=True))).astype(BF)
            mix[rows,ln]=nn(pr,vo[:K,ln]).astype(BF)
        loop(heads,head)
    per=G//bq//3
    for g in range(3):
        loop(per,lambda i,g=g: block(i+g*per,(g+1)*per*bq))
        if g+1<E: rows_w.round(g+1)
    for r in range(4,E): rows_w.round(r)
    rows_w.finish()

def attn_fwd(raw,cos,sin,lab_r,lab_c,gains,wo,N,C,E,heads,cid,bq=512):
    G=raw.shape[0]; cols=heads*HEAD; R=2*G//HEAD; dma=pltpu.SemaphoreType.DMA
    o=jax.ShapeDtypeStruct((G,cols),BF)
    V=pl.BlockSpec(memory_space=pltpu.VMEM); A=pl.BlockSpec(memory_space=pl.ANY)
    return pl.pallas_call(functools.partial(attn_fwd_kernel,N,C,E,heads,bq,HEAD**-0.5),out_shape=[o]*4+[jax.ShapeDtypeStruct((R,HEAD),F32),jax.ShapeDtypeStruct((N,E)+wo.shape,BF)],in_specs=[V]*6+[A],out_specs=[V]*5+[A],
        scratch_shapes=[pltpu.VMEM((bq,G),F32),pltpu.VMEM((C,R,HEAD),F32),dma((C-1,)),dma((C-1,)),dma(()),dma((E,)),dma((E,)),dma((E,)),dma((E,)),dma((N-1,E)),dma((N-1,E))],
        cost_estimate=pl.CostEstimate(flops=2*2*heads*G*G*HEAD,bytes_accessed=G*cols*20,transcendentals=heads*G*G),
        compiler_params=pltpu.CompilerParams(collective_id=cid,has_side_effects=True,vmem_limit_bytes=48*2**20),name="attn_fwd")(raw,cos,sin,lab_r,lab_c,gains,wo)

def attn_bwd_kernel(C,heads,bq,scale,q,k,v,dm,raw,inv,cos,sin,lab_r,lab_c,gains,draw,gsum,bias,aq,ak,av,buf,ss,rs):
    G=q.shape[0]; cols=heads*HEAD; nb=G//HEAD
    c=lax.axis_index("ctx")
    greet_ctx(C)
    ak[...]=jnp.zeros_like(ak); av[...]=jnp.zeros_like(av)
    def block(i,K):
        rows=pl.ds(pl.multiple_of(i*bq,bq),bq)
        bias[:,:K]=mask_bias(lab_r,lab_c[rows,:],i*bq,bq,K)
        def head(hd):
            ln=pl.ds(pl.multiple_of(hd*HEAD,HEAD),HEAD)
            qb=q[rows,ln]; kb=k[:K,ln]; db=dm[rows,ln]
            s=nt(qb,kb)*scale+bias[:,:K]
            p=jnp.exp(s-jnp.max(s,axis=1,keepdims=True))
            p=p*(1.0/jnp.sum(p,axis=1,keepdims=True))
            dp=nt(db,v[:K,ln])
            ds=(p*(dp-jnp.sum(p*dp,axis=1,keepdims=True))).astype(BF)
            aq[rows,ln]=nn(ds,kb)
            ak[:K,ln]+=tn(ds,qb)
            av[:K,ln]+=tn(p.astype(BF),db)
        loop(heads,head)
    per=G//bq//3
    for g in range(3):
        loop(per,lambda i,g=g: block(i+g*per,(g+1)*per*bq))
    gsum[...]=jnp.zeros_like(gsum)
    def unrope(i):
        sl=pl.ds(pl.multiple_of(i*HEAD,HEAD),HEAD)
        for t,a in ((0,aq),(1,ak)):
            r=to_col(inv[pl.ds(t*nb+i,1),:])
            dot=jnp.zeros((HEAD,1),F32)
            for hd in range(heads):
                b=hd*HEAD
                g=a[sl,b:b+HEAD]*scale
                g=g*cos[sl,:]-pltpu.roll(g,HEAD//2,1)*sin[sl,:]
                x=raw[sl,t*cols+b:t*cols+b+HEAD]
                gsum[t:t+1,b:b+HEAD]+=jnp.sum(g*x*r,axis=0,keepdims=True)
                g=g*gains[t:t+1,b:b+HEAD]
                a[sl,b:b+HEAD]=g
                dot=dot+jnp.sum(g*x,axis=1,keepdims=True)
            buf[c,pl.ds(t*nb+i,1),:]=to_row(dot)
        draw[sl,2*cols:]=av[sl,:].astype(BF)
    loop(nb,unrope)
    buf[0]=sum_ctx(C,buf,ss,rs)/(C*cols)
    def fin(i):
        sl=pl.ds(pl.multiple_of(i*HEAD,HEAD),HEAD)
        for t,a in ((0,aq),(1,ak)):
            r=to_col(inv[pl.ds(t*nb+i,1),:]); dot=to_col(buf[0,pl.ds(t*nb+i,1),:])
            m=r*r*r*dot
            draw[sl,t*cols:(t+1)*cols]=(a[sl,:]*r-raw[sl,t*cols:(t+1)*cols]*m).astype(BF)
    loop(nb,fin)

def attn_bwd(q,k,v,dm,raw,inv,cos,sin,lab_r,lab_c,gains,C,heads,cid,bq=512):
    G,cols=q.shape; R=2*G//HEAD; dma=pltpu.SemaphoreType.DMA
    V=pl.BlockSpec(memory_space=pltpu.VMEM)
    acc=pltpu.VMEM((G,cols),F32)
    return pl.pallas_call(functools.partial(attn_bwd_kernel,C,heads,bq,HEAD**-0.5),out_shape=[jax.ShapeDtypeStruct((G,3*cols),BF),jax.ShapeDtypeStruct((2,cols),F32)],in_specs=[V]*11,out_specs=[V]*2,
        scratch_shapes=[pltpu.VMEM((bq,G),F32),acc,acc,acc,pltpu.VMEM((C,R,HEAD),F32),dma((C-1,)),dma((C-1,))],
        cost_estimate=pl.CostEstimate(flops=5*2*heads*G*G*HEAD,bytes_accessed=G*cols*20,transcendentals=heads*G*G),
        compiler_params=pltpu.CompilerParams(collective_id=cid,has_side_effects=True,vmem_limit_bytes=56*2**20),name="attn_bwd")(q,k,v,dm,raw,inv,cos,sin,lab_r,lab_c,gains)

def ctx_barrier(H,c,h,l):
    bar=pltpu.get_barrier_semaphore()
    pl.semaphore_signal(bar,inc=1,device_id={"ctx":h*2+1-l},device_id_type=MESH)
    for j in range(1,H):
        pl.semaphore_signal(bar,inc=1,device_id={"ctx":lax.rem(h+j,H)*2+l},device_id_type=MESH)
    pl.semaphore_wait(bar,H)

def ag_ctx_kernel(H,Q,x,o,xs,xr,bs,br,lsem):
    c=lax.axis_index("ctx"); h=c//2; l=c%2
    T=x.shape[0]; R=T//Q
    loc=pltpu.make_async_copy(x,o.at[c],lsem); loc.start()
    ctx_barrier(H,c,h,l)
    sib=h*2+1-l
    def sl(q): return pl.ds(q*R,R)
    def rc(a,b,s,r,to): return pltpu.make_async_remote_copy(a,b,s,r,device_id={"ctx":to},device_id_type=MESH)
    def xc(j,q): return rc(x.at[sl(q)],o.at[c,sl(q)],xs.at[j-1,q],xr.at[j-1,q],lax.rem(h+j,H)*2+l)
    def xw(j,q):
        p=lax.rem(h+H-j,H)*2+l; return rc(x.at[sl(q)],o.at[p,sl(q)],xs.at[j-1,q],xr.at[j-1,q],p)
    def bc(j,q):
        p=c if j==0 else lax.rem(h+H-j,H)*2+l
        src=x if j==0 else o.at[p]
        return rc(src.at[sl(q)],o.at[p,sl(q)],bs.at[j,q],br.at[j,q],sib)
    def bw(j,q):
        p=sib if j==0 else lax.rem(h+H-j,H)*2+1-l
        return rc(x.at[sl(q)],o.at[p,sl(q)],bs.at[j,q],br.at[j,q],sib)
    for q in range(Q):
        for j in range(1,H): xc(j,q).start()
    for q in range(Q): bc(0,q).start()
    for q in range(Q):
        for j in range(1,H):
            xw(j,q).wait_recv(); bc(j,q).start()
    for j in range(H):
        for q in range(Q):
            bw(j,q).wait_recv(); bc(j,q).wait_send()
            if j>0: xc(j,q).wait_send()
    loc.wait()

def ag_ctx(x,C,cid,Q=4):
    T,D=x.shape; H=C//2; dma=pltpu.SemaphoreType.DMA
    A=pl.BlockSpec(memory_space=pl.ANY)
    return pl.pallas_call(functools.partial(ag_ctx_kernel,H,Q),out_shape=jax.ShapeDtypeStruct((C,T,D),x.dtype),in_specs=[A],out_specs=A,
        scratch_shapes=[dma((H-1,Q)),dma((H-1,Q)),dma((H,Q)),dma((H,Q)),dma(())],
        compiler_params=pltpu.CompilerParams(collective_id=cid,has_side_effects=True),name="ag_ctx")(x)

def rs_ctx_kernel(H,Q,mix,w,o,own,sd,r1,r2,s1,q1,s2,q2,osem):
    c=lax.axis_index("ctx"); h=c//2; l=c%2
    T=own.shape[1]; R=T//Q; D=w.shape[1]
    def sl(q): return pl.ds(q*R,R)
    hs=[lax.rem(h+j,H) for j in range(1,H)]+[h]
    def product(cc,put):
        rw=pl.ds(pl.multiple_of(cc*T,T),T)
        def chunk(n):
            cl=pl.ds(pl.multiple_of(n*512,512),512)
            put[:,cl]=nn(mix[rw,:],w[:,cl]).astype(BF)
        loop(D//512,chunk)
    def c1(i,q): return pltpu.make_async_remote_copy(sd.at[hs[i],sl(q)],r1.at[hs[i],sl(q)],s1.at[hs[i],q],q1.at[hs[i],q],device_id={"ctx":h*2+1-l},device_id_type=MESH)
    def c2(j,q): return pltpu.make_async_remote_copy(own.at[hs[j-1],sl(q)],r2.at[j-1,sl(q)],s2.at[j-1,q],q2.at[j-1,q],device_id={"ctx":hs[j-1]*2+l},device_id_type=MESH)
    ctx_barrier(H,c,h,l)
    for i in range(H):
        product(hs[i]*2+1-l,sd.at[hs[i]])
        for q in range(Q): c1(i,q).start()
        product(hs[i]*2+l,own.at[hs[i]])
        if i<H-1:
            for q in range(Q):
                c1(i,q).wait_recv()
                add_into(own.at[hs[i],sl(q)],r1.at[hs[i],sl(q)])
                c2(i+1,q).start()
    for q in range(Q):
        c1(H-1,q).wait_recv()
        add_into(own.at[h,sl(q)],r1.at[h,sl(q)])
    for q in range(Q):
        for j in range(1,H):
            c2(j,q).wait_recv()
            add_into(own.at[h,sl(q)],r2.at[j-1,sl(q)])
    out=pltpu.make_async_copy(own.at[h],o,osem); out.start()
    for q in range(Q):
        for i in range(H): c1(i,q).wait_send()
        for j in range(1,H): c2(j,q).wait_send()
    out.wait()


def rs_ctx(mix,w,C,cid,Q=4):
    G,cols=mix.shape; D=w.shape[1]; T=G//C; H=C//2; dma=pltpu.SemaphoreType.DMA
    A=pl.BlockSpec(memory_space=pl.ANY); V=pl.BlockSpec(memory_space=pltpu.VMEM)
    buf=pltpu.VMEM((H,T,D),BF)
    return pl.pallas_call(functools.partial(rs_ctx_kernel,H,Q),out_shape=jax.ShapeDtypeStruct((T,D),BF),in_specs=[V,V],out_specs=A,
        scratch_shapes=[buf,buf,buf,pltpu.VMEM((H-1,T,D),BF),dma((H,Q)),dma((H,Q)),dma((H-1,Q)),dma((H-1,Q)),dma(())],
        cost_estimate=pl.CostEstimate(flops=2*G*cols*D,bytes_accessed=2*(G*cols+cols*D+T*D),transcendentals=0),
        compiler_params=pltpu.CompilerParams(collective_id=cid,has_side_effects=True,vmem_limit_bytes=40*2**20),name="rs_ctx")(mix,w)


def front_kernel(N,C,E,Q,wq,wk,wv,nx,qkv,na,a_s,a_r,up_s,up_r,dn_s,dn_r,y_s,y_r,xs_,xr_,bs_,br_,lsem):
    p=lax.axis_index("dp"); c=lax.axis_index("ctx"); e=lax.axis_index("exp")
    H=C//2; h=c//2; l=c%2; sib=h*2+1-l
    D=wq.shape[1]; cols=D//C; piece=cols//N; T=nx.shape[0]; R=T//Q
    def dpeer(j): return lax.rem(p+j,N)
    def cpeer(j): return lax.rem(c+j,C)
    bar=pltpu.get_barrier_semaphore()
    def sig(**kw): pl.semaphore_signal(bar,inc=1,device_id=kw,device_id_type=MESH)
    for j in range(1,N): sig(dp=dpeer(j))
    for j in range(1,C): sig(ctx=cpeer(j))
    @pl.when(e>0)
    def _(): sig(exp=e-1)
    @pl.when(e<E-1)
    def _(): sig(exp=e+1)
    def rc(a,b,s,r,**kw): return pltpu.make_async_remote_copy(a,b,s,r,device_id=kw,device_id_type=MESH)
    W=(wq,wk,wv)
    def src(t,d,q): return W[t].at[:,pl.ds(pl.multiple_of(d*(D//N)+q*piece,128),piece)]
    def dst(t,d,q): return qkv.at[p,q,e,:,pl.ds(t*cols+d*piece,piece)]
    TD=[(t,d) for t in range(3) for d in range(N)]
    local=[pltpu.make_async_copy(src(t,d,c),dst(t,d,c),lsem.at[i]) for i,(t,d) in enumerate(TD)]
    local_n=pltpu.make_async_copy(nx,na.at[c],lsem.at[len(TD)+1])
    for x in local+[local_n]: x.start()
    def away(j,i):
        t,d=TD[i]; q=cpeer(j)
        return rc(src(t,d,q),dst(t,d,c),a_s.at[j-1,i],a_r.at[j-1,i],ctx=q)
    def home(j,i):
        t,d=TD[i]; q=lax.rem(c+C-j,C)
        return rc(src(t,d,q),dst(t,d,q),a_s.at[j-1,i],a_r.at[j-1,i],ctx=q)
    def both(q,ee): return ((0,qkv.at[q,:,ee]),)
    def up(i,ee): b=both(p,ee)[i][1]; return rc(b,b,up_s.at[i,ee],up_r.at[i,ee],exp=e+1)
    def dn(i,ee): b=both(p,ee)[i][1]; return rc(b,b,dn_s.at[i,ee],dn_r.at[i,ee],exp=e-1)
    def ys(i,j,ee): b=both(p,ee)[i][1]; return rc(b,b,y_s.at[i,j-1,ee],y_r.at[i,j-1,ee],dp=dpeer(j))
    def yr(i,j,ee): q=lax.rem(p+N-j,N); b=both(q,ee)[i][1]; return rc(b,b,y_s.at[i,j-1,ee],y_r.at[i,j-1,ee],dp=q)
    def sl(q): return pl.ds(q*R,R)
    def xc(j,q): return rc(nx.at[sl(q)],na.at[c,sl(q)],xs_.at[j-1,q],xr_.at[j-1,q],ctx=lax.rem(h+j,H)*2+l)
    def xw(j,q):
        s=lax.rem(h+H-j,H)*2+l; return rc(nx.at[sl(q)],na.at[s,sl(q)],xs_.at[j-1,q],xr_.at[j-1,q],ctx=s)
    def bc(j,q):
        s=c if j==0 else lax.rem(h+H-j,H)*2+l
        a=nx if j==0 else na.at[s]
        return rc(a.at[sl(q)],na.at[s,sl(q)],bs_.at[j,q],br_.at[j,q],ctx=sib)
    def bw(j,q):
        s=sib if j==0 else lax.rem(h+H-j,H)*2+1-l
        return rc(nx.at[sl(q)],na.at[s,sl(q)],bs_.at[j,q],br_.at[j,q],ctx=sib)
    pl.semaphore_wait(bar,(N-1)+(C-1)+(e>0).astype(jnp.int32)+(e<E-1).astype(jnp.int32))
    for j in range(1,C):
        for i in range(len(TD)): away(j,i).start()
    for q in range(Q):
        for j in range(1,H): xc(j,q).start()
    for q in range(Q): bc(0,q).start()
    for x in local: x.wait()
    for j in range(1,C):
        for i in range(len(TD)): home(j,i).wait_recv()
    for i in range(1):
        for j in range(1,N): ys(i,j,e).start()
        @pl.when(e<E-1)
        def _(): up(i,e).start()
        @pl.when(e>0)
        def _(): dn(i,e).start()
    def rounds(r0):
        r=r0+1
        for i in range(1):
            @pl.when(e>=r)
            def _():
                up(i,e-r).wait_recv()
                @pl.when(e<E-1)
                def _(): up(i,e-r).start()
                for j in range(1,N): ys(i,j,e-r).start()
            @pl.when(e+r<E)
            def _():
                dn(i,e+r).wait_recv()
                @pl.when(e>0)
                def _(): dn(i,e+r).start()
                for j in range(1,N): ys(i,j,e+r).start()
        @pl.when(r0==0)
        def _():
            for q in range(Q):
                for j in range(1,H):
                    xw(j,q).wait_recv(); bc(j,q).start()
    loop(E-1,rounds)
    def finish(ee):
        for i in range(1):
            for j in range(1,N):
                yr(i,j,ee).wait_recv(); ys(i,j,ee).wait_send()
            @pl.when(jnp.logical_and(e<E-1,ee<=e))
            def _(): up(i,ee).wait_send()
            @pl.when(jnp.logical_and(e>0,ee>=e))
            def _(): dn(i,ee).wait_send()
    loop(E,finish)
    for j in range(1,C):
        for i in range(len(TD)): away(j,i).wait_send()
    for q in range(Q):
        for j in range(1,H): xc(j,q).wait_send()
        for j in range(H):
            bc(j,q).wait_send(); bw(j,q).wait_recv()
    local_n.wait()


def front(wq,wk,wv,nx,N,C,E,cid,Q=2):
    S,D=wq.shape; T=nx.shape[0]; H=C//2; dma=pltpu.SemaphoreType.DMA
    A=pl.BlockSpec(memory_space=pl.ANY)
    return pl.pallas_call(functools.partial(front_kernel,N,C,E,Q),
        out_shape=[jax.ShapeDtypeStruct((N,C,E,S,3*D//C),BF),jax.ShapeDtypeStruct((C,T,D),BF)],
        in_specs=[A]*4,out_specs=[A]*2,
        scratch_shapes=[dma((C-1,3*N)),dma((C-1,3*N)),dma((2,E)),dma((2,E)),dma((2,E)),dma((2,E)),dma((2,N-1,E)),dma((2,N-1,E)),dma((H-1,Q)),dma((H-1,Q)),dma((H,Q)),dma((H,Q)),dma((3*N+2,))],
        compiler_params=pltpu.CompilerParams(collective_id=cid,has_side_effects=True),name="front")(wq,wk,wv,nx)


def add_kernel(split,*refs):
    g,og,u,oa,ob,d,od,sg,su,sd=refs
    i=pl.program_id(0)
    sg[...]=g[...].astype(F32)+og[...].astype(F32)
    su[...]=u[...].astype(F32)+jnp.where(i<split,oa[...].astype(F32),ob[...].astype(F32))
    sd[...]=d[...].astype(F32)+od[...].astype(F32)


def add_shares(g,og,u,oa,ob,d,od,steps=16):
    D,FF=g.shape; F2,D2=d.shape
    r,r2=D//steps,F2//steps
    split=oa.shape[0]//r
    wide=pl.BlockSpec((r,FF),lambda i:(i,0)); tall=pl.BlockSpec((r2,D2),lambda i:(i,0))
    return pl.pallas_call(functools.partial(add_kernel,split),grid=(steps,),
        in_specs=[wide,wide,wide,pl.BlockSpec((r,FF),lambda i:(jnp.minimum(i,split-1),0)),pl.BlockSpec((r,FF),lambda i:(jnp.maximum(i-split,0),0)),tall,tall],
        out_specs=[wide,wide,tall],
        out_shape=[jax.ShapeDtypeStruct((D,FF),F32)]*2+[jax.ShapeDtypeStruct((F2,D2),F32)],
        cost_estimate=pl.CostEstimate(flops=6*D*FF,bytes_accessed=24*D*FF,transcendentals=0),
        compiler_params=pltpu.CompilerParams(dimension_semantics=("arbitrary",),vmem_limit_bytes=32*2**20),name="add_shares")(g,og,u,oa,ob,d,od)


def dot_nn(a, b):
    return lax.dot_general(a, b, (((1,), (0,)), ((), ())), preferred_element_type=F32)


def dot_tn(a, b):
    return lax.dot_general(a, b, (((0,), (0,)), ((), ())), preferred_element_type=F32)


def dot_nt(a, b):
    return lax.dot_general(a, b, (((1,), (1,)), ((), ())), preferred_element_type=F32)


def per_device(
    hidden_in,
    segments,
    routes,
    attn_gain,
    query_weight,
    key_weight,
    value_weight,
    query_gain,
    key_gain,
    output_weight,
    ffn_gain,
    router_weight,
    gate_weight,
    up_weight,
    down_weight,
    cotangent,
):
    n_dp, n_ctx, n_exp = (lax.axis_size(a) for a in ALL)
    tok, width = hidden_in.shape[2:]
    topk = routes.shape[3]
    experts = n_ctx * n_exp
    cap = (5 * tok * topk + 4 * experts - 1) // (4 * experts)
    cap = -(-cap // 16) * 16
    group = segments.shape[2]
    shard = query_weight.shape[0]
    cols = width // n_ctx
    piece = cols // n_dp
    heads = cols // HEAD
    ctx_me = lax.axis_index("ctx")
    exp_me = lax.axis_index("exp")
    expert_me = ctx_me * n_exp + exp_me

    def own_cols(vec):
        return lax.dynamic_index_in_dim(
            vec.reshape(n_dp, n_ctx, piece), ctx_me, 1, keepdims=False
        ).reshape(cols)

    own_routes = routes[0, 0]
    expert_ids = jnp.arange(experts, dtype=jnp.int32)
    hits = jnp.sum((own_routes[:, :, None] == expert_ids).astype(jnp.int32), axis=1)
    tokens = jnp.arange(tok, dtype=jnp.int32)
    lower = (tokens[:, None] > tokens[None, :]).astype(BF)
    earlier = dot_nn(lower, hits.astype(BF)).astype(jnp.int32)
    slot_local = jnp.where(hits > 0, earlier, -1).T
    slot = lax.all_to_all(slot_local, MOE, split_axis=0, concat_axis=0, tiled=True)
    slot = slot.reshape(experts, tok)
    cot = cotangent[0, 0]

    hidden = hidden_in[0, 0].astype(F32)
    labels = segments[0, 0]
    index = jnp.arange(group, dtype=jnp.int32)
    before = jnp.sum((labels[None, :] < labels[:, None]).astype(jnp.int32), axis=1)
    positions = index - before + jnp.where(labels > 0, PROMPT, 0).astype(jnp.int32)
    half = HEAD // 2
    frequency = THETA ** (-(jnp.arange(half, dtype=F32) * 2.0 / HEAD))
    angles = positions.astype(F32)[:, None] * frequency[None, :]
    cos, sin = jnp.cos(angles), jnp.sin(angles)
    cos = jnp.concatenate([cos, cos], axis=1)
    sin = jnp.concatenate([-sin, sin], axis=1)
    label_row, label_col = labels[None, :], labels[:, None]
    attn_gain_f = attn_gain.astype(F32)
    ffn_gain_f = ffn_gain.astype(F32)
    q_gain = own_cols(query_gain.astype(F32))
    k_gain = own_cols(key_gain.astype(F32))

    attn_r = lax.rsqrt(jnp.mean(hidden * hidden, axis=-1, keepdims=True) + EPS)
    normed = (hidden * attn_r * attn_gain_f).astype(BF)
    qkv_w, normed_g = front(query_weight, key_weight, value_weight, normed, n_dp, n_ctx, n_exp, 5)
    qkv_w = qkv_w.reshape(width, 3 * cols)
    normed_g = normed_g.reshape(group, width)
    cot, normed_g = lax.optimization_barrier((cot, normed_g))
    cot_all = lax.all_gather(cot, MOE, axis=0, tiled=False)
    raw = dot_nn(normed_g, qkv_w)
    gains = jnp.stack([q_gain, k_gain])
    q_rot, k_rot, v_low, mix, inv, out_w = attn_fwd(
        raw, cos, sin, label_row, label_col, gains, output_weight, n_dp, n_ctx, n_exp, heads, 9
    )
    out_w = out_w.reshape(cols, width)
    branch = rs_ctx(mix, out_w, n_ctx, 6)
    residual = hidden + branch.astype(F32)

    ffn_r = lax.rsqrt(jnp.mean(residual * residual, axis=-1, keepdims=True) + EPS)
    ffn_normed = (residual * ffn_r * ffn_gain_f).astype(BF)
    logits = dot_nn(ffn_normed, router_weight)
    router_prob = jax.nn.softmax(logits, axis=-1)
    gates = jnp.where(hits > 0, router_prob, 0.0).astype(BF)
    padded = jnp.zeros((experts, width), BF).at[:, :tok].set(gates.T)
    rows_ext = jnp.concatenate([ffn_normed, padded], axis=0)
    gate_mat, up_mat, down_mat = gate_weight[0], up_weight[0], down_weight[0]
    received, expert_hidden, d_out, d_gate_pre, d_up_pre, moe_a, moe_b, d_gate_at = fwd_call(
        slot, rows_ext, cot_all, gate_mat, up_mat, down_mat, cap, n_ctx, n_exp, tok
    )
    total = experts * cap

    d_gate = lax.all_to_all(
        d_gate_at.reshape(experts, tok), MOE, split_axis=0, concat_axis=0, tiled=True
    ).T
    received = received.reshape(total, width)
    gate_low = dot_tn(received, d_gate_pre.reshape(total, -1)).astype(BF)
    moe_a = lax.psum_scatter(
        moe_a.reshape(experts * tok, width // 2), MOE, scatter_dimension=0, tiled=True
    )
    up_low = dot_tn(received, d_up_pre.reshape(total, -1)).astype(BF)
    down_low = dot_tn(expert_hidden.reshape(total, -1), d_out.reshape(total, width)).astype(BF)
    most = width * 3 // 4
    swap = ((gate_low, width), (up_low, most)) if n_dp == 2 else ()
    d_gate_pre, down_low = lax.optimization_barrier((d_gate_pre, down_low))
    d_tokens, others = back_call(
        slot, d_gate_pre, d_up_pre, gate_mat, up_mat, swap, n_ctx, n_exp, tok, (1, 8)
    )
    down_low, d_tokens = lax.optimization_barrier((down_low, d_tokens))
    if swap:
        pair = lambda x: lax.ppermute(x, "dp", [(0, 1), (1, 0)])
        wide = (gate_low, others[0], up_low, others[1], pair(up_low[most:]), down_low, pair(down_low))
    else:
        wide = tuple(lax.psum(x, "dp") for x in (gate_low, up_low, down_low))

    d_router = d_gate
    d_logits = (
        router_prob * (d_router - jnp.sum(router_prob * d_router, axis=-1, keepdims=True))
    ).astype(BF)
    router_grad = dot_tn(d_logits, ffn_normed)
    d_ffn = d_tokens.astype(F32) + dot_nt(d_logits, router_weight)
    ffn_gain_grad = jnp.sum(d_ffn * residual * ffn_r, axis=0)
    weighted = d_ffn * ffn_gain_f
    d_residual = cot.astype(F32) + (
        weighted * ffn_r
        - residual * ffn_r**3 * jnp.mean(residual * weighted, axis=-1, keepdims=True)
    )
    d_branch = d_residual.astype(BF)

    moe_b, d_branch = lax.optimization_barrier((moe_b, d_branch))
    moe_b = lax.psum_scatter(
        moe_b.reshape(experts * tok, width // 2), MOE, scatter_dimension=0, tiled=True
    )
    moe_out = jnp.concatenate([moe_a, moe_b], axis=1)
    d_branch_g = ag_ctx(d_branch, n_ctx, 7).reshape(group, width)
    out_grad = dot_tn(mix, d_branch_g)
    d_mix = dot_nt(d_branch_g, out_w).astype(BF)
    d_raw, gain_parts = attn_bwd(
        q_rot, k_rot, v_low, d_mix, raw, inv, cos, sin, label_row, label_col, gains, n_ctx, heads, 10
    )
    spread = jnp.zeros((2, n_dp, n_ctx, piece), F32)
    spread = lax.dynamic_update_slice(
        spread, gain_parts.reshape(2, n_dp, 1, piece), (0, 0, ctx_me, 0)
    ).reshape(2, width)
    small = jnp.concatenate([router_grad, spread, ffn_gain_grad[None]], axis=0)
    small = jnp.pad(small, ((0, 8 - small.shape[0] % 8), (0, 0)))
    out_part = out_grad.astype(BF).reshape(n_dp, n_exp, shard, width)
    query_sum, key_sum, value_sum, out_sum, hidden_grad, small = tail(
        normed_g, d_raw, qkv_w, out_part, hidden_in[0, 0], d_residual, attn_gain_f[None], small, n_ctx
    )
    query_sum, key_sum, value_sum, out_sum = (
        x.astype(F32) for x in (query_sum, key_sum, value_sum, out_sum)
    )
    wide, moe_out, small = lax.optimization_barrier((wide, moe_out, small))
    output = (residual + moe_out.astype(F32)).astype(BF)
    gate_sum, up_sum, down_sum = (
        add_shares(*wide) if n_dp == 2 else (x.astype(F32) for x in wide)
    )
    return (
        output[None, None],
        hidden_grad[None, None],
        small[-1],
        query_sum,
        key_sum,
        value_sum,
        small[experts],
        small[experts + 1],
        out_sum,
        small[experts + 2],
        small[:experts].T,
        gate_sum[None],
        up_sum[None],
        down_sum[None],
    )


def solution(mesh):
    tokens = P("dp", "exp", "ctx", None)
    rows = P(ALL, None)
    expert = P(MOE, None, None)
    return jax.shard_map(
        per_device,
        mesh=mesh,
        in_specs=(
            tokens,
            P("dp", "exp", None),
            tokens,
            P(),
            rows,
            rows,
            rows,
            P(),
            P(),
            rows,
            P(),
            P(),
            expert,
            expert,
            expert,
            tokens,
        ),
        out_specs=(
            tokens,
            tokens,
            P(),
            rows,
            rows,
            rows,
            P(),
            P(),
            rows,
            P(),
            P(),
            expert,
            expert,
            expert,
        ),
        check_vma=False,
    )
```

```python
import functools

import jax
import jax.numpy as jnp
from jax import lax
from jax.experimental import pallas as pl
from jax.experimental.pallas import tpu as pltpu
from jax.sharding import PartitionSpec as P

HEAD = 128
PROMPT = 512
EPS = 1e-05
THETA = 10000.0
MASKED = -1e30
BF = jnp.bfloat16
F32 = jnp.float32
ALL = ("dp", "ctx", "exp")
MOE = ("ctx", "exp")
ROWS = ("dp", "exp")
MESH = pl.DeviceIdType.MESH


def by_distance(me, n):
    far=[jnp.abs(me-j)*n+j for j in range(n)]
    rank=[sum(((far[i]>far[j]).astype(jnp.int32) for i in range(n) if i!=j), jnp.int32(0)) for j in range(n)]
    def at(k):
        v=jnp.int32(0)
        for j in range(n): v=v+jnp.where(rank[j]==k,j,0)
        return v
    return at


def loop(n, body):
    def step(i,_):
        body(i)
        return 0
    lax.fori_loop(0,n,step,0)


def add_into(dst, src, rows=16):
    n=dst.shape[-2]//rows
    lead=dst.shape[:-2]
    assert not lead
    def body(i,_):
        sl=pl.ds(pl.multiple_of(i*rows,rows),rows)
        dst[sl,:]=dst[sl,:]+src[sl,:]
        return 0
    lax.fori_loop(0,n,body,0)


def add3(dst,src):
    if len(dst.shape)==2: add_into(dst,src); return
    def body(i,_):
        add_into(dst.at[i],src.at[i]); return 0
    lax.fori_loop(0,dst.shape[0],body,0)

def tail_kernel(N,C,E,nrm,dr,w,go,hid,dres,gain,sm,o1,o2,o3,oo,od,osm,own_q,own_o,own_d,yq,yo,uq,uo,vq,vo,d1,d2,ld,ldd,ys,yr,zs,zu,zd,s1,r1,s2,r2,a_s,a_r,osem,hv,rv,gv,b0,b1,b2,t_s,t_r,nv,drv,wv,sq,sd,m_s):
    p=lax.axis_index("dp"); c=lax.axis_index("ctx"); e=lax.axis_index("exp")
    H=C//2; h=c//2; l=c%2
    def dpeer(j): return lax.rem(p+j,N)
    def cpeer(j): return lax.rem(c+j,C)
    def hpeer(j): return lax.rem(h+j,H)
    bar=pltpu.get_barrier_semaphore()
    def sig(**kw): pl.semaphore_signal(bar,inc=1,device_id=kw,device_id_type=MESH)
    for j in range(1,N): sig(dp=dpeer(j))
    for j in range(1,C): sig(ctx=cpeer(j))
    for j in range(1,E): sig(exp=lax.rem(e+j,E))
    order=by_distance(e,E)
    def rc(src,dst,ss,rs,**kw): return pltpu.make_async_remote_copy(src,dst,ss,rs,device_id=kw,device_id_type=MESH)
    def loads(o): return [pltpu.make_async_copy(go.at[p,o],own_o.at[o],ld.at[1,o])]
    def cy(j,o):
        q=dpeer(j)
        return [rc(sq.at[j-1,o],yq.at[j-1,o],ys.at[0,j-1,o],yr.at[0,j-1,o],dp=q), rc(go.at[q,o],yo.at[j-1,o],ys.at[1,j-1,o],yr.at[1,j-1,o],dp=q)]
    def cu(o): return [rc(own_q.at[o],uq.at[o],zs.at[0,o],zu.at[0,o],exp=e+1), rc(own_o.at[o],uo.at[o],zs.at[1,o],zu.at[1,o],exp=e+1)]
    def cd(o): return [rc(own_q.at[o],vq.at[o],zs.at[0,o],zd.at[0,o],exp=e-1), rc(own_o.at[o],vo.at[o],zs.at[1,o],zd.at[1,o],exp=e-1)]
    def c1(hh): return rc(sd.at[hh],d1.at[hh],s1.at[hh],r1.at[hh],ctx=h*2+1-l)
    def c2(j):
        hh=hpeer(j); return rc(own_d.at[hh],d2.at[j-1],s2.at[j-1],r2.at[j-1],ctx=hh*2+l)
    hs=[hpeer(j) for j in range(1,H)]+[h]
    def start_loads(k):
        for x in loads(k): x.start()
    side=[pltpu.make_async_copy(hid,hv,osem.at[3]),pltpu.make_async_copy(dres,rv,osem.at[4]),pltpu.make_async_copy(gain,gv,osem.at[5]),pltpu.make_async_copy(sm,b0.at[p],osem.at[6])]
    for x in side: x.start()
    loop(E,start_loads)
    big=[pltpu.make_async_copy(a,b,m_s.at[i]) for i,(a,b) in enumerate(((nrm,nv),(dr,drv),(w,wv)))]
    for x in big: x.start()
    Dm=wv.shape[0]; W3=wv.shape[1]; S_=own_q.shape[2]; T_=own_d.shape[1]; pc=Dm//(N*C)
    def grads(q,put):
        def chunk(cc):
            cl=pl.ds(pl.multiple_of(q*(Dm//N)+cc*pc,128),pc)
            st=W3//3
            for t in range(3):
                g=tn(nv[:,cl],drv[:,t*st:(t+1)*st]).astype(BF)
                for ee in range(E): put.at[ee][cc,:,t*st:(t+1)*st]=g[ee*S_:(ee+1)*S_]
        loop(C,chunk)
    def dnorm(cc,put):
        rw=pl.ds(pl.multiple_of(cc*T_,T_),T_)
        def chunk(n):
            cl=pl.ds(pl.multiple_of(n*512,512),512)
            put[:,cl]=nt(drv[rw,:],wv[cl,:]).astype(BF)
        loop(Dm//512,chunk)
    pl.semaphore_wait(bar,(N-1)+(C-1)+(E-1))
    def start_o(k):
        for j in range(1,N): cy(j,order(k))[1].start()
    loop(E,start_o)
    big[0].wait(); big[1].wait()
    for j in range(1,N): grads(dpeer(j),sq.at[j-1])
    def start_q(k):
        for j in range(1,N): cy(j,order(k))[0].start()
    loop(E,start_q)
    big[2].wait()
    for hh in hs:
        dnorm(hh*2+1-l,sd.at[hh]); c1(hh).start()
        dnorm(hh*2+l,own_d.at[hh])
    grads(p,own_q)
    for i,hh in enumerate(hs):
        c1(hh).wait_recv(); add_into(own_d.at[hh],d1.at[hh])
        if i<H-1: c2(i+1).start()
    def line(k):
        o=order(k)
        for x in loads(o): x.wait()
        for j in range(1,N):
            for x in cy(j,o): x.wait_recv()
            add3(own_q.at[o],yq.at[j-1,o]); add3(own_o.at[o],yo.at[j-1,o])
        if True:
            @pl.when(o>e)
            def _():
                @pl.when(e>0)
                def _():
                    for x in cu(o): x.wait_recv()
                    add3(own_q.at[o],uq.at[o]); add3(own_o.at[o],uo.at[o])
                for x in cu(o): x.start()
            @pl.when(o<e)
            def _():
                @pl.when(e<E-1)
                def _():
                    for x in cd(o): x.wait_recv()
                    add3(own_q.at[o],vq.at[o]); add3(own_o.at[o],vo.at[o])
                for x in cd(o): x.start()
    small=((b0,"dp",N,p),(b1,"ctx",C,c),(b2,"exp",E,e))
    def hop(t,j):
        b,a,n,i=small[t]
        return rc(b.at[i],b.at[i],t_s.at[t,j-1],t_r.at[t,j-1],**{a:lax.rem(i+j,n)})
    def gathered(t):
        b,a,n,i=small[t]
        for j in range(1,n):
            q=lax.rem(i+n-j,n)
            rc(b.at[q],b.at[q],t_s.at[t,j-1],t_r.at[t,j-1],**{a:q}).wait_recv()
        x=b[0]
        for j in range(1,n): x=x+b[j]
        return x
    def send(t):
        for j in range(1,small[t][2]): hop(t,j).start()
    T,D=hv.shape; RB=16
    lastrow=b0.shape[1]-1
    def epilogue(i):
        sl=pl.ds(pl.multiple_of(i*RB,RB),RB)
        d=own_d[h,sl,:].astype(F32); x=hv[sl,:].astype(F32)
        r=lax.rsqrt(jnp.mean(x*x,axis=1,keepdims=True)+EPS)
        b0[p,lastrow:,:]+=jnp.sum(d*x*r,axis=0,keepdims=True)
        w=d*gv[...]
        own_d[h,sl,:]=(rv[sl,:]+(w*r-x*(r*r*r)*jnp.mean(x*w,axis=1,keepdims=True))).astype(BF)
    def lines(k):
        line(k)
        @pl.when(k==1)
        def _():
            for j in range(1,H):
                c2(j).wait_recv(); add_into(own_d.at[h],d2.at[j-1])
            for x in side: x.wait()
            loop(T//RB,epilogue)
            send(0)
            pltpu.make_async_copy(own_d.at[h],od,osem.at[0]).start()
        @pl.when(k==2)
        def _():
            b1[c]=gathered(0); send(1)
        @pl.when(k==3)
        def _():
            b2[e]=gathered(1); send(2)
    loop(E,lines)
    @pl.when(e>0)
    def _():
        for x in cu(e): x.wait_recv()
        add3(own_q.at[e],uq.at[e]); add3(own_o.at[e],uo.at[e])
    @pl.when(e<E-1)
    def _():
        for x in cd(e): x.wait_recv()
        add3(own_q.at[e],vq.at[e]); add3(own_o.at[e],vo.at[e])
    outs=(o1,o2,o3); cols=W3//3
    TD=[(t,d) for t in range(3) for d in range(N)]
    def src(q,t,d): return own_q.at[e,q,:,pl.ds(t*cols+d*pc,pc)]
    def dst(q,t,d): return outs[t].at[:,pl.ds(pl.multiple_of(d*(Dm//N)+q*pc,128),pc)]
    def ca(j,i): q=cpeer(j); return rc(src(q,*TD[i]),dst(c,*TD[i]),a_s.at[j-1,i],a_r.at[j-1,i],ctx=q)
    def cw(j,i): q=lax.rem(c+C-j,C); return rc(src(q,*TD[i]),dst(q,*TD[i]),a_s.at[j-1,i],a_r.at[j-1,i],ctx=q)
    for j in range(1,C):
        for i in range(len(TD)): ca(j,i).start()
    l1=[pltpu.make_async_copy(src(c,*TD[i]),dst(c,*TD[i]),m_s.at[3+i]) for i in range(len(TD))]
    for x in l1: x.start()
    l2=pltpu.make_async_copy(own_o.at[e],oo,osem.at[2]); l2.start()
    def drain(k):
        for j in range(1,N):
            for x in cy(j,k): x.wait_send()
        @pl.when(k!=e)
        def _():
            for x in cu(k): x.wait_send()
    loop(E,drain)
    for hh in hs: c1(hh).wait_send()
    for j in range(1,H): c2(j).wait_send()
    for j in range(1,C):
        for i in range(len(TD)):
            ca(j,i).wait_send(); cw(j,i).wait_recv()
    for t in range(3):
        for j in range(1,small[t][2]): hop(t,j).wait_send()
    b0[0]=gathered(2)
    so=pltpu.make_async_copy(b0.at[0],osm,osem.at[7]); so.start()
    pltpu.make_async_copy(own_d.at[h],od,osem.at[0]).wait(); l2.wait(); so.wait()
    for x in l1: x.wait()

def tail(nrm,dr,w,go,hid,dres,gain,sm,C,cid=2):
    N,E,S,D=go.shape; W3=dr.shape[1]; G=nrm.shape[0]; T=G//C; H=C//2; R=sm.shape[0]
    dma=pltpu.SemaphoreType.DMA; V=lambda *s: pltpu.VMEM(s,BF); FV=lambda *s: pltpu.VMEM(s,F32)
    M=max(N,C,E)-1
    sd=jax.ShapeDtypeStruct((S,D),BF)
    return pl.pallas_call(functools.partial(tail_kernel,N,C,E),
        out_shape=[sd]*4+[jax.ShapeDtypeStruct((T,D),BF),jax.ShapeDtypeStruct((R,D),F32)],
        in_specs=[pl.BlockSpec(memory_space=pl.ANY)]*8,
        out_specs=[pl.BlockSpec(memory_space=pl.ANY)]*6,
        scratch_shapes=[V(E,C,S,W3),V(E,S,D),V(H,T,D),V(N-1,E,C,S,W3),V(N-1,E,S,D),V(E,C,S,W3),V(E,S,D),V(E,C,S,W3),V(E,S,D),V(H,T,D),V(H-1,T,D),
            dma((2,E)),dma((H,)),dma((2,N-1,E)),dma((2,N-1,E)),dma((2,E)),dma((2,E)),dma((2,E)),dma((H,)),dma((H,)),dma((H-1,)),dma((H-1,)),dma((C-1,3*N)),dma((C-1,3*N)),dma((8,)),
            V(T,D),FV(T,D),FV(1,D),FV(N,R,D),FV(C,R,D),FV(E,R,D),dma((3,M)),dma((3,M)),
            V(G,D),V(G,W3),V(D,W3),V(N-1,E,C,S,W3),V(H,T,D),dma((3+3*N,))],
        cost_estimate=pl.CostEstimate(flops=4*G*D*W3,bytes_accessed=2*(G*D+G*W3+D*W3),transcendentals=0),
        compiler_params=pltpu.CompilerParams(collective_id=cid,has_side_effects=True,vmem_limit_bytes=61*2**20),
        name="tail")(nrm,dr,w,go,hid,dres,gain,sm)

def nn(a,b): return lax.dot_general(a,b,(((1,),(0,)),((),())),preferred_element_type=F32)
def tn(a,b): return lax.dot_general(a,b,(((0,),(0,)),((),())),preferred_element_type=F32)
def nt(a,b): return lax.dot_general(a,b,(((1,),(1,)),((),())),preferred_element_type=F32)

def pick_of(slot_row, cap):
    T=slot_row.shape[1]
    return jnp.broadcast_to(slot_row,(cap,T))==lax.broadcasted_iota(jnp.int32,(cap,T),0)

def back_kernel(H,E,cap,X,slot,dgp,dup,gw,uw,*rest):
    ex_in,o_ref,ex_out=rest[:X],rest[X],rest[X+1:2*X+1]
    own,r1,r2,rz,snd,gb,ub,slv,wg,wu,ld_sem,w_sem,s1,q1,s2,q2,s3,qz,o_sem=rest[2*X+1:2*X+20]
    c=lax.axis_index("ctx"); e=lax.axis_index("exp")
    h=c//2; l=c%2
    T,W=own.shape[2:]; FF=wg.shape[1]
    sib={"ctx":h*2+1-l}
    def xpeer(j): return lax.rem(h+j,H)
    bar=pltpu.get_barrier_semaphore()
    pl.semaphore_signal(bar,inc=1,device_id=sib,device_id_type=MESH)
    for j in range(1,H):
        pl.semaphore_signal(bar,inc=1,device_id={"ctx":xpeer(j)*2+l},device_id_type=MESH)
    @pl.when(e>0)
    def _(): pl.semaphore_signal(bar,inc=1,device_id={"exp":e-1},device_id_type=MESH)
    @pl.when(e<E-1)
    def _(): pl.semaphore_signal(bar,inc=1,device_id={"exp":e+1},device_id_type=MESH)
    def ex(i):
        es,er=rest[2*X+20:]
        return pltpu.make_async_remote_copy(ex_in[i].at[:ex_out[i].shape[0]],ex_out[i],es.at[i],er.at[i],device_id={"dp":1-lax.axis_index("dp")},device_id_type=MESH)
    if X: pl.semaphore_signal(bar,inc=1,device_id={"dp":1-lax.axis_index("dp")},device_id_type=MESH)
    order=by_distance(e,E)
    wl=[pltpu.make_async_copy(gw,wg,w_sem.at[0]),pltpu.make_async_copy(uw,wu,w_sem.at[1])]
    for x in wl: x.start()
    NS=snd.shape[0]; M=H*E
    def place(m):
        return lax.rem(h+1+m//E,H),order(lax.rem(m,E))
    def loads(n):
        hh,o=place(n//2)
        s=(hh*2+jnp.where(lax.rem(n,2)==0,1-l,l))*E+o; b=lax.rem(n,2)
        return [pltpu.make_async_copy(dgp.at[s],gb.at[b],ld_sem.at[0,b]),pltpu.make_async_copy(dup.at[s],ub.at[b],ld_sem.at[1,b])],s
    for x in loads(0)[0]: x.start()
    def c1(m):
        hh,o=place(m)
        return pltpu.make_async_remote_copy(snd.at[lax.rem(m,NS)],r1.at[hh,o],s1.at[m],q1.at[hh,o],device_id=sib,device_id_type=MESH)
    def c2(j,o):
        hh=xpeer(j)
        return pltpu.make_async_remote_copy(own.at[hh,o],r2.at[j-1,o],s2.at[j-1,o],q2.at[j-1,o],device_id={"ctx":hh*2+l},device_id_type=MESH)
    def cz(o,to,slot_): return pltpu.make_async_remote_copy(own.at[h,o],rz.at[slot_],s3.at[o],qz.at[slot_],device_id={"exp":to},device_id_type=MESH)
    step=min(512,W)
    def compute(n,dst):
        x,s=loads(n); b=lax.rem(n,2)
        for y in x: y.wait()
        @pl.when(n+1<2*M)
        def _():
            for y in loads(n+1)[0]: y.start()
        low=pick_of(slv[pl.ds(s,1),:],cap).astype(F32).astype(BF)
        def body(i):
            sl=pl.ds(pl.multiple_of(i*step,step),step)
            d=(nt(gb[b],wg[sl,:])+nt(ub[b],wu[sl,:])).astype(BF)
            dst[:,sl]=tn(low,d).astype(BF)
        loop(W//step,body)
    pltpu.sync_copy(slot,slv)
    for x in wl: x.wait()
    pl.semaphore_wait(bar,H+min(X,1)+(e>0).astype(jnp.int32)+(e<E-1).astype(jnp.int32))
    for i in range(X): ex(i).start()
    def zstep(k):
        o=order(k)
        for j in range(1,H):
            c2(j,o).wait_recv()
            add_into(own.at[h,o],r2.at[j-1,o])
        @pl.when(o>e)
        def _():
            @pl.when(e>0)
            def _():
                cz(o,e-1,o).wait_recv(); add_into(own.at[h,o],rz.at[o])
            cz(o,e+1,o).start()
        @pl.when(o<e)
        def _():
            @pl.when(e<E-1)
            def _():
                cz(o,e+1,o).wait_recv(); add_into(own.at[h,o],rz.at[o])
            cz(o,e-1,jnp.where(o==e-1,E,o)).start()
    def pair(m):
        hh,o=place(m)
        @pl.when(m>=NS)
        def _(): c1(m-NS).wait_send()
        compute(2*m,snd.at[lax.rem(m,NS)])
        c1(m).start()
        compute(2*m+1,own.at[hh,o])
        c1(m).wait_recv()
        add_into(own.at[hh,o],r1.at[hh,o])
        for j in range(1,H):
            @pl.when(m//E==j-1)
            def _(): c2(j,o).start()
        @pl.when(m//E==H-1)
        def _(): zstep(lax.rem(m,E))
    loop(M,pair)
    for m in range(max(0,M-NS),M): c1(m).wait_send()
    @pl.when(e>0)
    def _():
        cz(e,e-1,e).wait_recv(); add_into(own.at[h,e],rz.at[e])
    @pl.when(e<E-1)
    def _():
        cz(e,e+1,E).wait_recv(); add_into(own.at[h,e],rz.at[E])
    out=pltpu.make_async_copy(own.at[h,e],o_ref,o_sem); out.start()
    def drain(k):
        for j in range(1,H): c2(j,order(k)).wait_send()
        @pl.when(k<E-1)
        def _(): cz(order(k),e,order(k)).wait_send()
    loop(E,drain)
    out.wait()
    for i in range(X): ex(i).wait()


def back_call(slot,dgp,dup,gw,uw,swap,C,E,T,cids):
    S,cap,FF=dgp.shape; D=gw.shape[0]; H=C//2
    dma=pltpu.SemaphoreType.DMA; V=lambda *s: pltpu.VMEM(s,BF)
    blocks=2*H*E+(H-1)*E+E+4
    parts=1
    while 2*(blocks*T*D//parts+2*D//parts*FF+4*cap*FF)>60*2**20: parts*=2
    W=D//parts
    A=pl.BlockSpec(memory_space=pl.ANY)
    def part(i):
        a,b=(gw,uw) if parts==1 else (gw[i*W:(i+1)*W],uw[i*W:(i+1)*W])
        ex=tuple(swap) if i==0 else ()
        X=len(ex)
        return pl.pallas_call(functools.partial(back_kernel,H,E,cap,X),
            out_shape=[jax.ShapeDtypeStruct((T,W),BF)]+[jax.ShapeDtypeStruct((n,g.shape[1]),g.dtype) for g,n in ex],
            in_specs=[A]*(5+X),
            out_specs=[A]*(1+X),
            scratch_shapes=[V(H,E,T,W),V(H,E,T,W),V(H-1,E,T,W),V(E+1,T,W),V(3,T,W),V(2,cap,FF),V(2,cap,FF),pltpu.VMEM((S,T),jnp.int32),V(W,FF),V(W,FF),
                dma((2,2)),dma((2,)),dma((H*E,)),dma((H,E)),dma((H-1,E)),dma((H-1,E)),dma((E,)),dma((E+1,)),dma(())]+([dma((X,)),dma((X,))] if X else []),
            cost_estimate=pl.CostEstimate(flops=2*S*cap*(2*W*FF+T*W),bytes_accessed=S*4*cap*FF,transcendentals=0),
            compiler_params=pltpu.CompilerParams(collective_id=cids[i],has_side_effects=True,vmem_limit_bytes=61*2**20),
            name="back")(slot,dgp,dup,a,b,*[g for g,_ in ex])
    out=[part(i) for i in range(parts)]
    tok=out[0][0] if parts==1 else jnp.concatenate([o[0] for o in out],axis=1)
    return tok,out[0][1:]


def fwd_kernel(H,E,T,cap,in_vmem,slot,rows,cot,gw,uw,dw,recv,hid,dout,dgp,dup,moe_a,moe_b,dg,*scr):
    if in_vmem: allr=scr[0]; scr=scr[1:]; rb=None
    else: allr=scr[0]; rb=scr[1]; scr=scr[2:]
    (slv,wg,wu,wd,cb,srecv,shid,sdout,sdgp,sdup,smoe,sdg,cr,w_sem,c_sem,l_sem,o_sem,up_s,dn_s,up_r,dn_r,x_s,x_r,b_s,b_r)=scr
    c=lax.axis_index("ctx"); e=lax.axis_index("exp")
    h=c//2; l=c%2; C=2*H; S=C*E
    D=wg.shape[0]; FF=wg.shape[1]; EXT=allr.shape[1]
    expert=c*E+e
    def xpeer(j): return lax.rem(h+j,H)
    def idx(hh,ll,ee): return (hh*2+ll)*E+ee
    bar=pltpu.get_barrier_semaphore()
    pl.semaphore_signal(bar,inc=1,device_id={"ctx":h*2+1-l},device_id_type=MESH)
    for j in range(1,H):
        pl.semaphore_signal(bar,inc=1,device_id={"ctx":xpeer(j)*2+l},device_id_type=MESH)
    @pl.when(e>0)
    def _(): pl.semaphore_signal(bar,inc=1,device_id={"exp":e-1},device_id_type=MESH)
    @pl.when(e<E-1)
    def _(): pl.semaphore_signal(bar,inc=1,device_id={"exp":e+1},device_id_type=MESH)
    order=by_distance(e,E)
    def near(k): return order(E-1-k)
    own=idx(h,l,e)
    wl=[pltpu.make_async_copy(a,b,w_sem.at[i]) for i,(a,b) in enumerate(((gw,wg),(uw,wu),(dw,wd)))]
    first=pltpu.make_async_copy(rows,allr.at[own],w_sem.at[3])
    first.start()
    for x in wl: x.start()
    def job(n):
        m=jnp.maximum(n-2,0)
        r=jnp.where(n<2,0,1+m//(2*H)); t=jnp.where(n<2,n,lax.rem(m,2*H))
        t=jnp.where(r==E,t+2,t)
        j=t//2
        return r,t,j,lax.rem(t,2),jnp.where(j==0,r,r-1)
    def hi(j): return jnp.where(j==0,h,lax.rem(h+H-j,H))
    def sender(n):
        r,t,j,s,k=job(n)
        return idx(hi(j),jnp.where(s==1,1-l,l),near(k))
    def cload(n): return pltpu.make_async_copy(cot.at[sender(n)],cb.at[lax.rem(n,2)],c_sem.at[lax.rem(n,2)])
    cload(0).start()
    def rc(i,ss,rs,**kw): return pltpu.make_async_remote_copy(allr.at[i],allr.at[i],ss,rs,device_id=kw,device_id_type=MESH)
    def up(ee): return rc(idx(h,l,ee),up_s.at[ee],up_r.at[ee],exp=e+1)
    def dn(ee): return rc(idx(h,l,ee),dn_s.at[ee],dn_r.at[ee],exp=e-1)
    def xs(j,ee): return rc(idx(h,l,ee),x_s.at[j-1,ee],x_r.at[j-1,ee],ctx=xpeer(j)*2+l)
    def xr(j,ee):
        return rc(idx(hi(j),l,ee),x_s.at[j-1,ee],x_r.at[j-1,ee],ctx=hi(j)*2+l)
    def bs(j,ee): return rc(idx(hi(j),l,ee),b_s.at[j,ee],b_r.at[j,ee],ctx=h*2+1-l)
    def br(j,ee): return rc(idx(hi(j),1-l,ee),b_s.at[j,ee],b_r.at[j,ee],ctx=h*2+1-l)
    outs=[(srecv,recv),(shid,hid),(sdout,dout),(sdgp,dgp),(sdup,dup),(smoe.at[:,:,:D//2],moe_a),(smoe.at[:,:,D//2:],moe_b),(sdg,dg)]
    def odma(n):
        s=sender(n); b=lax.rem(n,2)
        return [pltpu.make_async_copy(a.at[b],o.at[s],o_sem.at[i,b]) for i,(a,o) in enumerate(outs)]
    def compute(n):
        s=sender(n); b=lax.rem(n,2)
        if in_vmem: rw=allr.at[s]
        else:
            cp=pltpu.make_async_copy(allr.at[s],rb,l_sem); cp.start(); cp.wait(); rw=rb
        cload(n).wait()
        @pl.when(n+1<S)
        def _(): cload(n+1).start()
        @pl.when(n>=2)
        def _():
            for x in odma(n-2): x.wait()
        ct=cb.at[b]
        pk=pick_of(slv[pl.ds(s,1),:],cap); pf=pk.astype(F32); low=pf.astype(BF)
        gm=rw[T:EXT,:T].astype(F32)
        g=jnp.sum(jnp.where(lax.broadcasted_iota(jnp.int32,gm.shape,0)==expert,gm,0.0),axis=0,keepdims=True)
        gsel=jnp.where(pk,jnp.broadcast_to(g,(cap,T)),0.0)
        grow=jnp.sum(gsel,axis=1,keepdims=True)
        comb=gsel.astype(BF)
        step=512
        for m in range(0,D,step):
            srecv[b,:,m:m+step]=nn(low,rw[:T,m:m+step]).astype(BF)
            q=nn(low,ct[:,m:m+step])
            sdout[b,:,m:m+step]=(q*grow).astype(BF)
            cr[:,m:m+step]=q.astype(BF)
        half=FF//2
        for m in range(0,FF,half):
            gp=nn(srecv[b],wg[:,m:m+half]); upp=nn(srecv[b],wu[:,m:m+half])
            dh=nt(sdout[b],wd[m:m+half,:])
            sg=jax.nn.sigmoid(gp); si=gp*sg
            shid[b,:,m:m+half]=(si*upp).astype(BF)
            sdgp[b,:,m:m+half]=(dh*upp*sg*(1.0+gp*(1.0-sg))).astype(BF)
            sdup[b,:,m:m+half]=(dh*si).astype(BF)
        acc=jnp.zeros((cap,1),F32)
        for m in range(0,D,step):
            ev=nn(shid[b],wd[:,m:m+step]).astype(BF)
            acc=acc+jnp.sum(cr[:,m:m+step].astype(F32)*ev.astype(F32),axis=1,keepdims=True)
            smoe[b,:,m:m+step]=tn(comb,ev).astype(BF)
        sdg[b]=jnp.sum(pf*acc,axis=0,keepdims=True)
        for x in odma(n): x.start()
    pltpu.sync_copy(slot,slv)
    first.wait()
    pl.semaphore_wait(bar,H+(e>0).astype(jnp.int32)+(e<E-1).astype(jnp.int32))
    @pl.when(e<E-1)
    def _(): up(e).start()
    @pl.when(e>0)
    def _(): dn(e).start()
    for j in range(1,H): xs(j,e).start()
    bs(0,e).start()
    for x in wl: x.wait()
    def step_(n):
        r,t,j,sib_,k=job(n)
        @pl.when(jnp.logical_and(t==0,r>0))
        def _():
            @pl.when(e>=r)
            def _():
                up(e-r).wait_recv()
                @pl.when(e<E-1)
                def _(): up(e-r).start()
                for q in range(1,H): xs(q,e-r).start()
                bs(0,e-r).start()
            @pl.when(e+r<E)
            def _():
                dn(e+r).wait_recv()
                @pl.when(e>0)
                def _(): dn(e+r).start()
                for q in range(1,H): xs(q,e+r).start()
                bs(0,e+r).start()
        @pl.when(jnp.logical_and(sib_==0,j>0))
        def _():
            xr(j,near(k)).wait_recv(); bs(j,near(k)).start()
        @pl.when(sib_==1)
        def _(): br(j,near(k)).wait_recv()
        compute(n)
    loop(S,step_)
    for x in odma(S-2)+odma(S-1): x.wait()
    def drain(ee):
        @pl.when(jnp.logical_and(e<E-1,ee<=e))
        def _(): up(ee).wait_send()
        @pl.when(jnp.logical_and(e>0,ee>=e))
        def _(): dn(ee).wait_send()
        for j in range(1,H): xs(j,ee).wait_send()
        for j in range(H): bs(j,ee).wait_send()
    loop(E,drain)


def fwd_call(slot,rows,cot,gw,uw,dw,cap,C,E,T,cid=4):
    EXT,D=rows.shape; S=C*E; H=C//2; FF=gw.shape[1]
    dma=pltpu.SemaphoreType.DMA; V=lambda *s: pltpu.VMEM(s,BF)
    in_vmem=S*EXT*D*2<=28*2**20
    A=pl.BlockSpec(memory_space=pl.ANY)
    sd=lambda a,b,dt=BF: jax.ShapeDtypeStruct((S,a,b),dt)
    out_shape=[sd(cap,D),sd(cap,FF),sd(cap,D),sd(cap,FF),sd(cap,FF),sd(T,D//2),sd(T,D//2),sd(1,T,F32)]
    land=[V(S,EXT,D)] if in_vmem else [V(EXT,D)]
    if not in_vmem: out_shape=out_shape+[sd(EXT,D)]
    body=functools.partial(fwd_kernel,H,E,T,cap,in_vmem)
    r=pl.pallas_call(body,out_shape=out_shape,in_specs=[A]*6,out_specs=[A]*len(out_shape),
        scratch_shapes=land+[pltpu.VMEM((S,T),jnp.int32),V(D,FF),V(D,FF),V(FF,D),V(2,T,D),V(2,cap,D),V(2,cap,FF),V(2,cap,D),V(2,cap,FF),V(2,cap,FF),V(2,T,D),pltpu.VMEM((2,1,T),F32),V(cap,D),
            dma((4,)),dma((2,)),dma(()),dma((8,2)),dma((E,)),dma((E,)),dma((E,)),dma((E,)),dma((H-1,E)),dma((H-1,E)),dma((H,E)),dma((H,E))],
        cost_estimate=pl.CostEstimate(flops=2*S*cap*(4*D*FF+3*T*D),bytes_accessed=S*2*(T*D+2*cap*D+3*cap*FF+T*D)+6*D*FF,transcendentals=S*cap*FF),
        compiler_params=pltpu.CompilerParams(collective_id=cid,has_side_effects=True,vmem_limit_bytes=61*2**20),name="experts_fwd")(slot,rows,cot,gw,uw,dw)
    return r[:8]


def mask_bias(lab_r,lab_c,i0,bq,K):
    lr=lab_r[:,:K]; lc=lab_c
    row=lax.broadcasted_iota(jnp.int32,(bq,K),0)+i0; col=lax.broadcasted_iota(jnp.int32,(bq,K),1)
    ok=(col<=row)&((lr==0)|(lr==lc))
    return jnp.where(ok,0.0,-1e30).astype(F32)

def eye_mask():
    return lax.broadcasted_iota(jnp.int32,(HEAD,HEAD),0)==lax.broadcasted_iota(jnp.int32,(HEAD,HEAD),1)

def to_row(col):
    return jnp.sum(jnp.where(eye_mask(),jnp.broadcast_to(col,(HEAD,HEAD)),0.0),axis=0,keepdims=True)

def to_col(row):
    return jnp.sum(jnp.where(eye_mask(),jnp.broadcast_to(row,(HEAD,HEAD)),0.0),axis=1,keepdims=True)

def greet_ctx(C):
    c=lax.axis_index("ctx"); bar=pltpu.get_barrier_semaphore()
    for j in range(1,C): pl.semaphore_signal(bar,inc=1,device_id={"ctx":lax.rem(c+j,C)},device_id_type=MESH)

def sum_ctx(C,buf,ss,rs,others=0):
    c=lax.axis_index("ctx")
    pl.semaphore_wait(pltpu.get_barrier_semaphore(),C-1+others)
    def cp(j): return pltpu.make_async_remote_copy(buf.at[c],buf.at[c],ss.at[j-1],rs.at[j-1],device_id={"ctx":lax.rem(c+j,C)},device_id_type=MESH)
    for j in range(1,C): cp(j).start()
    for j in range(1,C):
        q=lax.rem(c+C-j,C)
        pltpu.make_async_remote_copy(buf.at[q],buf.at[q],ss.at[j-1],rs.at[j-1],device_id={"ctx":q},device_id_type=MESH).wait_recv()
    acc=buf[0]
    for j in range(1,C): acc=acc+buf[j]
    for j in range(1,C): cp(j).wait_send()
    return acc

class Rows:
    def __init__(self,N,E,x,o,ls,us,ur,ds_,dr_,ys,yr):
        self.N,self.E,self.x,self.o=N,E,x,o
        self.ls,self.us,self.ur,self.ds,self.dr,self.ys,self.yr=ls,us,ur,ds_,dr_,ys,yr
        self.p=lax.axis_index("dp"); self.e=lax.axis_index("exp")
        self.peers=(N-1)+(self.e>0).astype(jnp.int32)+(self.e<E-1).astype(jnp.int32)
    def greet(self):
        bar=pltpu.get_barrier_semaphore()
        def sig(**kw): pl.semaphore_signal(bar,inc=1,device_id=kw,device_id_type=MESH)
        for j in range(1,self.N): sig(dp=lax.rem(self.p+j,self.N))
        @pl.when(self.e>0)
        def _(): sig(exp=self.e-1)
        @pl.when(self.e<self.E-1)
        def _(): sig(exp=self.e+1)
        self.local=pltpu.make_async_copy(self.x,self.o.at[self.p,self.e],self.ls)
        self.local.start()
    def rc(self,q,ee,s,r,**kw): return pltpu.make_async_remote_copy(self.o.at[q,ee],self.o.at[q,ee],s,r,device_id=kw,device_id_type=MESH)
    def up(self,ee): return self.rc(self.p,ee,self.us.at[ee],self.ur.at[ee],exp=self.e+1)
    def dn(self,ee): return self.rc(self.p,ee,self.ds.at[ee],self.dr.at[ee],exp=self.e-1)
    def across(self,j,ee): return self.rc(self.p,ee,self.ys.at[j-1,ee],self.yr.at[j-1,ee],dp=lax.rem(self.p+j,self.N))
    def came(self,j,ee):
        q=lax.rem(self.p+self.N-j,self.N)
        return self.rc(q,ee,self.ys.at[j-1,ee],self.yr.at[j-1,ee],dp=q)
    def begin(self):
        e,E=self.e,self.E
        self.local.wait()
        for j in range(1,self.N): self.across(j,e).start()
        @pl.when(e<E-1)
        def _(): self.up(e).start()
        @pl.when(e>0)
        def _(): self.dn(e).start()
    def round(self,r):
        e,E=self.e,self.E
        @pl.when(e>=r)
        def _():
            self.up(e-r).wait_recv()
            @pl.when(e<E-1)
            def _(): self.up(e-r).start()
            for j in range(1,self.N): self.across(j,e-r).start()
        @pl.when(e+r<E)
        def _():
            self.dn(e+r).wait_recv()
            @pl.when(e>0)
            def _(): self.dn(e+r).start()
            for j in range(1,self.N): self.across(j,e+r).start()
    def finish(self):
        e,E=self.e,self.E
        def one(ee):
            for j in range(1,self.N):
                self.came(j,ee).wait_recv(); self.across(j,ee).wait_send()
            @pl.when(jnp.logical_and(e<E-1,ee<=e))
            def _(): self.up(ee).wait_send()
            @pl.when(jnp.logical_and(e>0,ee>=e))
            def _(): self.dn(ee).wait_send()
        loop(E,one)


def attn_fwd_kernel(N,C,E,heads,bq,scale,raw,cos,sin,lab_r,lab_c,gains,wo,qo,ko,vo,mix,inv,ow,bias,buf,ss,rs,*gs):
    G=raw.shape[0]; cols=heads*HEAD; nb=G//HEAD
    c=lax.axis_index("ctx")
    greet_ctx(C)
    rows_w=Rows(N,E,wo,ow,*gs)
    rows_w.greet()
    def squares(i):
        sl=pl.ds(pl.multiple_of(i*HEAD,HEAD),HEAD)
        for t in range(2):
            v=raw[sl,t*cols:(t+1)*cols]
            buf[c,pl.ds(t*nb+i,1),:]=to_row(jnp.sum(v*v,axis=1,keepdims=True))
        vo[sl,:]=raw[sl,2*cols:].astype(BF)
    loop(nb,squares)
    inv[...]=lax.rsqrt(sum_ctx(C,buf,ss,rs,rows_w.peers)/(C*cols)+EPS)
    rows_w.begin()
    def prep(i):
        sl=pl.ds(pl.multiple_of(i*HEAD,HEAD),HEAD)
        cs,sn=cos[sl,:],sin[sl,:]
        for t,o in ((0,qo),(1,ko)):
            r=to_col(inv[pl.ds(t*nb+i,1),:])
            for hd in range(heads):
                a=hd*HEAD
                v=raw[sl,t*cols+a:t*cols+a+HEAD]*r*gains[t:t+1,a:a+HEAD]
                o[sl,a:a+HEAD]=(v*cs+pltpu.roll(v,HEAD//2,1)*sn).astype(BF)
    loop(nb,prep)
    def block(i,K):
        rows=pl.ds(pl.multiple_of(i*bq,bq),bq)
        bias[:,:K]=mask_bias(lab_r,lab_c[rows,:],i*bq,bq,K)
        def head(hd):
            ln=pl.ds(pl.multiple_of(hd*HEAD,HEAD),HEAD)
            s=nt(qo[rows,ln],ko[:K,ln])*scale+bias[:,:K]
            p=jnp.exp(s-jnp.max(s,axis=1,keepdims=True))
            pr=(p*(1.0/jnp.sum(p,axis=1,keepdims=True))).astype(BF)
            mix[rows,ln]=nn(pr,vo[:K,ln]).astype(BF)
        loop(heads,head)
    per=G//bq//3
    for g in range(3):
        loop(per,lambda i,g=g: block(i+g*per,(g+1)*per*bq))
        if g+1<E: rows_w.round(g+1)
    for r in range(4,E): rows_w.round(r)
    rows_w.finish()

def attn_fwd(raw,cos,sin,lab_r,lab_c,gains,wo,N,C,E,heads,cid,bq=512):
    G=raw.shape[0]; cols=heads*HEAD; R=2*G//HEAD; dma=pltpu.SemaphoreType.DMA
    o=jax.ShapeDtypeStruct((G,cols),BF)
    V=pl.BlockSpec(memory_space=pltpu.VMEM); A=pl.BlockSpec(memory_space=pl.ANY)
    return pl.pallas_call(functools.partial(attn_fwd_kernel,N,C,E,heads,bq,HEAD**-0.5),out_shape=[o]*4+[jax.ShapeDtypeStruct((R,HEAD),F32),jax.ShapeDtypeStruct((N,E)+wo.shape,BF)],in_specs=[V]*6+[A],out_specs=[V]*5+[A],
        scratch_shapes=[pltpu.VMEM((bq,G),F32),pltpu.VMEM((C,R,HEAD),F32),dma((C-1,)),dma((C-1,)),dma(()),dma((E,)),dma((E,)),dma((E,)),dma((E,)),dma((N-1,E)),dma((N-1,E))],
        cost_estimate=pl.CostEstimate(flops=2*2*heads*G*G*HEAD,bytes_accessed=G*cols*20,transcendentals=heads*G*G),
        compiler_params=pltpu.CompilerParams(collective_id=cid,has_side_effects=True,vmem_limit_bytes=48*2**20),name="attn_fwd")(raw,cos,sin,lab_r,lab_c,gains,wo)

def attn_bwd_kernel(C,heads,bq,scale,q,k,v,dm,raw,inv,cos,sin,lab_r,lab_c,gains,draw,gsum,bias,aq,ak,av,buf,ss,rs):
    G=q.shape[0]; cols=heads*HEAD; nb=G//HEAD
    c=lax.axis_index("ctx")
    greet_ctx(C)
    ak[...]=jnp.zeros_like(ak); av[...]=jnp.zeros_like(av)
    def block(i,K):
        rows=pl.ds(pl.multiple_of(i*bq,bq),bq)
        bias[:,:K]=mask_bias(lab_r,lab_c[rows,:],i*bq,bq,K)
        def head(hd):
            ln=pl.ds(pl.multiple_of(hd*HEAD,HEAD),HEAD)
            qb=q[rows,ln]; kb=k[:K,ln]; db=dm[rows,ln]
            s=nt(qb,kb)*scale+bias[:,:K]
            p=jnp.exp(s-jnp.max(s,axis=1,keepdims=True))
            p=p*(1.0/jnp.sum(p,axis=1,keepdims=True))
            dp=nt(db,v[:K,ln])
            ds=(p*(dp-jnp.sum(p*dp,axis=1,keepdims=True))).astype(BF)
            aq[rows,ln]=nn(ds,kb)
            ak[:K,ln]+=tn(ds,qb)
            av[:K,ln]+=tn(p.astype(BF),db)
        loop(heads,head)
    per=G//bq//3
    for g in range(3):
        loop(per,lambda i,g=g: block(i+g*per,(g+1)*per*bq))
    gsum[...]=jnp.zeros_like(gsum)
    def unrope(i):
        sl=pl.ds(pl.multiple_of(i*HEAD,HEAD),HEAD)
        for t,a in ((0,aq),(1,ak)):
            r=to_col(inv[pl.ds(t*nb+i,1),:])
            dot=jnp.zeros((HEAD,1),F32)
            for hd in range(heads):
                b=hd*HEAD
                g=a[sl,b:b+HEAD]*scale
                g=g*cos[sl,:]-pltpu.roll(g,HEAD//2,1)*sin[sl,:]
                x=raw[sl,t*cols+b:t*cols+b+HEAD]
                gsum[t:t+1,b:b+HEAD]+=jnp.sum(g*x*r,axis=0,keepdims=True)
                g=g*gains[t:t+1,b:b+HEAD]
                a[sl,b:b+HEAD]=g
                dot=dot+jnp.sum(g*x,axis=1,keepdims=True)
            buf[c,pl.ds(t*nb+i,1),:]=to_row(dot)
        draw[sl,2*cols:]=av[sl,:].astype(BF)
    loop(nb,unrope)
    buf[0]=sum_ctx(C,buf,ss,rs)/(C*cols)
    def fin(i):
        sl=pl.ds(pl.multiple_of(i*HEAD,HEAD),HEAD)
        for t,a in ((0,aq),(1,ak)):
            r=to_col(inv[pl.ds(t*nb+i,1),:]); dot=to_col(buf[0,pl.ds(t*nb+i,1),:])
            m=r*r*r*dot
            draw[sl,t*cols:(t+1)*cols]=(a[sl,:]*r-raw[sl,t*cols:(t+1)*cols]*m).astype(BF)
    loop(nb,fin)

def attn_bwd(q,k,v,dm,raw,inv,cos,sin,lab_r,lab_c,gains,C,heads,cid,bq=512):
    G,cols=q.shape; R=2*G//HEAD; dma=pltpu.SemaphoreType.DMA
    V=pl.BlockSpec(memory_space=pltpu.VMEM)
    acc=pltpu.VMEM((G,cols),F32)
    return pl.pallas_call(functools.partial(attn_bwd_kernel,C,heads,bq,HEAD**-0.5),out_shape=[jax.ShapeDtypeStruct((G,3*cols),BF),jax.ShapeDtypeStruct((2,cols),F32)],in_specs=[V]*11,out_specs=[V]*2,
        scratch_shapes=[pltpu.VMEM((bq,G),F32),acc,acc,acc,pltpu.VMEM((C,R,HEAD),F32),dma((C-1,)),dma((C-1,))],
        cost_estimate=pl.CostEstimate(flops=5*2*heads*G*G*HEAD,bytes_accessed=G*cols*20,transcendentals=heads*G*G),
        compiler_params=pltpu.CompilerParams(collective_id=cid,has_side_effects=True,vmem_limit_bytes=56*2**20),name="attn_bwd")(q,k,v,dm,raw,inv,cos,sin,lab_r,lab_c,gains)

def ctx_barrier(H,c,h,l):
    bar=pltpu.get_barrier_semaphore()
    pl.semaphore_signal(bar,inc=1,device_id={"ctx":h*2+1-l},device_id_type=MESH)
    for j in range(1,H):
        pl.semaphore_signal(bar,inc=1,device_id={"ctx":lax.rem(h+j,H)*2+l},device_id_type=MESH)
    pl.semaphore_wait(bar,H)

def ag_ctx_kernel(H,Q,x,o,xs,xr,bs,br,lsem):
    c=lax.axis_index("ctx"); h=c//2; l=c%2
    T=x.shape[0]; R=T//Q
    loc=pltpu.make_async_copy(x,o.at[c],lsem); loc.start()
    ctx_barrier(H,c,h,l)
    sib=h*2+1-l
    def sl(q): return pl.ds(q*R,R)
    def rc(a,b,s,r,to): return pltpu.make_async_remote_copy(a,b,s,r,device_id={"ctx":to},device_id_type=MESH)
    def xc(j,q): return rc(x.at[sl(q)],o.at[c,sl(q)],xs.at[j-1,q],xr.at[j-1,q],lax.rem(h+j,H)*2+l)
    def xw(j,q):
        p=lax.rem(h+H-j,H)*2+l; return rc(x.at[sl(q)],o.at[p,sl(q)],xs.at[j-1,q],xr.at[j-1,q],p)
    def bc(j,q):
        p=c if j==0 else lax.rem(h+H-j,H)*2+l
        src=x if j==0 else o.at[p]
        return rc(src.at[sl(q)],o.at[p,sl(q)],bs.at[j,q],br.at[j,q],sib)
    def bw(j,q):
        p=sib if j==0 else lax.rem(h+H-j,H)*2+1-l
        return rc(x.at[sl(q)],o.at[p,sl(q)],bs.at[j,q],br.at[j,q],sib)
    for q in range(Q):
        for j in range(1,H): xc(j,q).start()
    for q in range(Q): bc(0,q).start()
    for q in range(Q):
        for j in range(1,H):
            xw(j,q).wait_recv(); bc(j,q).start()
    for j in range(H):
        for q in range(Q):
            bw(j,q).wait_recv(); bc(j,q).wait_send()
            if j>0: xc(j,q).wait_send()
    loc.wait()

def ag_ctx(x,C,cid,Q=4):
    T,D=x.shape; H=C//2; dma=pltpu.SemaphoreType.DMA
    A=pl.BlockSpec(memory_space=pl.ANY)
    return pl.pallas_call(functools.partial(ag_ctx_kernel,H,Q),out_shape=jax.ShapeDtypeStruct((C,T,D),x.dtype),in_specs=[A],out_specs=A,
        scratch_shapes=[dma((H-1,Q)),dma((H-1,Q)),dma((H,Q)),dma((H,Q)),dma(())],
        compiler_params=pltpu.CompilerParams(collective_id=cid,has_side_effects=True),name="ag_ctx")(x)

def rs_ctx_kernel(H,Q,mix,w,o,own,sd,r1,r2,s1,q1,s2,q2,osem):
    c=lax.axis_index("ctx"); h=c//2; l=c%2
    T=own.shape[1]; R=T//Q; D=w.shape[1]
    def sl(q): return pl.ds(q*R,R)
    hs=[lax.rem(h+j,H) for j in range(1,H)]+[h]
    def product(cc,put):
        rw=pl.ds(pl.multiple_of(cc*T,T),T)
        def chunk(n):
            cl=pl.ds(pl.multiple_of(n*512,512),512)
            put[:,cl]=nn(mix[rw,:],w[:,cl]).astype(BF)
        loop(D//512,chunk)
    def c1(i,q): return pltpu.make_async_remote_copy(sd.at[hs[i],sl(q)],r1.at[hs[i],sl(q)],s1.at[hs[i],q],q1.at[hs[i],q],device_id={"ctx":h*2+1-l},device_id_type=MESH)
    def c2(j,q): return pltpu.make_async_remote_copy(own.at[hs[j-1],sl(q)],r2.at[j-1,sl(q)],s2.at[j-1,q],q2.at[j-1,q],device_id={"ctx":hs[j-1]*2+l},device_id_type=MESH)
    ctx_barrier(H,c,h,l)
    for i in range(H):
        product(hs[i]*2+1-l,sd.at[hs[i]])
        for q in range(Q): c1(i,q).start()
        product(hs[i]*2+l,own.at[hs[i]])
        if i<H-1:
            for q in range(Q):
                c1(i,q).wait_recv()
                add_into(own.at[hs[i],sl(q)],r1.at[hs[i],sl(q)])
                c2(i+1,q).start()
    for q in range(Q):
        c1(H-1,q).wait_recv()
        add_into(own.at[h,sl(q)],r1.at[h,sl(q)])
    for q in range(Q):
        for j in range(1,H):
            c2(j,q).wait_recv()
            add_into(own.at[h,sl(q)],r2.at[j-1,sl(q)])
    out=pltpu.make_async_copy(own.at[h],o,osem); out.start()
    for q in range(Q):
        for i in range(H): c1(i,q).wait_send()
        for j in range(1,H): c2(j,q).wait_send()
    out.wait()


def rs_ctx(mix,w,C,cid,Q=4):
    G,cols=mix.shape; D=w.shape[1]; T=G//C; H=C//2; dma=pltpu.SemaphoreType.DMA
    A=pl.BlockSpec(memory_space=pl.ANY); V=pl.BlockSpec(memory_space=pltpu.VMEM)
    buf=pltpu.VMEM((H,T,D),BF)
    return pl.pallas_call(functools.partial(rs_ctx_kernel,H,Q),out_shape=jax.ShapeDtypeStruct((T,D),BF),in_specs=[V,V],out_specs=A,
        scratch_shapes=[buf,buf,buf,pltpu.VMEM((H-1,T,D),BF),dma((H,Q)),dma((H,Q)),dma((H-1,Q)),dma((H-1,Q)),dma(())],
        cost_estimate=pl.CostEstimate(flops=2*G*cols*D,bytes_accessed=2*(G*cols+cols*D+T*D),transcendentals=0),
        compiler_params=pltpu.CompilerParams(collective_id=cid,has_side_effects=True,vmem_limit_bytes=40*2**20),name="rs_ctx")(mix,w)


def front_kernel(N,C,E,Q,wq,wk,wv,nx,qkv,na,a_s,a_r,up_s,up_r,dn_s,dn_r,y_s,y_r,xs_,xr_,bs_,br_,lsem):
    p=lax.axis_index("dp"); c=lax.axis_index("ctx"); e=lax.axis_index("exp")
    H=C//2; h=c//2; l=c%2; sib=h*2+1-l
    D=wq.shape[1]; cols=D//C; piece=cols//N; T=nx.shape[0]; R=T//Q
    def dpeer(j): return lax.rem(p+j,N)
    def cpeer(j): return lax.rem(c+j,C)
    bar=pltpu.get_barrier_semaphore()
    def sig(**kw): pl.semaphore_signal(bar,inc=1,device_id=kw,device_id_type=MESH)
    for j in range(1,N): sig(dp=dpeer(j))
    for j in range(1,C): sig(ctx=cpeer(j))
    @pl.when(e>0)
    def _(): sig(exp=e-1)
    @pl.when(e<E-1)
    def _(): sig(exp=e+1)
    def rc(a,b,s,r,**kw): return pltpu.make_async_remote_copy(a,b,s,r,device_id=kw,device_id_type=MESH)
    W=(wq,wk,wv)
    def src(t,d,q): return W[t].at[:,pl.ds(pl.multiple_of(d*(D//N)+q*piece,128),piece)]
    def dst(t,d,q): return qkv.at[p,q,e,:,pl.ds(t*cols+d*piece,piece)]
    TD=[(t,d) for t in range(3) for d in range(N)]
    local=[pltpu.make_async_copy(src(t,d,c),dst(t,d,c),lsem.at[i]) for i,(t,d) in enumerate(TD)]
    local_n=pltpu.make_async_copy(nx,na.at[c],lsem.at[len(TD)+1])
    for x in local+[local_n]: x.start()
    def away(j,i):
        t,d=TD[i]; q=cpeer(j)
        return rc(src(t,d,q),dst(t,d,c),a_s.at[j-1,i],a_r.at[j-1,i],ctx=q)
    def home(j,i):
        t,d=TD[i]; q=lax.rem(c+C-j,C)
        return rc(src(t,d,q),dst(t,d,q),a_s.at[j-1,i],a_r.at[j-1,i],ctx=q)
    def both(q,ee): return ((0,qkv.at[q,:,ee]),)
    def up(i,ee): b=both(p,ee)[i][1]; return rc(b,b,up_s.at[i,ee],up_r.at[i,ee],exp=e+1)
    def dn(i,ee): b=both(p,ee)[i][1]; return rc(b,b,dn_s.at[i,ee],dn_r.at[i,ee],exp=e-1)
    def ys(i,j,ee): b=both(p,ee)[i][1]; return rc(b,b,y_s.at[i,j-1,ee],y_r.at[i,j-1,ee],dp=dpeer(j))
    def yr(i,j,ee): q=lax.rem(p+N-j,N); b=both(q,ee)[i][1]; return rc(b,b,y_s.at[i,j-1,ee],y_r.at[i,j-1,ee],dp=q)
    def sl(q): return pl.ds(q*R,R)
    def xc(j,q): return rc(nx.at[sl(q)],na.at[c,sl(q)],xs_.at[j-1,q],xr_.at[j-1,q],ctx=lax.rem(h+j,H)*2+l)
    def xw(j,q):
        s=lax.rem(h+H-j,H)*2+l; return rc(nx.at[sl(q)],na.at[s,sl(q)],xs_.at[j-1,q],xr_.at[j-1,q],ctx=s)
    def bc(j,q):
        s=c if j==0 else lax.rem(h+H-j,H)*2+l
        a=nx if j==0 else na.at[s]
        return rc(a.at[sl(q)],na.at[s,sl(q)],bs_.at[j,q],br_.at[j,q],ctx=sib)
    def bw(j,q):
        s=sib if j==0 else lax.rem(h+H-j,H)*2+1-l
        return rc(nx.at[sl(q)],na.at[s,sl(q)],bs_.at[j,q],br_.at[j,q],ctx=sib)
    pl.semaphore_wait(bar,(N-1)+(C-1)+(e>0).astype(jnp.int32)+(e<E-1).astype(jnp.int32))
    for j in range(1,C):
        for i in range(len(TD)): away(j,i).start()
    for q in range(Q):
        for j in range(1,H): xc(j,q).start()
    for q in range(Q): bc(0,q).start()
    for x in local: x.wait()
    for j in range(1,C):
        for i in range(len(TD)): home(j,i).wait_recv()
    for i in range(1):
        for j in range(1,N): ys(i,j,e).start()
        @pl.when(e<E-1)
        def _(): up(i,e).start()
        @pl.when(e>0)
        def _(): dn(i,e).start()
    def rounds(r0):
        r=r0+1
        for i in range(1):
            @pl.when(e>=r)
            def _():
                up(i,e-r).wait_recv()
                @pl.when(e<E-1)
                def _(): up(i,e-r).start()
                for j in range(1,N): ys(i,j,e-r).start()
            @pl.when(e+r<E)
            def _():
                dn(i,e+r).wait_recv()
                @pl.when(e>0)
                def _(): dn(i,e+r).start()
                for j in range(1,N): ys(i,j,e+r).start()
        @pl.when(r0==0)
        def _():
            for q in range(Q):
                for j in range(1,H):
                    xw(j,q).wait_recv(); bc(j,q).start()
    loop(E-1,rounds)
    def finish(ee):
        for i in range(1):
            for j in range(1,N):
                yr(i,j,ee).wait_recv(); ys(i,j,ee).wait_send()
            @pl.when(jnp.logical_and(e<E-1,ee<=e))
            def _(): up(i,ee).wait_send()
            @pl.when(jnp.logical_and(e>0,ee>=e))
            def _(): dn(i,ee).wait_send()
    loop(E,finish)
    for j in range(1,C):
        for i in range(len(TD)): away(j,i).wait_send()
    for q in range(Q):
        for j in range(1,H): xc(j,q).wait_send()
        for j in range(H):
            bc(j,q).wait_send(); bw(j,q).wait_recv()
    local_n.wait()


def front(wq,wk,wv,nx,N,C,E,cid,Q=2):
    S,D=wq.shape; T=nx.shape[0]; H=C//2; dma=pltpu.SemaphoreType.DMA
    A=pl.BlockSpec(memory_space=pl.ANY)
    return pl.pallas_call(functools.partial(front_kernel,N,C,E,Q),
        out_shape=[jax.ShapeDtypeStruct((N,C,E,S,3*D//C),BF),jax.ShapeDtypeStruct((C,T,D),BF)],
        in_specs=[A]*4,out_specs=[A]*2,
        scratch_shapes=[dma((C-1,3*N)),dma((C-1,3*N)),dma((2,E)),dma((2,E)),dma((2,E)),dma((2,E)),dma((2,N-1,E)),dma((2,N-1,E)),dma((H-1,Q)),dma((H-1,Q)),dma((H,Q)),dma((H,Q)),dma((3*N+2,))],
        compiler_params=pltpu.CompilerParams(collective_id=cid,has_side_effects=True),name="front")(wq,wk,wv,nx)


def add_kernel(split,*refs):
    g,og,u,oa,ob,d,od,sg,su,sd=refs
    i=pl.program_id(0)
    sg[...]=g[...].astype(F32)+og[...].astype(F32)
    su[...]=u[...].astype(F32)+jnp.where(i<split,oa[...].astype(F32),ob[...].astype(F32))
    sd[...]=d[...].astype(F32)+od[...].astype(F32)


def add_shares(g,og,u,oa,ob,d,od,steps=16):
    D,FF=g.shape; F2,D2=d.shape
    r,r2=D//steps,F2//steps
    split=oa.shape[0]//r
    wide=pl.BlockSpec((r,FF),lambda i:(i,0)); tall=pl.BlockSpec((r2,D2),lambda i:(i,0))
    return pl.pallas_call(functools.partial(add_kernel,split),grid=(steps,),
        in_specs=[wide,wide,wide,pl.BlockSpec((r,FF),lambda i:(jnp.minimum(i,split-1),0)),pl.BlockSpec((r,FF),lambda i:(jnp.maximum(i-split,0),0)),tall,tall],
        out_specs=[wide,wide,tall],
        out_shape=[jax.ShapeDtypeStruct((D,FF),F32)]*2+[jax.ShapeDtypeStruct((F2,D2),F32)],
        cost_estimate=pl.CostEstimate(flops=6*D*FF,bytes_accessed=24*D*FF,transcendentals=0),
        compiler_params=pltpu.CompilerParams(dimension_semantics=("arbitrary",),vmem_limit_bytes=32*2**20),name="add_shares")(g,og,u,oa,ob,d,od)


def dot_nn(a, b):
    return lax.dot_general(a, b, (((1,), (0,)), ((), ())), preferred_element_type=F32)


def dot_tn(a, b):
    return lax.dot_general(a, b, (((0,), (0,)), ((), ())), preferred_element_type=F32)


def dot_nt(a, b):
    return lax.dot_general(a, b, (((1,), (1,)), ((), ())), preferred_element_type=F32)


def per_device(
    hidden_in,
    segments,
    routes,
    attn_gain,
    query_weight,
    key_weight,
    value_weight,
    query_gain,
    key_gain,
    output_weight,
    ffn_gain,
    router_weight,
    gate_weight,
    up_weight,
    down_weight,
    cotangent,
):
    n_dp, n_ctx, n_exp = (lax.axis_size(a) for a in ALL)
    tok, width = hidden_in.shape[2:]
    topk = routes.shape[3]
    experts = n_ctx * n_exp
    cap = (5 * tok * topk + 4 * experts - 1) // (4 * experts)
    cap = -(-cap // 16) * 16
    group = segments.shape[2]
    shard = query_weight.shape[0]
    cols = width // n_ctx
    piece = cols // n_dp
    heads = cols // HEAD
    ctx_me = lax.axis_index("ctx")
    exp_me = lax.axis_index("exp")
    expert_me = ctx_me * n_exp + exp_me

    def own_cols(vec):
        return lax.dynamic_index_in_dim(
            vec.reshape(n_dp, n_ctx, piece), ctx_me, 1, keepdims=False
        ).reshape(cols)

    own_routes = routes[0, 0]
    expert_ids = jnp.arange(experts, dtype=jnp.int32)
    hits = jnp.sum((own_routes[:, :, None] == expert_ids).astype(jnp.int32), axis=1)
    tokens = jnp.arange(tok, dtype=jnp.int32)
    lower = (tokens[:, None] > tokens[None, :]).astype(BF)
    earlier = dot_nn(lower, hits.astype(BF)).astype(jnp.int32)
    slot_local = jnp.where(hits > 0, earlier, -1).T
    slot = lax.all_to_all(slot_local, MOE, split_axis=0, concat_axis=0, tiled=True)
    slot = slot.reshape(experts, tok)
    cot = cotangent[0, 0]

    hidden = hidden_in[0, 0].astype(F32)
    labels = segments[0, 0]
    index = jnp.arange(group, dtype=jnp.int32)
    before = jnp.sum((labels[None, :] < labels[:, None]).astype(jnp.int32), axis=1)
    positions = index - before + jnp.where(labels > 0, PROMPT, 0).astype(jnp.int32)
    half = HEAD // 2
    frequency = THETA ** (-(jnp.arange(half, dtype=F32) * 2.0 / HEAD))
    angles = positions.astype(F32)[:, None] * frequency[None, :]
    cos, sin = jnp.cos(angles), jnp.sin(angles)
    cos = jnp.concatenate([cos, cos], axis=1)
    sin = jnp.concatenate([-sin, sin], axis=1)
    label_row, label_col = labels[None, :], labels[:, None]
    attn_gain_f = attn_gain.astype(F32)
    ffn_gain_f = ffn_gain.astype(F32)
    q_gain = own_cols(query_gain.astype(F32))
    k_gain = own_cols(key_gain.astype(F32))

    attn_r = lax.rsqrt(jnp.mean(hidden * hidden, axis=-1, keepdims=True) + EPS)
    normed = (hidden * attn_r * attn_gain_f).astype(BF)
    qkv_w, normed_g = front(query_weight, key_weight, value_weight, normed, n_dp, n_ctx, n_exp, 5)
    qkv_w = qkv_w.reshape(width, 3 * cols)
    normed_g = normed_g.reshape(group, width)
    cot, normed_g = lax.optimization_barrier((cot, normed_g))
    cot_all = lax.all_gather(cot, MOE, axis=0, tiled=False)
    raw = dot_nn(normed_g, qkv_w)
    gains = jnp.stack([q_gain, k_gain])
    q_rot, k_rot, v_low, mix, inv, out_w = attn_fwd(
        raw, cos, sin, label_row, label_col, gains, output_weight, n_dp, n_ctx, n_exp, heads, 9
    )
    out_w = out_w.reshape(cols, width)
    branch = rs_ctx(mix, out_w, n_ctx, 6)
    residual = hidden + branch.astype(F32)

    ffn_r = lax.rsqrt(jnp.mean(residual * residual, axis=-1, keepdims=True) + EPS)
    ffn_normed = (residual * ffn_r * ffn_gain_f).astype(BF)
    logits = dot_nn(ffn_normed, router_weight)
    router_prob = jax.nn.softmax(logits, axis=-1)
    gates = jnp.where(hits > 0, router_prob, 0.0).astype(BF)
    padded = jnp.zeros((experts, width), BF).at[:, :tok].set(gates.T)
    rows_ext = jnp.concatenate([ffn_normed, padded], axis=0)
    gate_mat, up_mat, down_mat = gate_weight[0], up_weight[0], down_weight[0]
    received, expert_hidden, d_out, d_gate_pre, d_up_pre, moe_a, moe_b, d_gate_at = fwd_call(
        slot, rows_ext, cot_all, gate_mat, up_mat, down_mat, cap, n_ctx, n_exp, tok
    )
    total = experts * cap

    d_gate = lax.all_to_all(
        d_gate_at.reshape(experts, tok), MOE, split_axis=0, concat_axis=0, tiled=True
    ).T
    received = received.reshape(total, width)
    gate_low = dot_tn(received, d_gate_pre.reshape(total, -1)).astype(BF)
    moe_a = lax.psum_scatter(
        moe_a.reshape(experts * tok, width // 2), MOE, scatter_dimension=0, tiled=True
    )
    up_low = dot_tn(received, d_up_pre.reshape(total, -1)).astype(BF)
    down_low = dot_tn(expert_hidden.reshape(total, -1), d_out.reshape(total, width)).astype(BF)
    most = width * 3 // 4
    swap = ((gate_low, width), (up_low, most)) if n_dp == 2 else ()
    d_gate_pre, down_low = lax.optimization_barrier((d_gate_pre, down_low))
    d_tokens, others = back_call(
        slot, d_gate_pre, d_up_pre, gate_mat, up_mat, swap, n_ctx, n_exp, tok, (1, 8)
    )
    down_low, d_tokens = lax.optimization_barrier((down_low, d_tokens))
    if swap:
        pair = lambda x: lax.ppermute(x, "dp", [(0, 1), (1, 0)])
        wide = (gate_low, others[0], up_low, others[1], pair(up_low[most:]), down_low, pair(down_low))
    else:
        wide = tuple(lax.psum(x, "dp") for x in (gate_low, up_low, down_low))

    d_router = d_gate
    d_logits = (
        router_prob * (d_router - jnp.sum(router_prob * d_router, axis=-1, keepdims=True))
    ).astype(BF)
    router_grad = dot_tn(d_logits, ffn_normed)
    d_ffn = d_tokens.astype(F32) + dot_nt(d_logits, router_weight)
    ffn_gain_grad = jnp.sum(d_ffn * residual * ffn_r, axis=0)
    weighted = d_ffn * ffn_gain_f
    d_residual = cot.astype(F32) + (
        weighted * ffn_r
        - residual * ffn_r**3 * jnp.mean(residual * weighted, axis=-1, keepdims=True)
    )
    d_branch = d_residual.astype(BF)

    moe_b, d_branch = lax.optimization_barrier((moe_b, d_branch))
    moe_b = lax.psum_scatter(
        moe_b.reshape(experts * tok, width // 2), MOE, scatter_dimension=0, tiled=True
    )
    moe_out = jnp.concatenate([moe_a, moe_b], axis=1)
    d_branch_g = ag_ctx(d_branch, n_ctx, 7).reshape(group, width)
    out_grad = dot_tn(mix, d_branch_g)
    d_mix = dot_nt(d_branch_g, out_w).astype(BF)
    d_raw, gain_parts = attn_bwd(
        q_rot, k_rot, v_low, d_mix, raw, inv, cos, sin, label_row, label_col, gains, n_ctx, heads, 10
    )
    spread = jnp.zeros((2, n_dp, n_ctx, piece), F32)
    spread = lax.dynamic_update_slice(
        spread, gain_parts.reshape(2, n_dp, 1, piece), (0, 0, ctx_me, 0)
    ).reshape(2, width)
    small = jnp.concatenate([router_grad, spread, ffn_gain_grad[None]], axis=0)
    small = jnp.pad(small, ((0, 8 - small.shape[0] % 8), (0, 0)))
    out_part = out_grad.astype(BF).reshape(n_dp, n_exp, shard, width)
    query_sum, key_sum, value_sum, out_sum, hidden_grad, small = tail(
        normed_g, d_raw, qkv_w, out_part, hidden_in[0, 0], d_residual, attn_gain_f[None], small, n_ctx
    )
    query_sum, key_sum, value_sum, out_sum = (
        x.astype(F32) for x in (query_sum, key_sum, value_sum, out_sum)
    )
    wide, moe_out, small = lax.optimization_barrier((wide, moe_out, small))
    output = (residual + moe_out.astype(F32)).astype(BF)
    gate_sum, up_sum, down_sum = (
        add_shares(*wide) if n_dp == 2 else (x.astype(F32) for x in wide)
    )
    return (
        output[None, None],
        hidden_grad[None, None],
        small[-1],
        query_sum,
        key_sum,
        value_sum,
        small[experts],
        small[experts + 1],
        out_sum,
        small[experts + 2],
        small[:experts].T,
        gate_sum[None],
        up_sum[None],
        down_sum[None],
    )


def solution(mesh):
    tokens = P("dp", "exp", "ctx", None)
    rows = P(ALL, None)
    expert = P(MOE, None, None)
    return jax.shard_map(
        per_device,
        mesh=mesh,
        in_specs=(
            tokens,
            P("dp", "exp", None),
            tokens,
            P(),
            rows,
            rows,
            rows,
            P(),
            P(),
            rows,
            P(),
            P(),
            expert,
            expert,
            expert,
            tokens,
        ),
        out_specs=(
            tokens,
            tokens,
            P(),
            rows,
            rows,
            rows,
            P(),
            P(),
            rows,
            P(),
            P(),
            expert,
            expert,
            expert,
        ),
        check_vma=False,
    )
```
